32 devices in a mesh: row: 4 (over y, x), col: 8 (over z, core).
Axes of the slice: x: 2, y: 2, z: 4, core: 2. Of those that a mesh axis runs over, the one named last changes fastest.
Arguments:
- tokens: bfloat16 [8192, 1024], P(('row', 'col')), may hold values from -6 to 6
- block_ids: int32 [4, 2048], P('row', 'col'), may hold values from 0 to 7, never falling along the last dimension, each value on 1 to 512 neighbouring positions
- expert_ids: int32 [8192], P(('row', 'col')), may hold values from 0 to 7, as said below
- cotangent: bfloat16 [8192, 1024], P(('row', 'col')), may hold values from -6 to 6
- norm_gain: bfloat16 [1024], P(('row', 'col')), may hold values from 0.5 to 1.5
- norm_shift: bfloat16 [1024], P(('row', 'col')), may hold values from -0.059814453 to 0.059814453
- w_query: bfloat16 [1024, 1024], P('row', 'col'), may hold values from -0.1875 to 0.1875
- w_key: bfloat16 [1024, 1024], P('row', 'col'), may hold values from -0.1875 to 0.1875
- w_value: bfloat16 [1024, 1024], P('row', 'col'), may hold values from -0.1875 to 0.1875
- w_output: bfloat16 [1024, 1024], P('row', 'col'), may hold values from -2 to 2
- centroids: bfloat16 [8, 1024], P('col', 'row'), may hold values from -0.09375 to 0.09375
- expert_gain: bfloat16 [8, 2, 1024], P('col', None, 'row'), may hold values from 0.5 to 1.5
- expert_shift: bfloat16 [8, 2, 1024], P('col', None, 'row'), may hold values from -0.59765625 to 0.59765625
- w_in: bfloat16 [8, 2, 1024, 4096], P('col', None, None, 'row'), may hold values from -0.1875 to 0.1875
- b_in: bfloat16 [8, 2, 4096], P('col', None, 'row'), may hold values from -0.59765625 to 0.59765625
- w_back: bfloat16 [8, 2, 4096, 1024], P('col', None, 'row'), may hold values from -0.09375 to 0.09375
- b_back: bfloat16 [8, 2, 1024], P('col', None, 'row'), may hold values from -0.59765625 to 0.59765625
Outputs:
- output: bfloat16 [8192, 1024], P(('row', 'col'))
- tokens_grad: float32 [8192, 1024], P(('row', 'col'))
- norm_gain_grad: float32 [1024], P(('row', 'col'))
- norm_shift_grad: float32 [1024], P(('row', 'col'))
- w_query_grad: float32 [1024, 1024], P('row', 'col')
- w_key_grad: float32 [1024, 1024], P('row', 'col')
- w_value_grad: float32 [1024, 1024], P('row', 'col')
- w_output_grad: float32 [1024, 1024], P('row', 'col')
- centroids_grad: float32 [8, 1024], P('col', 'row')
- expert_gain_grad: float32 [8, 2, 1024], P('col', None, 'row')
- expert_shift_grad: float32 [8, 2, 1024], P('col', None, 'row')
- w_in_grad: float32 [8, 2, 1024, 4096], P('col', None, None, 'row')
- b_in_grad: float32 [8, 2, 4096], P('col', None, 'row')
- w_back_grad: float32 [8, 2, 4096, 1024], P('col', None, 'row')
- b_back_grad: float32 [8, 2, 1024], P('col', None, 'row')
The draws below stay inside these ranges and needn't reach their ends.
Inputs may be any that keep to these rules, and one draw needn't show every extreme that they name: `block_ids`: in each sequence the block numbers start at 0, never fall and rise by one at each new block; a block holds 1 to 512 positions. `expert_ids`: the rows of one device (256 aligned rows) name every expert exactly 32 times.
All inputs are finite; a program needn't handle non-finite values.
Results may differ from the reference program's by a relative error of at most 0.02.
Values may be sent and summed in bfloat16 or wider, within the bound.
No kernel may reach another device: no remote copies, remote signals or barrier semaphores. Data moves between devices by JAX's collectives and lax.ppermute only.
A program may use at most 320 MiB of HBM per device.

```python
import math
import jax
import jax.numpy as jnp
import numpy as np
from jax import lax

D = 1024
HEADS = 16
FF = 4096
TOK_DEV = 256
BLOCK = 256
EXPERTS = 8
SEQS = 4
LENGTH = 2048
TOKENS = 8192


def draw_expert_ids(key, part):
    shuffle_keys = jax.random.randint(key, (TOKENS // TOK_DEV, TOK_DEV), 0, 65536, dtype=jnp.int32) * TOK_DEV + jnp.arange(TOK_DEV, dtype=jnp.int32)[None, :]
    ranking = jnp.argsort(shuffle_keys, axis=1)
    return (ranking % EXPERTS).reshape(TOKENS).astype(jnp.int32)


def raised(values, rng, source, target, blocks, factor):
    owner, partner = [(jnp.arange(values.shape[dim]) // (values.shape[dim] // blocks)).reshape([-1 if axis == dim else 1 for axis in range(values.ndim)]) for dim in (source, target)]
    chosen = jax.random.permutation(rng, blocks)[partner]
    strong = (owner == chosen) | (owner == (partner + blocks // 2) % blocks)
    return jnp.where(strong, factor * values, values)


def shard_levels(own_key, extent, pieces, smallest, largest):
    level, own = 1.0, jax.random.fold_in(own_key, 6)
    for axis_at, shards_of in pieces:
        draws = jnp.exp(jax.random.uniform(jax.random.fold_in(own, axis_at), (shards_of,), jnp.float32, smallest / len(pieces), largest / len(pieces)))
        level = level * jnp.repeat(draws, extent[axis_at] // shards_of).reshape([-1 if axis == axis_at else 1 for axis in range(len(extent))])
    return level


def profile(count, total, bound, slope):
    weights = [(1 << 20) // math.isqrt(grade ** slope) + 1 for grade in range(2, count + 1)]
    spare, holding = total - bound - (count - 1), [1] * (count - 1)
    while spare > 0:
        candidates = [i for i in range(count - 1) if holding[i] < bound]
        pool, remaining = sum([weights[i] for i in candidates]), spare
        for i in candidates:
            addition = min(bound - holding[i], max(1, remaining * weights[i] // pool), spare)
            holding[i] = holding[i] + addition
            spare = spare - addition
    return np.array([bound] + holding)


def uneven(stream_key, amount, total, most, slope):
    if amount == 2:
        one = jax.random.randint(stream_key, (), max(1, total - most), min(most, total - 1) + 1)
        return jnp.stack([one, total - one])
    tallies = jnp.asarray(profile(amount, total, most, slope), jnp.int32)
    pairs = (amount - 1) // 2
    source_of, receiver = tallies[1:1 + 2 * pairs:2], tallies[2:2 + 2 * pairs:2]
    slack = jnp.minimum(source_of - 1, most - receiver)
    passed = jax.random.randint(jax.random.fold_in(stream_key, 1), (pairs,), 0, 1 << 20) % (slack + 1)
    tallies = tallies.at[1:1 + 2 * pairs:2].set(source_of - passed).at[2:2 + 2 * pairs:2].set(receiver + passed)
    return tallies[jax.random.permutation(jax.random.fold_in(stream_key, 2), amount)]


def centred(key, dims, scale, limit, shards=(), kind=jnp.bfloat16):
    array = scale * jax.random.normal(key, dims, jnp.float32)
    if shards:
        array = array * shard_levels(key, dims, shards, -0.22, 0.18)
    return jnp.clip(array, -limit, limit).astype(kind)


def heavy_noise(rng, shape, width, most, shards, heavy, held_as=jnp.bfloat16):
    values = width * jax.random.normal(rng, shape, jnp.float32)
    if shards:
        values = values * shard_levels(rng, shape, shards, -0.22, 0.18)
    return jnp.clip(raised(values, jax.random.fold_in(rng, 3), *heavy), -most, most).astype(held_as)


def setup_inputs(seed: int = 0) -> dict:
    streams_of = jax.random.split(jax.random.key(seed), 18)
    return {
        "tokens": centred(streams_of[0], (TOKENS, D), 1.0, 6.0, ((0, 32),)),
        "block_ids": jax.vmap(lambda own: jnp.searchsorted(jnp.cumsum(uneven(own, LENGTH // BLOCK, LENGTH, 2 * BLOCK, 0)), jnp.arange(LENGTH), side="right"))(jax.random.split(streams_of[1], SEQS)).reshape((SEQS, LENGTH)).astype(jnp.int32),
        "expert_ids": draw_expert_ids(jax.random.fold_in(streams_of[17], 71), 0),
        "cotangent": heavy_noise(streams_of[3], (TOKENS, D), 1.0, 6.0, ((0, 32),), (0, 1, 32, 2.75)),
        "norm_gain": jnp.clip(1.0 + 0.1 * jax.random.normal(streams_of[4], (D,), jnp.float32), 0.5, 1.5).astype(jnp.bfloat16),
        "norm_shift": centred(streams_of[5], (D,), 0.01, 0.059814453, ((0, 32),)),
        "w_query": centred(streams_of[6], (D, D), D ** -0.5, 0.1875, ((0, 4), (1, 8))),
        "w_key": centred(streams_of[7], (D, D), D ** -0.5, 0.1875, ((0, 4), (1, 8))),
        "w_value": centred(streams_of[8], (D, D), D ** -0.5, 0.1875, ((0, 4), (1, 8))),
        "w_output": centred(streams_of[9], (D, D), (max(1, 16 * D // LENGTH)) ** -0.5, 2.0, ((0, 4), (1, 8))),
        "centroids": centred(streams_of[10], (EXPERTS, D), (4 * D) ** -0.5, 0.09375, ((0, 8), (1, 4))),
        "expert_gain": jnp.clip(1.0 + 0.1 * jax.random.normal(streams_of[11], (EXPERTS, 2, D), jnp.float32), 0.5, 1.5).astype(jnp.bfloat16),
        "expert_shift": centred(streams_of[12], (EXPERTS, 2, D), 0.1, 0.59765625, ((0, 8), (2, 4))),
        "w_in": centred(streams_of[13], (EXPERTS, 2, D, FF), D ** -0.5, 0.1875, ((0, 8), (3, 4))),
        "b_in": centred(streams_of[14], (EXPERTS, 2, FF), 0.1, 0.59765625, ((0, 8), (2, 4))),
        "w_back": centred(streams_of[15], (EXPERTS, 2, FF, D), FF ** -0.5, 0.09375, ((0, 8), (2, 4))),
        "b_back": centred(streams_of[16], (EXPERTS, 2, D), 0.1, 0.59765625, ((0, 8), (2, 4))),
    }


@jax.custom_vjp
def low(v):
    return lax.optimization_barrier(v.astype(jnp.bfloat16)).astype(jnp.float32)

@jax.custom_vjp
def low_back(v):
    return v

def low_keep(v):
    return (low(v), None)

def low_pass(kept, grad):
    return (grad,)

def back_keep(v):
    return (v, None)

def back_low(kept, grad):
    return (low(grad),)
low.defvjp(low_keep, low_pass)
low_back.defvjp(back_keep, back_low)
EPS = 1e-05
NEG = -1e+30
HIGH = lax.Precision.HIGHEST

def norm_rows(stream, gain_vec, shift_vec):
    center = stream - lax.optimization_barrier(jnp.mean(stream, axis=-1, keepdims=True))
    spread = lax.optimization_barrier(jnp.mean(center * center, axis=-1, keepdims=True))
    return center * lax.rsqrt(spread + EPS) * gain_vec + shift_vec

def attend_block(block_items, key_heads, value_heads, seg_keys):
    query_block, seg_block = block_items
    head_size = query_block.shape[-1]
    scores = jnp.einsum('qhd,khd->hqk', query_block, key_heads, precision=HIGH) * head_size ** (-0.5)
    scores = low_back(scores)
    allowed = seg_keys[None, None, :] <= seg_block[None, :, None]
    scores = jnp.where(allowed, scores, NEG)
    highest = lax.optimization_barrier(jnp.max(scores, axis=2, keepdims=True))
    weights = jnp.exp(scores - highest)
    softmax_out = low(weights / lax.optimization_barrier(jnp.sum(weights, axis=2, keepdims=True)))
    return jnp.einsum('hqk,khd->qhd', softmax_out, value_heads, precision=HIGH)

def attend_sequence(members):
    query_seq, key_seq, value_seq, seg_seq = members
    length = query_seq.shape[0]
    block_rows = math.gcd(length, 512)
    query_blocks = query_seq.reshape((length // block_rows, block_rows) + query_seq.shape[1:])
    seg_blocks = seg_seq.reshape(length // block_rows, block_rows)

    def one_block(block_items):
        return attend_block(block_items, key_seq, value_seq, seg_seq)
    result = lax.map(jax.checkpoint(one_block), (query_blocks, seg_blocks))
    return result.reshape(query_seq.shape)

def one_expert(members):
    stream, gains, shifts, weights_in, biases_in, weights_back, biases_back = members
    for sublayer in range(2):
        normed_expert = low(norm_rows(stream, gains[sublayer], shifts[sublayer]))
        pre_act = low_back(jnp.dot(normed_expert, weights_in[sublayer], precision=HIGH) + biases_in[sublayer])
        hidden = low(jax.nn.gelu(pre_act, approximate=False))
        branch = low_back(jnp.dot(hidden, weights_back[sublayer], precision=HIGH))
        stream = stream + branch + biases_back[sublayer]
    return low(low_back(stream))

def forward(tokens, norm_gain, norm_shift, w_query, w_key, w_value, w_output, centroids, expert_gain, expert_shift, w_in, b_in, w_back, b_back, block_ids, expert_ids):
    count_tok, model_width = tokens.shape
    head_size = model_width // HEADS
    normed = low(norm_rows(tokens, norm_gain, norm_shift))
    queries = low(low_back(jnp.dot(normed, w_query, precision=HIGH)))
    key_rows = low(low_back(jnp.dot(normed, w_key, precision=HIGH)))
    value_rows = low(low_back(jnp.dot(normed, w_value, precision=HIGH)))
    seq_count, length = block_ids.shape
    four_dims = (seq_count, length, HEADS, head_size)
    seg_float = block_ids.astype(jnp.float32)
    context = lax.map(jax.checkpoint(attend_sequence), (queries.reshape(four_dims), key_rows.reshape(four_dims), value_rows.reshape(four_dims), seg_float))
    context = low(low_back(context.reshape(count_tok, model_width)))
    attn_out = low_back(jnp.dot(context, w_output, precision=HIGH))
    residual = tokens + attn_out
    shared = low(residual)
    logits = lax.optimization_barrier(jnp.sum(shared * centroids[expert_ids], axis=1))
    gate_vals = jax.nn.sigmoid(logits)
    sent_rows = low_back(shared)
    sorting = jnp.argsort(expert_ids, stable=True)
    inverse = jnp.argsort(sorting, stable=True)
    experts = centroids.shape[0]
    grouped = sent_rows[sorting].reshape(experts, count_tok // experts, model_width)
    processed = lax.map(jax.checkpoint(one_expert), (grouped, expert_gain, expert_shift, w_in, b_in, w_back, b_back))
    back_vals = processed.reshape(count_tok, model_width)[inverse]
    return residual + gate_vals[:, None] * back_vals

def reference(tokens, block_ids, expert_ids, cotangent, norm_gain, norm_shift, w_query, w_key, w_value, w_output, centroids, expert_gain, expert_shift, w_in, b_in, w_back, b_back):
    floats = (tokens.astype(jnp.float32), norm_gain.astype(jnp.float32), norm_shift.astype(jnp.float32), w_query.astype(jnp.float32), w_key.astype(jnp.float32), w_value.astype(jnp.float32), w_output.astype(jnp.float32), centroids.astype(jnp.float32), expert_gain.astype(jnp.float32), expert_shift.astype(jnp.float32), w_in.astype(jnp.float32), b_in.astype(jnp.float32), w_back.astype(jnp.float32), b_back.astype(jnp.float32))

    def closed(*values):
        return forward(*values, block_ids, expert_ids)
    result, pullback = jax.vjp(closed, *floats)
    grad_list = pullback(cotangent.astype(jnp.float32))
    return (result.astype(jnp.bfloat16), grad_list[0], grad_list[1], grad_list[2], grad_list[3], grad_list[4], grad_list[5], grad_list[6], grad_list[7], grad_list[8], grad_list[9], grad_list[10], grad_list[11], grad_list[12], grad_list[13])
```

```python
import functools

import jax
import jax.numpy as jnp
from jax import lax
from jax.experimental import pallas as pl
from jax.experimental.pallas import tpu as pltpu
from jax.sharding import PartitionSpec as P

HEADS = 16
EPS = 1e-05
NEG = -1e30
BF = jnp.bfloat16
F32 = jnp.float32
NT = (((1,), (1,)), ((), ()))
NN = (((1,), (0,)), ((), ()))
VMEM_BYTES = 56 * 1024 * 1024


def dot(left, right, dims=NN):
    return lax.dot_general(left, right, dims, preferred_element_type=F32)


def add_low(left, right):
    return (left.astype(F32) + right.astype(F32)).astype(BF)


def send_xor(value, axis, size, mask):
    return lax.ppermute(value, axis, [(i, i ^ mask) for i in range(size)])


def bits_of(size):
    return list(range(size.bit_length() - 1))


def gather_path(value, axis, size, bits):
    held = {0: value}
    for bit in bits:
        held.update({m | (1 << bit): send_xor(v, axis, size, 1 << bit) for m, v in list(held.items())})
    return [held[m] for m in range(size)]


def scatter_path(blocks, axis, size, bits):
    held = dict(enumerate(blocks))
    for bit in bits:
        leaving = {m: v for m, v in held.items() if (m >> bit) & 1}
        held = {m: v for m, v in held.items() if not (m >> bit) & 1}
        for m, v in leaving.items():
            keep = m & ~(1 << bit)
            held[keep] = add_low(held[keep], send_xor(v, axis, size, 1 << bit))
    return held[0]


def dual_gather(value, axis, size):
    half = value.shape[0] // 2
    bits = bits_of(size)
    first = gather_path(value[:half], axis, size, bits)
    second = gather_path(value[half:], axis, size, bits[::-1])
    return jnp.concatenate(first + second)


def dual_scatter(partial, axis, size):
    half = partial.shape[0] // (2 * size)
    pieces = partial.reshape(2 * size, half, partial.shape[1])
    bits = bits_of(size)
    first = scatter_path([pieces[m] for m in range(size)], axis, size, bits)
    second = scatter_path([pieces[size + m] for m in range(size)], axis, size, bits[::-1])
    return jnp.concatenate([first, second])


def direct_gather(value, axis, size):
    return [value] + [send_xor(value, axis, size, m) for m in range(1, size)]


def direct_exchange(blocks, axis, size):
    return [blocks[0]] + [send_xor(blocks[m], axis, size, m) for m in range(1, size)]


def reorder(stacked, mine, size):
    return jnp.concatenate(
        [lax.dynamic_index_in_dim(stacked, mine ^ j, 0, keepdims=True) for j in range(size)]
    )


def swap_core(value, size):
    return send_xor(value, "col", size, 1)


def right_pairs(first, last, size):
    return [(i, i + 2) for i in range(size) if first <= i // 2 <= last]


def left_pairs(first, last, size):
    return [(i, i - 2) for i in range(size) if first <= i // 2 <= last]


def line_order(mine, size):
    chips = size // 2
    return [
        ((mine // 2 + turn) % chips) * 2 + ((mine % 2) ^ core)
        for turn in range(chips)
        for core in range(2)
    ]


def line_gather(value, size):
    chips = size // 2
    right, left = [value], [value]
    for step in range(1, chips):
        from_left = lax.ppermute(right[-1], "col", right_pairs(step - 1, chips - 2, size))
        from_right = lax.ppermute(left[-1], "col", left_pairs(1, chips - step, size))
        from_left, from_right = lax.optimization_barrier((from_left, from_right))
        right.append(from_left)
        left.append(from_right)
    merged = [value] + [left[s] + right[chips - s] for s in range(1, chips)]
    return [v for m in merged for v in (m, swap_core(m, size))]


def line_scatter(blocks, size):
    chips = size // 2
    halves = [
        add_low(blocks[2 * turn], swap_core(blocks[2 * turn + 1], size)) for turn in range(chips)
    ]
    from_left = from_right = None
    for step in range(1, chips):
        to_right = halves[chips - step] if step == 1 else add_low(from_left, halves[chips - step])
        to_left = halves[step] if step == 1 else add_low(from_right, halves[step])
        to_right, to_left = lax.optimization_barrier((to_right, to_left))
        from_left = lax.ppermute(to_right, "col", right_pairs(0, min(step - 1, chips - 2), size))
        from_right = lax.ppermute(to_left, "col", left_pairs(max(chips - step, 1), chips - 1, size))
        from_left, from_right = lax.optimization_barrier((from_left, from_right))
    return halves[0].astype(F32) + from_left.astype(F32) + from_right.astype(F32)


def col_order(mine, size):
    return line_order(mine, size) if size == 8 else [mine ^ m for m in range(size)]


def col_gather(value, size):
    if size == 8:
        return line_gather(value, size)
    return gather_path(value, "col", size, bits_of(size))


def col_scatter(blocks, size):
    if size == 8:
        return line_scatter(blocks, size)
    return scatter_path(blocks, "col", size, bits_of(size)).astype(F32)


def layer_stats(stream):
    center = stream - jnp.mean(stream, axis=-1, keepdims=True)
    inv_root = lax.rsqrt(jnp.mean(center * center, axis=-1, keepdims=True) + EPS)
    return (center * inv_root, inv_root)


def norm_back(grad_normed, unit_rows, inv_root, gain_full):
    grad_unit = grad_normed * gain_full
    mean_first = jnp.mean(grad_unit, axis=-1, keepdims=True)
    mean_second = jnp.mean(grad_unit * unit_rows, axis=-1, keepdims=True)
    return inv_root * (grad_unit - mean_first - unit_rows * mean_second)


def project_kernel(scale, x_ref, gain_ref, shift_ref, wq_ref, wk_ref, wv_ref, normed_ref, q_ref, k_ref, v_ref, kt_ref, vt_ref):
    unit_rows, unused = layer_stats(x_ref[...].astype(F32))
    normed = (unit_rows * gain_ref[...] + shift_ref[...]).astype(BF)
    normed_ref[...] = normed
    q_ref[...] = (dot(normed, wq_ref[...]).astype(BF).astype(F32) * scale).astype(BF)
    keys = dot(normed, wk_ref[...])
    values = dot(normed, wv_ref[...])
    k_ref[...] = keys.astype(BF)
    v_ref[...] = values.astype(BF)
    kt_ref[...] = keys.T.astype(BF)
    vt_ref[...] = values.T.astype(BF)


def project(block, gain, shift, wq, wk, wv, rows, scale):
    width = block.shape[1]
    fw = wq.shape[1]
    fixed = lambda *shape: pl.BlockSpec(shape, lambda i: (0,) * len(shape))
    return pl.pallas_call(
        functools.partial(project_kernel, scale),
        grid=(1,),
        in_specs=[
            fixed(rows, width),
            fixed(1, width),
            fixed(1, width),
            fixed(width, fw),
            fixed(width, fw),
            fixed(width, fw),
        ],
        out_specs=[
            fixed(rows, width),
            fixed(rows, fw),
            fixed(rows, fw),
            fixed(rows, fw),
            fixed(fw, rows),
            fixed(fw, rows),
        ],
        out_shape=[
            jax.ShapeDtypeStruct((rows, width), BF),
            jax.ShapeDtypeStruct((rows, fw), BF),
            jax.ShapeDtypeStruct((rows, fw), BF),
            jax.ShapeDtypeStruct((rows, fw), BF),
            jax.ShapeDtypeStruct((fw, rows), BF),
            jax.ShapeDtypeStruct((fw, rows), BF),
        ],
        cost_estimate=pl.CostEstimate(
            flops=2 * rows * width * fw * 3 + 10 * rows * width,
            bytes_accessed=2 * (2 * rows * width + 3 * width * fw + 5 * rows * fw),
            transcendentals=0,
        ),
        name="project",
    )(block, gain, shift, wq, wk, wv)


def split_lanes(rows, count):
    width = rows.shape[1] // count
    if count == 1:
        return rows
    head_of = lax.broadcasted_iota(jnp.int32, rows.shape, 1) // width
    return jnp.concatenate(
        [jnp.where(head_of == h, rows, jnp.zeros_like(rows)) for h in range(count)], axis=0
    )


def split_rows(cols, count):
    width = cols.shape[0] // count
    if count == 1:
        return cols
    head_of = lax.broadcasted_iota(jnp.int32, cols.shape, 0) // width
    return jnp.concatenate(
        [jnp.where(head_of == h, cols, jnp.zeros_like(cols)) for h in range(count)], axis=1
    )


def attend_kernel(heads, pos_ref, out_ref_index, count_ref, q_ref, k_ref, vt_ref, row_ids_ref, col_ids_ref, ctx_ref, low_ref, lse_ref):
    i = pl.program_id(0)
    queries = split_lanes(q_ref[0], heads)
    rows = q_ref.shape[1]
    fw = q_ref.shape[2]
    head = fw // heads
    row_ids = jnp.concatenate([row_ids_ref[0]] * heads, axis=1)

    def step(j, state):
        run_max, run_sum, held = state
        at = pos_ref[j]
        scores = dot(k_ref[at], queries, NT)
        scores = jnp.where(col_ids_ref[at] <= row_ids, scores, NEG)
        new_max = jnp.maximum(run_max, jnp.max(scores, axis=0, keepdims=True))
        weights = jnp.exp(scores - new_max)
        factor = jnp.exp(run_max - new_max)
        new_sum = run_sum * factor + jnp.sum(weights, axis=0, keepdims=True)
        low = weights.astype(BF)
        values = vt_ref[at]
        new_held = tuple(
            held[h] * factor[:, h * rows : (h + 1) * rows]
            + dot(values[h * head : (h + 1) * head], low[:, h * rows : (h + 1) * rows])
            for h in range(heads)
        )
        return new_max, new_sum, new_held

    start = (
        jnp.full((1, heads * rows), NEG, F32),
        jnp.zeros((1, heads * rows), F32),
        tuple(jnp.zeros((head, rows), F32) for h in range(heads)),
    )
    run_max, run_sum, held = lax.fori_loop(0, count_ref[i], step, start)
    for h in range(heads):
        result = held[h] / run_sum[:, h * rows : (h + 1) * rows]
        ctx_ref[0, h * head : (h + 1) * head, :] = result
        low_ref[0, h * head : (h + 1) * head, :] = result.astype(BF)
    lse_ref[0] = run_max + jnp.log(run_sum)


def attend(q, k, vt, row_ids, col_ids, pos, rel, counts, heads):
    total, rows, fw = q.shape
    whole = lambda *shape: pl.BlockSpec(shape, lambda i, pos, rel, counts: (0,) * len(shape))
    pairs = total * rows * total * rows * heads
    return pl.pallas_call(
        functools.partial(attend_kernel, heads),
        grid_spec=pltpu.PrefetchScalarGridSpec(
            num_scalar_prefetch=3,
            grid=(total,),
            in_specs=[
                pl.BlockSpec((1, rows, fw), lambda i, pos, rel, counts: (pos[i], 0, 0)),
                whole(total, rows, fw),
                whole(total, fw, rows),
                pl.BlockSpec((1, 1, rows), lambda i, pos, rel, counts: (pos[i], 0, 0)),
                whole(total, rows, 1),
            ],
            out_specs=[
                pl.BlockSpec((1, fw, rows), lambda i, pos, rel, counts: (i, 0, 0)),
                pl.BlockSpec((1, fw, rows), lambda i, pos, rel, counts: (rel[i], 0, 0)),
                pl.BlockSpec((1, 1, heads * rows), lambda i, pos, rel, counts: (i, 0, 0)),
            ],
        ),
        out_shape=[
            jax.ShapeDtypeStruct((total, fw, rows), F32),
            jax.ShapeDtypeStruct((total, fw, rows), BF),
            jax.ShapeDtypeStruct((total, 1, heads * rows), F32),
        ],
        compiler_params=pltpu.CompilerParams(vmem_limit_bytes=VMEM_BYTES),
        cost_estimate=pl.CostEstimate(
            flops=2 * pairs * 128, bytes_accessed=10 * total * rows * fw, transcendentals=pairs // 2
        ),
        name="attend",
    )(pos, rel, counts, q, k, vt, row_ids, col_ids)


def attend_back_kernel(
    heads, scale, pos_ref, rel_ref, first_ref,
    q_ref, k_ref, v_ref, kt_ref, ctx_ref, grad_ref, lse_ref, row_ids_ref, col_ids_ref,
    dq_ref, dk_ref, dv_ref, q_all, grad_all, delta_all, dq_all,
):
    j = pl.program_id(0)
    total, rows, fw = q_ref.shape
    head = fw // heads

    @pl.when(j == 0)
    def prepare():
        def one(i, unused):
            at = pos_ref[i]
            q_all[i] = split_lanes(q_ref[at], heads)
            grad = grad_ref[rel_ref[i]]
            grad_all[i] = split_rows(grad, heads)
            product = grad.astype(F32) * ctx_ref[i]
            delta_all[i] = jnp.concatenate(
                [
                    jnp.sum(product[h * head : (h + 1) * head], axis=0, keepdims=True)
                    for h in range(heads)
                ],
                axis=1,
            )
            dq_all[i] = jnp.zeros((fw, rows), F32)
            return unused

        lax.fori_loop(0, total, one, 0)

    at_key = pos_ref[j]
    keys = k_ref[at_key]
    values = v_ref[at_key]
    keys_t = kt_ref[at_key]
    col_ids = col_ids_ref[at_key]

    def step(i, state):
        dk, dv = state
        queries = q_all[i]
        grads = grad_all[i]
        row_ids = jnp.concatenate([row_ids_ref[pos_ref[i]]] * heads, axis=1)
        scores = dot(keys, queries, NT)
        probs = jnp.exp(jnp.where(col_ids <= row_ids, scores - lse_ref[i], NEG))
        grad_probs = dot(values, grads)
        grad_scores = (probs * (grad_probs - delta_all[i])).astype(BF)
        dv = dv + dot(probs.astype(BF), grads, NT)
        dk = dk + dot(grad_scores, queries)
        for h in range(heads):
            dq_all[i, h * head : (h + 1) * head, :] += dot(
                keys_t[h * head : (h + 1) * head], grad_scores[:, h * rows : (h + 1) * rows]
            )
        return dk, dv

    zero = jnp.zeros((rows, fw), F32)
    dk, dv = lax.fori_loop(first_ref[j], total, step, (zero, zero))
    dk_ref[0] = dk.astype(BF)
    dv_ref[0] = dv.astype(BF)

    @pl.when(j == total - 1)
    def finish():
        def one(i, unused):
            dq_ref[pos_ref[i]] = (dq_all[i] * scale).T.astype(BF)
            return unused

        lax.fori_loop(0, total, one, 0)


def attend_back(q, k, v, kt, ctx, grad, lse, row_ids, col_ids, pos, rel, first, heads, scale):
    total, rows, fw = q.shape
    whole = lambda *shape: pl.BlockSpec(shape, lambda j, pos, rel, first: (0,) * len(shape))
    at_pos = pl.BlockSpec((1, rows, fw), lambda j, pos, rel, first: (pos[j], 0, 0))
    pairs = total * rows * total * rows * heads
    return pl.pallas_call(
        functools.partial(attend_back_kernel, heads, scale),
        grid_spec=pltpu.PrefetchScalarGridSpec(
            num_scalar_prefetch=3,
            grid=(total,),
            in_specs=[
                whole(total, rows, fw),
                whole(total, rows, fw),
                whole(total, rows, fw),
                whole(total, fw, rows),
                whole(total, fw, rows),
                whole(total, fw, rows),
                whole(total, 1, heads * rows),
                whole(total, 1, rows),
                whole(total, rows, 1),
            ],
            out_specs=[whole(total, rows, fw), at_pos, at_pos],
            scratch_shapes=[
                pltpu.VMEM((total, heads * rows, fw), BF),
                pltpu.VMEM((total, fw, heads * rows), BF),
                pltpu.VMEM((total, 1, heads * rows), F32),
                pltpu.VMEM((total, fw, rows), F32),
            ],
        ),
        out_shape=[jax.ShapeDtypeStruct((total, rows, fw), BF)] * 3,
        compiler_params=pltpu.CompilerParams(vmem_limit_bytes=VMEM_BYTES),
        cost_estimate=pl.CostEstimate(
            flops=5 * pairs * 128, bytes_accessed=20 * total * rows * fw, transcendentals=pairs // 2
        ),
        name="attend_back",
    )(pos, rel, first, q, k, v, kt, ctx, grad, lse, row_ids, col_ids)


def gelu_slope(pre_act):
    return (
        0.5 * (1.0 + lax.erf(pre_act * 0.7071067811865476))
        + pre_act * jnp.exp(-0.5 * pre_act * pre_act) * 0.3989422804014327
    )


def shards(
    tokens,
    block_ids,
    expert_ids,
    cotangent,
    norm_gain,
    norm_shift,
    w_query,
    w_key,
    w_value,
    w_output,
    centroids,
    expert_gain,
    expert_shift,
    w_in,
    b_in,
    w_back,
    b_back,
):
    rows_n = lax.axis_size("row")
    cols_n = lax.axis_size("col")
    r = lax.axis_index("row")
    c = lax.axis_index("col")
    tok, width = tokens.shape
    fw = width // cols_n
    heads = HEADS // cols_n
    scale = float(width // HEADS) ** (-0.5)
    part = width // rows_n
    own = norm_gain.shape[0]
    slot = tok // cols_n

    packet = jnp.concatenate([norm_gain, norm_shift, centroids[0]])[None]
    packet = jnp.concatenate(direct_gather(packet, "row", rows_n))[None]
    packet = reorder(jnp.concatenate(direct_gather(packet, "col", cols_n)), c, cols_n)
    packet = reorder(packet.transpose(1, 0, 2), r, rows_n)
    gain_attn = packet[:, :, :own].reshape(1, width).astype(F32)
    shift_attn = packet[:, :, own : 2 * own].reshape(1, width).astype(F32)
    full_centroids = packet[:, :, 2 * own :].transpose(1, 0, 2).reshape(cols_n, width)
    experts = jnp.concatenate([expert_gain[0], expert_shift[0], b_back[0]])
    experts = jnp.stack(direct_gather(experts, "row", rows_n))
    experts = reorder(experts, r, rows_n).transpose(1, 0, 2).reshape(6, width).astype(F32)

    ids = jnp.pad(block_ids.astype(BF), ((0, 15), (0, width - tok)))
    blocks = col_gather(jnp.concatenate([tokens, ids]), cols_n)
    order = jnp.stack(col_order(c, cols_n))
    w_cat = jnp.concatenate([w_query, w_key, w_value], axis=1)
    w_cat = jnp.stack(direct_gather(w_cat, "row", rows_n))
    w_cat = reorder(w_cat, r, rows_n).reshape(width, 3 * fw)
    wq, wk, wv = w_cat[:, :fw], w_cat[:, fw : 2 * fw], w_cat[:, 2 * fw :]
    projected = [project(b, gain_attn, shift_attn, wq, wk, wv, tok, scale) for b in blocks]
    normed, q, k, v, kt, vt = [jnp.stack([p[n] for p in projected]) for n in range(6)]
    row_ids = jnp.stack([b[tok, :tok] for b in blocks]).astype(F32)
    pos = jnp.zeros((cols_n,), jnp.int32).at[order].set(jnp.arange(cols_n, dtype=jnp.int32))
    rel = jnp.arange(cols_n, dtype=jnp.int32) ^ c
    lowest = row_ids[:, 0][pos]
    highest = row_ids[:, -1][pos]
    counts = jnp.sum((lowest[None, :] <= highest[:, None]).astype(jnp.int32), axis=1)
    first = jnp.sum((highest[None, :] < lowest[:, None]).astype(jnp.int32), axis=1)
    col_ids = row_ids[:, :, None]
    row_ids = row_ids[:, None, :]

    pieces = direct_gather(w_output, "row", rows_n)
    pieces = jnp.stack(pieces)
    pieces = reorder(pieces, r, rows_n).reshape(width, fw)
    full_output = jnp.stack(direct_gather(pieces, "col", cols_n))
    full_output = reorder(full_output, c, cols_n)
    full_output = full_output.reshape(cols_n, cols_n, fw, fw).transpose(1, 2, 0, 3)
    full_output = full_output.reshape(cols_n, fw, width)
    full_output = reorder(full_output, c, cols_n).reshape(width, width)

    ctx, ctx_low, lse = attend(q, k, vt, row_ids, col_ids, pos, rel, counts, heads)
    ctx_mine = jnp.concatenate(direct_exchange([ctx_low[m] for m in range(cols_n)], "col", cols_n))
    inputs = tokens.astype(F32)
    residual = inputs + lax.dot_general(
        ctx_mine, full_output, (((0,), (0,)), ((), ())), preferred_element_type=F32
    )
    shared = residual.astype(BF)
    shared_full = shared.astype(F32)

    onehot = expert_ids[:, None] == jnp.arange(cols_n, dtype=jnp.int32)[None, :]
    onehot_low = onehot.astype(BF)
    below = (jnp.arange(tok)[:, None] > jnp.arange(tok)[None, :]).astype(BF)
    before = dot(below, onehot_low)
    rank = jnp.sum(jnp.where(onehot, before, 0.0), axis=1).astype(jnp.int32)
    place = (expert_ids ^ c) * slot + rank
    route = (jnp.arange(tok, dtype=jnp.int32)[:, None] == place[None, :]).astype(BF)
    unroute = (place[:, None] == jnp.arange(tok, dtype=jnp.int32)[None, :]).astype(BF)
    cent_rows = dot(onehot_low, full_centroids)
    gate = jax.nn.sigmoid(jnp.sum(shared_full * cent_rows, axis=1, keepdims=True))
    grad_out = cotangent.astype(F32)
    grad_back = (grad_out * gate).astype(BF)

    def to_experts(rows):
        moved = dot(route, rows).astype(BF).reshape(cols_n, slot, width)
        return jnp.concatenate(direct_exchange([moved[m] for m in range(cols_n)], "col", cols_n))

    def from_experts(rows):
        moved = rows.reshape(cols_n, slot, width)
        back = direct_exchange([moved[m] for m in range(cols_n)], "col", cols_n)
        return dot(unroute, jnp.concatenate(back))

    stream = to_experts(shared).astype(F32)
    grad_stream = to_experts(grad_back).astype(F32)

    stored = []
    for sub in range(2):
        unit_rows, inv_root = layer_stats(stream)
        own_normed = (unit_rows * experts[sub] + experts[2 + sub]).astype(BF)
        normed_all = dual_gather(own_normed, "row", rows_n)
        pre_act = dot(normed_all, w_in[0, sub]) + b_in[0, sub].astype(F32)
        hidden = jax.nn.gelu(pre_act, approximate=False).astype(BF)
        branch = dual_scatter(dot(hidden, w_back[0, sub]).astype(BF), "row", rows_n)
        stored.append((unit_rows, inv_root, normed_all, pre_act, hidden))
        stream = stream + branch.astype(F32) + experts[4 + sub]
    back_vals = from_experts(stream.astype(BF))
    output = (residual + gate * back_vals).astype(BF)
    grad_logit = jnp.sum(grad_out * back_vals, axis=1, keepdims=True) * gate * (1.0 - gate)

    grads_in, grads_back, grads_bias, small_parts = [None] * 2, [None] * 2, [None] * 2, [None] * 6
    for sub in (1, 0):
        unit_rows, inv_root, normed_all, pre_act, hidden = stored[sub]
        small_parts[4 + sub] = jnp.sum(grad_stream, axis=0)
        grad_branch = dual_gather(grad_stream.astype(BF), "row", rows_n)
        grads_back[sub] = lax.dot_general(
            hidden, grad_branch, (((0,), (0,)), ((), ())), preferred_element_type=F32
        )
        grad_pre_full = dot(grad_branch, w_back[0, sub], NT) * gelu_slope(pre_act)
        grad_pre = grad_pre_full.astype(BF)
        grads_bias[sub] = jnp.sum(grad_pre.astype(F32), axis=0)
        grads_in[sub] = lax.dot_general(
            normed_all, grad_pre, (((0,), (0,)), ((), ())), preferred_element_type=F32
        )
        grad_normed = dual_scatter(dot(grad_pre, w_in[0, sub], NT).astype(BF), "row", rows_n)
        grad_normed = grad_normed.astype(F32)
        small_parts[sub] = jnp.sum(grad_normed * unit_rows, axis=0)
        small_parts[2 + sub] = jnp.sum(grad_normed, axis=0)
        grad_stream = grad_stream + norm_back(grad_normed, unit_rows, inv_root, experts[sub])

    grad_shared = from_experts(grad_stream.astype(BF)) + grad_logit * cent_rows
    grad_residual = grad_out + grad_shared
    part_cent = lax.dot_general(
        onehot.astype(F32),
        grad_logit * shared_full,
        (((0,), (0,)), ((), ())),
        precision=lax.Precision.HIGHEST,
        preferred_element_type=F32,
    )
    grad_attended = grad_residual.astype(BF)

    grad_ctx = dot(full_output, grad_attended, NT).astype(BF).reshape(cols_n, fw, tok)
    grad_ctx = jnp.stack(direct_exchange([grad_ctx[m] for m in range(cols_n)], "col", cols_n))
    dq, dk, dv = attend_back(
        q, k, v, kt, ctx, grad_ctx, lse, row_ids, col_ids, pos, rel, first, heads, scale
    )
    dqkv = jnp.concatenate([dq, dk, dv], axis=2)
    partial = lax.dot_general(
        dqkv, w_cat, (((2,), (1,)), ((), ())), preferred_element_type=F32
    ).astype(BF)
    grad_normed_attn = col_scatter([partial[m] for m in range(cols_n)], cols_n)
    unit_attn, inv_attn = layer_stats(inputs)
    tokens_grad = grad_residual + norm_back(grad_normed_attn, unit_attn, inv_attn, gain_attn)
    part_gain = jnp.sum(grad_normed_attn * unit_attn, axis=0)
    part_shift = jnp.sum(grad_normed_attn, axis=0)

    part_qkv = lax.dot_general(
        normed.reshape(cols_n * tok, width),
        dqkv.reshape(cols_n * tok, 3 * fw),
        (((0,), (0,)), ((), ())),
        preferred_element_type=F32,
    )
    part_qkv = reorder(part_qkv.astype(BF).reshape(rows_n, part, 3 * fw), r, rows_n)
    part_qkv = direct_exchange([part_qkv[m] for m in range(rows_n)], "row", rows_n)
    grad_qkv = sum(p.astype(F32) for p in part_qkv)

    part_output = dot(ctx_mine, grad_attended).astype(BF).reshape(cols_n, fw, width)
    part_output = reorder(part_output, c, cols_n).reshape(rows_n, part, cols_n, fw)
    part_output = reorder(part_output.transpose(2, 0, 1, 3), c, cols_n)
    part_output = direct_exchange([part_output[m] for m in range(cols_n)], "col", cols_n)
    part_output = sum(p.astype(F32) for p in part_output).astype(BF)
    part_output = reorder(part_output, r, rows_n)
    part_output = direct_exchange([part_output[m] for m in range(rows_n)], "row", rows_n)
    grad_output = sum(p.astype(F32) for p in part_output)

    all_rows = jnp.concatenate(
        [
            part_gain.reshape(rows_n, cols_n, own),
            part_shift.reshape(rows_n, cols_n, own),
            part_cent.reshape(cols_n, rows_n, part).transpose(1, 0, 2),
        ],
        axis=2,
    ).reshape(rows_n, cols_n * (2 * own + part))
    expert_rows = jnp.stack(small_parts).reshape(6, rows_n, part).transpose(1, 0, 2)
    packed = jnp.concatenate([all_rows, expert_rows.reshape(rows_n, 6 * part)], axis=1)[:, None]
    packed = reorder(packed, r, rows_n)
    packed = sum(direct_exchange([packed[m] for m in range(rows_n)], "row", rows_n))
    expert_sums = packed[0, cols_n * (2 * own + part) :].reshape(3, 2, part)
    packed = packed[0, : cols_n * (2 * own + part)].reshape(cols_n, 1, 2 * own + part)
    packed = reorder(packed, c, cols_n)
    packed = sum(direct_exchange([packed[m] for m in range(cols_n)], "col", cols_n))[0]

    return (
        output,
        tokens_grad,
        packed[:own],
        packed[own : 2 * own],
        grad_qkv[:, :fw],
        grad_qkv[:, fw : 2 * fw],
        grad_qkv[:, 2 * fw :],
        grad_output,
        packed[None, 2 * own :],
        expert_sums[None, 0],
        expert_sums[None, 1],
        jnp.stack(grads_in)[None],
        jnp.stack(grads_bias)[None],
        jnp.stack(grads_back)[None],
        expert_sums[None, 2],
    )


def solution(mesh):
    placed = (
        P(("row", "col"), None),
        P("row", "col"),
        P(("row", "col")),
        P(("row", "col"), None),
        P(("row", "col")),
        P(("row", "col")),
        P("row", "col"),
        P("row", "col"),
        P("row", "col"),
        P("row", "col"),
        P("col", "row"),
        P("col", None, "row"),
        P("col", None, "row"),
        P("col", None, None, "row"),
        P("col", None, "row"),
        P("col", None, "row", None),
        P("col", None, "row"),
    )
    return jax.shard_map(
        shards,
        mesh=mesh,
        in_specs=placed,
        out_specs=(
            P(("row", "col"), None),
            P(("row", "col"), None),
            P(("row", "col")),
            P(("row", "col")),
            P("row", "col"),
            P("row", "col"),
            P("row", "col"),
            P("row", "col"),
            P("col", "row"),
            P("col", None, "row"),
            P("col", None, "row"),
            P("col", None, None, "row"),
            P("col", None, "row"),
            P("col", None, "row", None),
            P("col", None, "row"),
        ),
        check_vma=False,
    )
```

```python
import functools

import jax
import jax.numpy as jnp
from jax import lax
from jax.experimental import pallas as pl
from jax.experimental.pallas import tpu as pltpu
from jax.sharding import PartitionSpec as P

HEADS = 16
EPS = 1e-05
NEG = -1e30
BF = jnp.bfloat16
F32 = jnp.float32
NT = (((1,), (1,)), ((), ()))
NN = (((1,), (0,)), ((), ()))
LANES = 128


def dot(left, right, dims=NN):
    return lax.dot_general(left, right, dims, preferred_element_type=F32)


def add_low(left, right):
    return (left.astype(F32) + right.astype(F32)).astype(BF)


def send_xor(value, axis, size, mask):
    return lax.ppermute(value, axis, [(i, i ^ mask) for i in range(size)])


def bits_of(size):
    return list(range(size.bit_length() - 1))


def gather_path(value, axis, size, bits):
    held = {0: value}
    for bit in bits:
        held.update({m | (1 << bit): send_xor(v, axis, size, 1 << bit) for m, v in list(held.items())})
    return [held[m] for m in range(size)]


def scatter_path(blocks, axis, size, bits):
    held = dict(enumerate(blocks))
    for bit in bits[:-1]:
        leaving = {m: v for m, v in held.items() if (m >> bit) & 1}
        held = {m: v for m, v in held.items() if not (m >> bit) & 1}
        for m, v in leaving.items():
            keep = m & ~(1 << bit)
            held[keep] = add_low(held[keep], send_xor(v, axis, size, 1 << bit))
    last = 1 << bits[-1]
    return [held[0], send_xor(held[last], axis, size, last)]


def direct_gather(value, axis, size):
    return [value] + [send_xor(value, axis, size, m) for m in range(1, size)]


def direct_exchange(blocks, axis, size):
    return [blocks[0]] + [send_xor(blocks[m], axis, size, m) for m in range(1, size)]


def reorder(stacked, mine, size):
    return jnp.concatenate(
        [lax.dynamic_index_in_dim(stacked, mine ^ j, 0, keepdims=True) for j in range(size)]
    )


def swap_core(value, size):
    return send_xor(value, "col", size, 1)


def right_pairs(first, last, size):
    return [(i, i + 2) for i in range(size) if first <= i // 2 <= last]


def left_pairs(first, last, size):
    return [(i, i - 2) for i in range(size) if first <= i // 2 <= last]


def line_order(mine, size):
    chips = size // 2
    return [
        ((mine // 2 + turn) % chips) * 2 + ((mine % 2) ^ core)
        for turn in range(chips)
        for core in range(2)
    ]


def col_order(mine, size):
    return line_order(mine, size) if size == 8 else [mine ^ m for m in range(size)]


def col_gather(value, size):
    return gather_path(value, "col", size, bits_of(size))


def col_scatter(blocks, size):
    mine, last = scatter_path(blocks, "col", size, bits_of(size))
    return mine.astype(F32) + last.astype(F32)


def layer_stats(stream):
    center = stream - jnp.mean(stream, axis=-1, keepdims=True)
    inv_root = lax.rsqrt(jnp.mean(center * center, axis=-1, keepdims=True) + EPS)
    return (center * inv_root, inv_root)


def norm_back(grad_normed, unit_rows, inv_root, gain_full):
    grad_unit = grad_normed * gain_full
    mean_first = jnp.mean(grad_unit, axis=-1, keepdims=True)
    mean_second = jnp.mean(grad_unit * unit_rows, axis=-1, keepdims=True)
    return inv_root * (grad_unit - mean_first - unit_rows * mean_second)


ANY = pl.BlockSpec(memory_space=pl.ANY)
HBM = pl.BlockSpec(memory_space=pltpu.HBM)
VMEM = pl.BlockSpec(memory_space=pltpu.VMEM)
SMEM = pl.BlockSpec(memory_space=pltpu.SMEM)


def shape(dims, kind):
    return jax.ShapeDtypeStruct(dims, kind)


def params(mib):
    return pltpu.CompilerParams(vmem_limit_bytes=mib * 1024 * 1024)


def copies_of(pairs, sems):
    return [pltpu.make_async_copy(s, d, sems.at[n]) for n, (s, d) in enumerate(pairs)]


def begin(pairs, sems):
    copies = copies_of(pairs, sems)
    for copy in copies:
        copy.start()
    return copies


def finish(copies):
    for copy in copies:
        copy.wait()


def arrange_kernel(count, rows, me_ref, *refs):
    out_ref = refs[count]
    for m in range(count):
        at = pl.ds(pl.multiple_of((me_ref[0] ^ m) * rows, rows), rows)
        out_ref[at, :] = refs[m][:rows, :]


def arrange_rows(pieces, rows, me):
    count = len(pieces)
    cols = pieces[0].shape[1]
    return pl.pallas_call(
        functools.partial(arrange_kernel, count, rows),
        in_specs=[SMEM] + [VMEM] * count,
        out_specs=VMEM,
        out_shape=shape((count * rows, cols), pieces[0].dtype),
        name="arrange_rows",
    )(me, *pieces)


def tile_rows(tiles_ref, block):
    return jnp.concatenate([tiles_ref[block, col] for col in range(tiles_ref.shape[1])], axis=1)


def scalar_lanes(values):
    high = values.astype(BF).astype(F32)
    lane = lax.broadcasted_iota(jnp.int32, (values.shape[0], LANES), 1)
    return jnp.where(lane == 0, high, jnp.where(lane == 1, values - high, 0.0)).astype(BF)


def forward_kernel(tiles_ref, tokens_ref, ctx_ref, cent_ref, onehot_ref, route_ref, residual_ref, gate_ref, moved_ref):
    rows_n, unused, part, unused = tiles_ref.shape
    held = tokens_ref[...].astype(F32)
    for n in range(rows_n):
        held = held + lax.dot_general(
            ctx_ref[n * part : (n + 1) * part, :],
            tile_rows(tiles_ref, n),
            (((0,), (0,)), ((), ())),
            preferred_element_type=F32,
        )
    residual_ref[...] = held
    shared = held.astype(BF)
    cent_rows = dot(onehot_ref[...], cent_ref[...])
    gate = jax.nn.sigmoid(jnp.sum(shared.astype(F32) * cent_rows, axis=1, keepdims=True))
    gate_ref[...] = gate
    sent = jnp.concatenate([shared, scalar_lanes(gate)], axis=1)
    moved_ref[...] = dot(route_ref[...], sent).astype(BF)


def forward_rows(ctx, tiles, tokens, cent, onehot, route):
    tok, width = tokens.shape
    return pl.pallas_call(
        forward_kernel,
        in_specs=[VMEM] * 6,
        out_specs=[VMEM] * 3,
        out_shape=[shape((tok, width), F32), shape((tok, 1), F32), shape((tok, width + LANES), BF)],
        cost_estimate=pl.CostEstimate(
            flops=3 * tok * width * width, bytes_accessed=2 * width * width + 8 * tok * width, transcendentals=0
        ),
        name="forward_rows",
    )(tiles, tokens, ctx, cent, onehot, route)


def enter_kernel(experts_ref, cot_ref, rows_ref, stream_ref, grad_ref, first_ref, second_ref):
    width = stream_ref.shape[1]
    half = first_ref.shape[0]
    stream = rows_ref[:, :width]
    lanes = rows_ref[:, width:]
    gate = jnp.sum(lanes.astype(F32), axis=1, keepdims=True)
    stream_ref[...] = stream
    unit_rows, unused = layer_stats(stream.astype(F32))
    normed = (unit_rows * experts_ref[0:1] + experts_ref[2:3]).astype(BF)
    first_ref[:, :width] = normed[:half]
    first_ref[:, width:] = lanes[:half]
    second_ref[:, :width] = normed[half:]
    second_ref[:, width:] = lanes[half:]
    grad_ref[...] = (cot_ref[...].astype(F32) * gate).astype(BF)


def enter_expert(rows, experts, cot):
    tok, width = cot.shape
    wide = (tok // 2, width + LANES)
    return pl.pallas_call(
        enter_kernel,
        in_specs=[VMEM] * 3,
        out_specs=[VMEM] * 4,
        out_shape=[shape((tok, width), BF)] * 2 + [shape(wide, BF)] * 2,
        cost_estimate=pl.CostEstimate(flops=20 * tok * width, bytes_accessed=10 * tok * width, transcendentals=0),
        name="enter_expert",
    )(experts, cot, rows)


def between_kernel(experts_ref, stream_ref, *refs):
    first_own, first_more, second_own, second_more, out_ref, first_ref, second_ref = refs
    half = first_ref.shape[0]
    for n, (own, more, low) in enumerate(
        ((first_own, first_more, first_ref), (second_own, second_more, second_ref))
    ):
        at = slice(n * half, (n + 1) * half)
        branch = own[...].astype(F32) + more[...].astype(F32)
        stream = stream_ref[at, :].astype(F32) + branch + experts_ref[4:5]
        out_ref[at, :] = stream
        unit_rows, unused = layer_stats(stream)
        low[...] = (unit_rows * experts_ref[1:2] + experts_ref[3:4]).astype(BF)


def between_experts(experts, stream, sums):
    tok, width = stream.shape
    return pl.pallas_call(
        between_kernel,
        in_specs=[VMEM] * 6,
        out_specs=[VMEM] * 3,
        out_shape=[shape((tok, width), F32)] + [shape((tok // 2, width), BF)] * 2,
        cost_estimate=pl.CostEstimate(flops=20 * tok * width, bytes_accessed=12 * tok * width, transcendentals=0),
        name="between_experts",
    )(experts, stream, *sums)


def norm_grads(half, sub, experts_ref, stream_ref, upper_ref, pairs, sums_ref):
    width = stream_ref.shape[1]
    grads = []
    for n, (own, more) in enumerate(pairs):
        at = slice(n * half, (n + 1) * half)
        grad_normed = own[:, :width].astype(F32) + more[:, :width].astype(F32)
        unit_rows, inv_root = layer_stats(stream_ref[at, :].astype(F32))
        upper = upper_ref[at, :].astype(F32)
        for row, values in enumerate((grad_normed * unit_rows, grad_normed, upper)):
            total = jnp.sum(values, axis=0, keepdims=True)
            if n == 0:
                sums_ref[row : row + 1, :] = total
            else:
                sums_ref[row : row + 1, :] += total
        grads.append(upper + norm_back(grad_normed, unit_rows, inv_root, experts_ref[sub : sub + 1]))
    return grads


def middle_back_kernel(experts_ref, stream_ref, upper_ref, *refs):
    first_own, first_more, second_own, second_more, out_ref, first_ref, second_ref, sums_ref = refs
    half = first_ref.shape[0]
    pairs = ((first_own, first_more), (second_own, second_more))
    grads = norm_grads(half, 1, experts_ref, stream_ref, upper_ref, pairs, sums_ref)
    for n, low in enumerate((first_ref, second_ref)):
        out_ref[n * half : (n + 1) * half, :] = grads[n]
        low[...] = grads[n].astype(BF)


def middle_back(experts, stream, upper, sums):
    tok, width = stream.shape
    return pl.pallas_call(
        middle_back_kernel,
        in_specs=[VMEM] * 7,
        out_specs=[VMEM] * 4,
        out_shape=[shape((tok, width), F32)] + [shape((tok // 2, width), BF)] * 2 + [shape((3, width), F32)],
        cost_estimate=pl.CostEstimate(flops=40 * tok * width, bytes_accessed=16 * tok * width, transcendentals=0),
        name="middle_back",
    )(experts, stream, upper, *sums)


def leave_back_kernel(experts_ref, stream_ref, upper_ref, cot_ref, later_ref, first_own, first_more, second_own, second_more, out_ref, sums_ref):
    width = stream_ref.shape[1]
    half = first_own.shape[0]
    pairs = ((first_own, first_more), (second_own, second_more))
    grads = norm_grads(half, 0, experts_ref, stream_ref, upper_ref, pairs, sums_ref)
    for n, (own, more) in enumerate(pairs):
        at = slice(n * half, (n + 1) * half)
        lanes = own[:, width:].astype(F32) + more[:, width:].astype(F32)
        kept = cot_ref[at, :].astype(F32) * (later_ref[at, :] + experts_ref[5:6])
        logit = jnp.sum(lanes, axis=1, keepdims=True) + jnp.sum(kept, axis=1, keepdims=True)
        out_ref[at, :width] = grads[n].astype(BF)
        out_ref[at, width:] = scalar_lanes(logit)


def leave_back(experts, stream, upper, cot, later, sums):
    tok, width = stream.shape
    return pl.pallas_call(
        leave_back_kernel,
        in_specs=[VMEM] * 9,
        out_specs=[VMEM] * 2,
        out_shape=[shape((tok, width + LANES), BF), shape((3, width), F32)],
        cost_estimate=pl.CostEstimate(flops=40 * tok * width, bytes_accessed=20 * tok * width, transcendentals=0),
        name="leave_back",
    )(experts, stream, upper, cot, later, *sums)


def backward_kernel(tiles_ref, unroute_ref, back_ref, cot_ref, cent_ref, onehot_ref, turned_ref, gate_ref, residual_ref, out_ref, low_ref, cent_out, ctx_ref):
    width = cot_ref.shape[1]
    rows_n, unused, part, unused = tiles_ref.shape
    back = dot(unroute_ref[...], back_ref[...])
    gate = gate_ref[...]
    grad_logit = jnp.sum(back[:, width:], axis=1, keepdims=True) * gate * (1.0 - gate)
    cent_rows = dot(onehot_ref[...], cent_ref[...])
    grad = cot_ref[...].astype(F32) + (back[:, :width] + grad_logit * cent_rows)
    out_ref[...] = grad
    low = grad.astype(BF)
    low_ref[...] = low
    for n in range(rows_n):
        ctx_ref[n * part : (n + 1) * part, :] = dot(tile_rows(tiles_ref, n), low, NT).astype(BF)
    cent_out[...] = lax.dot_general(
        turned_ref[...].astype(F32),
        grad_logit * residual_ref[...].astype(BF).astype(F32),
        NN,
        precision=lax.Precision.HIGHEST,
        preferred_element_type=F32,
    )


def backward_rows(back, tiles, unroute, cot, cent, onehot, gate, residual):
    tok, width = cot.shape
    return pl.pallas_call(
        backward_kernel,
        in_specs=[VMEM] * 9,
        out_specs=[VMEM] * 4,
        out_shape=[
            shape((tok, width), F32),
            shape((tok, width), BF),
            shape((LANES, width), F32),
            shape((width, tok), BF),
        ],
        cost_estimate=pl.CostEstimate(
            flops=3 * tok * width * width, bytes_accessed=2 * width * width + 12 * tok * width, transcendentals=0
        ),
        name="backward_rows",
    )(tiles, unroute, back, cot, cent, onehot, onehot.T, gate, residual)


def finish_kernel(stream_ref, branch_ref, experts_ref, out_ref):
    out_ref[...] = (stream_ref[...] + branch_ref[...].astype(F32) + experts_ref[5:6]).astype(BF)


def finish_rows(stream, branch, experts):
    return pl.pallas_call(
        finish_kernel,
        in_specs=[VMEM] * 3,
        out_specs=VMEM,
        out_shape=shape(stream.shape, BF),
        name="finish_rows",
    )(stream, branch, experts)


def project_kernel(scale, sources, rows, lead, gain_ref, shift_ref, w_ref, *refs):
    count = len(sources)
    total = sum(sources)
    blocks, refs = refs[:total], refs[total:]
    outs, refs = refs[:6], refs[6:]
    if lead:
        packets_ref, gain_out, shift_out, refs = *refs[:3], refs[3:]
    x_all, held, sems, out_sems = refs[0], refs[1:7], refs[7], refs[8]
    fw = w_ref.shape[1] // 3
    copies = begin([(b, x_all.at[n]) for n, b in enumerate(blocks)], sems)
    starts = [sum(sources[:n]) for n in range(count)]

    def merged(n, at):
        return sum(x_all[starts[n] + i, at, :].astype(F32) for i in range(sources[n]))

    if lead:
        finish(copies)
        packets = [merged(n, slice(rows, rows + 16)) for n in lead]
        for n, value in enumerate(packets):
            packets_ref[n] = value.astype(BF)
        value = sum(packets)
        gain, shift = value[0:1], value[1:2]
        gain_out[...] = gain
        shift_out[...] = shift
    else:
        gain, shift = gain_ref[...], shift_ref[...]
    leaving = []
    for n in range(count):
        if not lead:
            finish(copies[starts[n] : starts[n] + sources[n]])
        unit_rows, unused = layer_stats(merged(n, slice(0, rows)))
        normed = (unit_rows * gain + shift).astype(BF)
        held[0][n] = normed
        out = dot(normed, w_ref[...])
        keys = out[:, fw : 2 * fw]
        values = out[:, 2 * fw :]
        held[1][n] = (out[:, :fw].astype(BF).astype(F32) * scale).astype(BF)
        held[2][n] = keys.astype(BF)
        held[3][n] = values.astype(BF)
        held[4][n] = keys.T.astype(BF)
        held[5][n] = values.T.astype(BF)
        leaving += begin(
            [(h.at[n], o.at[n]) for h, o in zip(held, outs)], out_sems.at[pl.ds(6 * n, 6)]
        )
    finish(leaving)


def project(blocks, gain, shift, w, rows, scale, lead=()):
    sources = [len(b) for b in blocks]
    flat = [v for b in blocks for v in b]
    count = len(blocks)
    width = flat[0].shape[1]
    fw = w.shape[1] // 3
    kinds = [(count, rows, width)] + [(count, rows, fw)] * 3 + [(count, fw, rows)] * 2
    more = [shape((len(lead), 16, width), BF)] + [shape((1, width), F32)] * 2 if lead else []
    return pl.pallas_call(
        functools.partial(project_kernel, scale, sources, rows, lead),
        in_specs=[VMEM] * 3 + [ANY] * len(flat),
        out_specs=[ANY] * 6 + [VMEM] * len(more),
        out_shape=[shape(k, BF) for k in kinds] + more,
        scratch_shapes=[pltpu.VMEM((len(flat),) + flat[0].shape, BF)]
        + [pltpu.VMEM(k, BF) for k in kinds]
        + [pltpu.SemaphoreType.DMA((len(flat),)), pltpu.SemaphoreType.DMA((6 * count,))],
        cost_estimate=pl.CostEstimate(
            flops=count * (2 * rows * width * fw * 3 + 10 * rows * width),
            bytes_accessed=2 * count * (2 * rows * width + 5 * rows * fw) + 6 * width * fw,
            transcendentals=0,
        ),
        name="project",
    )(gain, shift, w, *flat)


def views(refs):
    return [ref.at[n] for ref in refs for n in range(ref.shape[0])]


def split_lanes(rows, count):
    width = rows.shape[1] // count
    if count == 1:
        return rows
    head_of = lax.broadcasted_iota(jnp.int32, rows.shape, 1) // width
    return jnp.concatenate(
        [jnp.where(head_of == h, rows, jnp.zeros_like(rows)) for h in range(count)], axis=0
    )


def split_rows(cols, count):
    width = cols.shape[0] // count
    if count == 1:
        return cols
    head_of = lax.broadcasted_iota(jnp.int32, cols.shape, 0) // width
    return jnp.concatenate(
        [jnp.where(head_of == h, cols, jnp.zeros_like(cols)) for h in range(count)], axis=1
    )


QB = 2
KB = 2


QB = 2
KB = 2


QB = 2
KB = 2


def attend_kernel(heads, total, groups, qb, kb, lead, order_ref, group_ref, ids_ref, *refs):
    q_in, k_in, vt_in = [views(refs[n * groups : (n + 1) * groups]) for n in range(3)]
    ctx_ref, low_ref, lse_ref, ends_ref, q_all, k_all, vt_all, low_all, count_ref, sems, out_sems = refs[
        3 * groups :
    ]
    rows = low_all.shape[2]
    fw = q_all.shape[2]
    head = fw // heads
    span = qb * rows
    key_rows = kb * rows
    pairs = []
    for n in range(total):
        at = order_ref[n]
        q_at = pl.ds(pl.multiple_of(lax.rem(at, qb) * rows, rows), rows)
        k_at = pl.ds(pl.multiple_of(lax.rem(at, kb) * rows, rows), rows)
        pairs += [
            (q_in[n], q_all.at[lax.div(at, qb), q_at, :]),
            (k_in[n], k_all.at[lax.div(at, kb), k_at, :]),
            (vt_in[n], vt_all.at[lax.div(at, kb), :, k_at]),
        ]
    copies = begin(pairs, sems)

    per = total // ids_ref.shape[0]
    ids = []
    for n in range(total):
        group = ids_ref[group_ref[n]].astype(F32)
        ids.append(group[lead + n % per : lead + n % per + 1, :rows])
    ids = jnp.concatenate(ids, axis=0)
    ends = jnp.zeros((total, rows), F32)
    for n in range(total):
        members = jnp.sum(jnp.where(ids == n, 1.0, 0.0))
        ends = ends + jnp.where(ids >= n, members, 0.0)
    for i in range(total // qb):
        ends_ref[i] = jnp.concatenate([ends[i * qb + b : i * qb + b + 1] for b in range(qb)], axis=1)
        last = jnp.max(ends[i * qb + qb - 1 : i * qb + qb]).astype(jnp.int32)
        count_ref[i] = lax.div(last + (key_rows - 1), key_rows)
    finish(copies)
    spots = lax.broadcasted_iota(jnp.int32, (key_rows, heads * span), 0).astype(F32)

    def block(i, unused):
        queries = split_lanes(q_all[i], heads)
        ends = jnp.concatenate([ends_ref[i]] * heads, axis=1)

        def step(j, state):
            run_max, run_sum, held = state
            scores = dot(k_all[j], queries, NT)
            scores = jnp.where(spots < ends - (j * key_rows).astype(F32), scores, NEG)
            new_max = jnp.maximum(run_max, jnp.max(scores, axis=0, keepdims=True))
            weights = jnp.exp(scores - new_max)
            factor = jnp.exp(run_max - new_max)
            new_sum = run_sum * factor + jnp.sum(weights, axis=0, keepdims=True)
            low = weights.astype(BF)
            values = vt_all[j]
            new_held = tuple(
                held[h] * factor[:, h * span : (h + 1) * span]
                + dot(values[h * head : (h + 1) * head], low[:, h * span : (h + 1) * span])
                for h in range(heads)
            )
            return new_max, new_sum, new_held

        start = (
            jnp.full((1, heads * span), NEG, F32),
            jnp.zeros((1, heads * span), F32),
            tuple(jnp.zeros((head, span), F32) for h in range(heads)),
        )
        run_max, run_sum, held = lax.fori_loop(0, count_ref[i], step, start)
        for h in range(heads):
            result = held[h] / run_sum[:, h * span : (h + 1) * span]
            ctx_ref[i, h * head : (h + 1) * head, :] = result
            for b in range(qb):
                low_all[i * qb + b, h * head : (h + 1) * head, :] = result[
                    :, b * rows : (b + 1) * rows
                ].astype(BF)
        lse_ref[i] = run_max + jnp.log(run_sum)
        return unused

    lax.fori_loop(0, total // qb, block, 0)
    finish(begin([(low_all, low_ref)], out_sems))


def attend(q, k, vt, ids, lead, group, order, heads):
    total = len(order)
    groups = len(q)
    rows, fw = q[0].shape[1:]
    qb, kb = QB, KB
    pairs = total * rows * total * rows * heads
    return pl.pallas_call(
        functools.partial(attend_kernel, heads, total, groups, qb, kb, lead),
        in_specs=[SMEM] * 2 + [VMEM] + [ANY] * (3 * groups),
        out_specs=[VMEM, ANY, VMEM, VMEM],
        out_shape=[
            shape((total // qb, fw, qb * rows), F32),
            shape((total, fw, rows), BF),
            shape((total // qb, 1, heads * qb * rows), F32),
            shape((total // qb, 1, qb * rows), F32),
        ],
        scratch_shapes=[
            pltpu.VMEM((total // qb, qb * rows, fw), BF),
            pltpu.VMEM((total // kb, kb * rows, fw), BF),
            pltpu.VMEM((total // kb, fw, kb * rows), BF),
            pltpu.VMEM((total, fw, rows), BF),
            pltpu.SMEM((total // qb,), jnp.int32),
            pltpu.SemaphoreType.DMA((3 * total,)),
            pltpu.SemaphoreType.DMA((1,)),
        ],
        cost_estimate=pl.CostEstimate(
            flops=2 * pairs * 128, bytes_accessed=10 * total * rows * fw, transcendentals=pairs // 2
        ),
        name="attend",
    )(order, group, ids, *q, *k, *vt)


def attend_back_kernel(heads, scale, total, groups, qb, kb, order_ref, ends_ref, ctx_ref, lse_ref, w_ref, gain_ref, shift_ref, cent_ref, *refs):
    q_in, k_in, v_in, kt_in, normed_in = [views(refs[n * groups : (n + 1) * groups]) for n in range(5)]
    refs = refs[5 * groups :]
    grad_in, refs = refs[0], refs[1:]
    out_refs, refs = refs[:total], refs[total:]
    dq_ref, dk_ref, dv_ref = refs[:3]
    q_raw, k_all, v_all, kt_all, g_raw, q_all, grad_all, delta_all, dq_all, out_all, normed_all, small_all, first_ref = refs[3:16]
    sems, normed_sems, out_sems, small_sems = refs[16:]
    unused, rows, width = out_all.shape
    normed_copies = begin([(normed_in[n], normed_all.at[n]) for n in range(total)], normed_sems)
    fw = q_raw.shape[2]
    head = fw // heads
    span = qb * rows
    pairs = []
    for n in range(total):
        at = order_ref[n]
        q_at = pl.ds(pl.multiple_of(lax.rem(at, qb) * rows, rows), rows)
        k_at = pl.ds(pl.multiple_of(lax.rem(at, kb) * rows, rows), rows)
        pairs += [
            (q_in[n], q_raw.at[lax.div(at, qb), q_at, :]),
            (k_in[n], k_all.at[lax.div(at, kb), k_at, :]),
            (v_in[n], v_all.at[lax.div(at, kb), k_at, :]),
            (kt_in[n], kt_all.at[lax.div(at, kb), :, k_at]),
            (grad_in.at[n], g_raw.at[n // qb, :, pl.ds((n % qb) * rows, rows)]),
        ]
    copies = begin(pairs, sems)
    lasts = [jnp.max(ends_ref[i]).astype(jnp.int32) for i in range(total // qb)]
    for j in range(total // kb):
        first_ref[j] = sum((last <= j * kb * rows).astype(jnp.int32) for last in lasts)
    finish(copies)

    def prepare(i, unused):
        q_all[i] = split_lanes(q_raw[i], heads)
        grad = g_raw[i]
        grad_all[i] = split_rows(grad, heads)
        product = grad.astype(F32) * ctx_ref[i]
        delta_all[i] = jnp.concatenate(
            [
                jnp.sum(product[h * head : (h + 1) * head], axis=0, keepdims=True)
                for h in range(heads)
            ],
            axis=1,
        )
        dq_all[i] = jnp.zeros((fw, span), F32)
        return unused

    lax.fori_loop(0, total // qb, prepare, 0)

    spots = lax.broadcasted_iota(jnp.int32, (kb * rows, span), 0).astype(F32)

    def key_block(j, unused):
        keys = k_all[j]
        values = v_all[j]
        keys_t = kt_all[j]

        def step(i, state):
            dk, dv = state
            ends = ends_ref[i] - (j * (kb * rows)).astype(F32)
            for h in range(heads):
                at = slice(h * span, (h + 1) * span)
                queries = q_all[i, at, :]
                grads = grad_all[i, :, at]
                scores = dot(keys, queries, NT) - lse_ref[i, :, at]
                probs = jnp.exp(jnp.where(spots < ends, scores, NEG))
                grad_probs = dot(values, grads) - delta_all[i, :, at]
                grad_scores = (probs * grad_probs).astype(BF)
                dv = dv + dot(probs.astype(BF), grads, NT)
                dk = dk + dot(grad_scores, queries)
                dq_all[i, h * head : (h + 1) * head, :] += dot(
                    keys_t[h * head : (h + 1) * head], grad_scores
                )
            return dk, dv

        zero = jnp.zeros((kb * rows, fw), F32)
        dk, dv = lax.fori_loop(first_ref[j], total // qb, step, (zero, zero))
        dk_ref[pl.ds(j * kb, kb)] = dk.astype(BF).reshape(kb, rows, fw)
        dv_ref[pl.ds(j * kb, kb)] = dv.astype(BF).reshape(kb, rows, fw)
        return unused

    lax.fori_loop(0, total // kb, key_block, 0)

    def turn(i, unused):
        dq_ref[pl.ds(i * qb, qb)] = (dq_all[i] * scale).T.astype(BF).reshape(qb, rows, fw)
        return unused

    lax.fori_loop(0, total // qb, turn, 0)

    leaving = []
    lifted = jnp.zeros((1, width), F32)
    shifted = jnp.zeros((1, width), F32)
    for n in range(total):
        at = order_ref[n]
        grad = dot(jnp.concatenate([dq_ref[at], dk_ref[at], dv_ref[at]], axis=1), w_ref[...], NT)
        out_all[n] = grad.astype(BF)
        leaving += begin(
            [(out_all.at[n], out_refs[n].at[pl.ds(0, rows), :])], out_sems.at[pl.ds(n, 1)]
        )
        normed_copies[n].wait()
        shifted = shifted + jnp.sum(grad, axis=0, keepdims=True)
        lifted = lifted + jnp.sum(grad * normed_all[n].astype(F32), axis=0, keepdims=True)
    lifted = (lifted - shift_ref[...] * shifted) / gain_ref[...]
    for n in range(total):
        rest = jnp.zeros((small_all.shape[1] - 3, width), F32)
        cent = cent_ref[pl.ds(order_ref[n], 1), :]
        small_all[n] = jnp.concatenate([lifted, shifted, cent, rest], axis=0).astype(BF)
    finish(
        leaving
        + begin(
            [(small_all.at[n], out_refs[n].at[pl.ds(rows, small_all.shape[1]), :]) for n in range(total)],
            small_sems,
        )
    )


def attend_back(q, k, v, kt, normed, grads, ctx, lse, w, gain, shift, cent, ends, order, heads, scale):
    total = len(order)
    groups = len(q)
    rows, fw = q[0].shape[1:]
    width = w.shape[0]
    qb, kb = QB, KB
    pairs = total * rows * total * rows * heads
    out = pl.pallas_call(
        functools.partial(attend_back_kernel, heads, scale, total, groups, qb, kb),
        in_specs=[SMEM] + [VMEM] * 7 + [ANY] * (5 * groups + 1),
        out_specs=[ANY] * total + [VMEM] * 3,
        out_shape=[shape((rows + 16, width), BF)] * total + [shape((total, rows, fw), BF)] * 3,
        scratch_shapes=[
            pltpu.VMEM((total // qb, qb * rows, fw), BF),
            pltpu.VMEM((total // kb, kb * rows, fw), BF),
            pltpu.VMEM((total // kb, kb * rows, fw), BF),
            pltpu.VMEM((total // kb, fw, kb * rows), BF),
            pltpu.VMEM((total // qb, fw, qb * rows), BF),
            pltpu.VMEM((total // qb, heads * qb * rows, fw), BF),
            pltpu.VMEM((total // qb, fw, heads * qb * rows), BF),
            pltpu.VMEM((total // qb, 1, heads * qb * rows), F32),
            pltpu.VMEM((total // qb, fw, qb * rows), F32),
            pltpu.VMEM((total, rows, width), BF),
            pltpu.VMEM((total, rows, width), BF),
            pltpu.VMEM((total, 16, width), BF),
            pltpu.SMEM((total // kb,), jnp.int32),
            pltpu.SemaphoreType.DMA((5 * total,)),
            pltpu.SemaphoreType.DMA((total,)),
            pltpu.SemaphoreType.DMA((total,)),
            pltpu.SemaphoreType.DMA((total,)),
        ],
        cost_estimate=pl.CostEstimate(
            flops=5 * pairs * 128, bytes_accessed=20 * total * rows * fw, transcendentals=pairs // 2
        ),
        name="attend_back",
    )(order, ends, ctx, lse, w, gain, shift, cent, *q, *k, *v, *kt, *normed, grads)
    return out[:total], out[total], out[total + 1], out[total + 2]


def project_grads_kernel(total, groups, parts, order_ref, dq_ref, dk_ref, dv_ref, *refs):
    normed_in, (out_ref, normed_all, sems) = views(refs[:groups]), refs[groups:]
    rows = dq_ref.shape[1]
    copies = begin(
        [
            (normed_in[n], normed_all.at[pl.ds(pl.multiple_of(order_ref[n] * rows, rows), rows)])
            for n in range(total)
        ],
        sems,
    )
    grads = jnp.concatenate(
        [ref[...].reshape(total * rows, ref.shape[2]) for ref in (dq_ref, dk_ref, dv_ref)], axis=1
    )
    finish(copies)
    step = out_ref.shape[0] // parts
    for n in range(parts):
        out_ref[n * step : (n + 1) * step, :] = lax.dot_general(
            normed_all[:, n * step : (n + 1) * step],
            grads,
            (((0,), (0,)), ((), ())),
            preferred_element_type=F32,
        ).astype(BF)


def project_grads(dq, dk, dv, normed, order, parts):
    total, rows, fw = dq.shape
    width = normed[0].shape[2]
    return pl.pallas_call(
        functools.partial(project_grads_kernel, total, len(normed), parts),
        in_specs=[SMEM] + [VMEM] * 3 + [ANY] * len(normed),
        out_specs=VMEM,
        out_shape=shape((width, 3 * fw), BF),
        scratch_shapes=[pltpu.VMEM((total * rows, width), BF), pltpu.SemaphoreType.DMA((total,))],
        cost_estimate=pl.CostEstimate(
            flops=2 * total * rows * width * 3 * fw,
            bytes_accessed=2 * total * rows * (width + 3 * fw) + 2 * width * 3 * fw,
            transcendentals=0,
        ),
        name="project_grads",
    )(order, dq, dk, dv, *normed)


def output_grads_kernel(ctx_ref, grad_ref, out_ref):
    cols_n, rows_n, part, fw = out_ref.shape
    for n in range(rows_n):
        result = dot(ctx_ref[n * part : (n + 1) * part, :], grad_ref[...]).astype(BF)
        for col in range(cols_n):
            out_ref[col, n] = result[:, col * fw : (col + 1) * fw]


def output_grads(ctx, grad, rows_n, cols_n):
    tok, width = grad.shape
    return pl.pallas_call(
        output_grads_kernel,
        in_specs=[VMEM] * 2,
        out_specs=VMEM,
        out_shape=shape((cols_n, rows_n, width // rows_n, width // cols_n), BF),
        cost_estimate=pl.CostEstimate(
            flops=2 * tok * width * width, bytes_accessed=2 * width * width, transcendentals=0
        ),
        name="output_grads",
    )(ctx, grad)


CHUNK = 512


def gelu_pair(pre_act):
    below = 0.5 * (1.0 + lax.erf(pre_act * 0.7071067811865476))
    bell = jnp.exp(-0.5 * pre_act * pre_act) * 0.3989422804014327
    return pre_act * below, below + pre_act * bell


def weight_copies(sub, w_in, w_back, first, second, sems):
    count, unused, chunk = first.shape

    def copy(n, which):
        at = pl.ds(pl.multiple_of(n * chunk, chunk), chunk)
        if which == 0:
            return pltpu.make_async_copy(w_in.at[0, sub, :, at], first.at[n], sems.at[2 * n])
        return pltpu.make_async_copy(w_back.at[0, sub, at, :], second.at[n], sems.at[2 * n + 1])

    for n in range(count):
        copy(n, 0).start()
        copy(n, 1).start()
    return copy


def add_to(total, n, more):
    @pl.when(n == 0)
    def begin_sum():
        total[...] = more

    @pl.when(n > 0)
    def add_sum():
        total[...] += more


def piece_pairs(pieces, held, first_lane=0):
    rows = held.shape[0] // len(pieces)
    lanes = pl.ds(first_lane, held.shape[1])
    return [(piece.at[:, lanes], held.at[pl.ds(m * rows, rows), :]) for m, piece in enumerate(pieces)]


def back_pairs(pieces, held):
    rows = held.shape[0] // len(pieces)
    return [(held.at[pl.ds(m * rows, rows), :], piece) for m, piece in enumerate(pieces)]


def spread_pairs(me_ref, whole, held, count):
    rows = held.shape[0] // count
    size = count // 2
    pairs = []
    for m in range(count):
        at = ((me_ref[0] ^ (m % size)) * 2 + m // size) * rows
        pairs.append((whole.at[pl.ds(pl.multiple_of(at, rows), rows), :], held.at[pl.ds(m * rows, rows), :]))
    return pairs


def expert_first_kernel(sub, count, bias_ref, w_in, w_back, *refs):
    pieces, refs = refs[:count], refs[count:]
    outs, refs = refs[:count], refs[count:]
    all_ref, hidden_ref, slope_ref = refs[:3]
    held, first, second, hidden, slope, total, low, sem_w, sem_x, sem_o, sem_r = refs[3:]
    chunks, unused, chunk = first.shape
    weights = weight_copies(sub, w_in, w_back, first, second, sem_w)
    finish(begin(piece_pairs(pieces, held), sem_x))
    leaving = begin([(held, all_ref)], sem_r.at[pl.ds(0, 1)])
    kept = [(hidden, hidden_ref), (slope, slope_ref)]

    def step(n, unused):
        weights(n, 0).wait()
        value, rise = gelu_pair(dot(held[...], first[n]) + bias_ref[n].astype(F32))
        hidden[n] = value.astype(BF)
        slope[n] = rise
        begin([(h.at[n], o.at[n]) for h, o in kept], sem_r.at[pl.ds(2 * n + 1, 2)])
        weights(n, 1).wait()
        add_to(total, n, dot(hidden[n], second[n]))
        return unused

    lax.fori_loop(0, chunks, step, 0)
    low[...] = total[...].astype(BF)
    leaving += begin(back_pairs(outs, low), sem_o)
    finish(leaving)
    for n in range(chunks):
        finish(copies_of([(h.at[n], o.at[n]) for h, o in kept], sem_r.at[pl.ds(2 * n + 1, 2)]))


def expert_first(pieces, sub, w_in, w_back, bias):
    count = len(pieces)
    rows, width = pieces[0].shape[0] * count, w_in.shape[2]
    ff = w_in.shape[3]
    chunk = min(CHUNK, ff)
    chunks = ff // chunk
    out = pl.pallas_call(
        functools.partial(expert_first_kernel, sub, count),
        in_specs=[VMEM, ANY, ANY] + [ANY] * count,
        out_specs=[ANY] * (count + 3),
        out_shape=[shape((rows // count, width), BF)] * count
        + [
            shape((rows, width), BF),
            shape((chunks, rows, chunk), BF),
            shape((chunks, rows, chunk), F32),
        ],
        scratch_shapes=[
            pltpu.VMEM((rows, width), BF),
            pltpu.VMEM((chunks, width, chunk), BF),
            pltpu.VMEM((chunks, chunk, width), BF),
            pltpu.VMEM((chunks, rows, chunk), BF),
            pltpu.VMEM((chunks, rows, chunk), F32),
            pltpu.VMEM((rows, width), F32),
            pltpu.VMEM((rows, width), BF),
            pltpu.SemaphoreType.DMA((2 * chunks,)),
            pltpu.SemaphoreType.DMA((count,)),
            pltpu.SemaphoreType.DMA((count,)),
            pltpu.SemaphoreType.DMA((2 * chunks + 1,)),
        ],
        cost_estimate=pl.CostEstimate(
            flops=4 * rows * width * ff, bytes_accessed=8 * rows * width, transcendentals=2 * rows * ff
        ),
        name="expert_first",
    )(bias.reshape(chunks, 1, chunk), w_in, w_back, *pieces)
    return out[:count], out[count], out[count + 1], out[count + 2]


def expert_second_kernel(sub, count, me_ref, bias_ref, w_in, w_back, *refs):
    cot_in, refs = refs[: count // 2], refs[count // 2 :]
    pieces, refs = refs[:count], refs[count:]
    gates, refs = refs[:count], refs[count:]
    grad_outs, refs = refs[:count], refs[count:]
    out_ref, all_ref, grad_all_ref, hidden_ref, pre_ref, bias_out, logit_ref = refs[:7]
    held, cot, gate, held_grad, first, second, hidden, grad_pre, total, low, low_grad = refs[7:18]
    sem_w, sem_x, sem_c, sem_g, sem_o, sem_p, sem_r = refs[18:]
    chunks, unused, chunk = first.shape
    weights = weight_copies(sub, w_in, w_back, first, second, sem_w)
    arriving = begin(piece_pairs(pieces, held), sem_x)
    width = held.shape[1]
    size, rows = count // 2, cot.shape[0] // count
    early = begin(
        [
            (cot_in[m % size].at[pl.ds(m // size * rows, rows), :], cot.at[pl.ds(m * rows, rows), :])
            for m in range(count)
        ],
        sem_c,
    )
    early += begin(piece_pairs(gates, gate, width), sem_g)
    finish(early)
    held_grad[...] = (
        cot[...].astype(F32) * jnp.sum(gate[...].astype(F32), axis=1, keepdims=True)
    ).astype(BF)
    finish(arriving)
    leaving = begin([(held, all_ref), (held_grad, grad_all_ref)], sem_r.at[pl.ds(0, 2)])
    kept = [(hidden, hidden_ref), (grad_pre, pre_ref)]

    def step(n, unused):
        weights(n, 0).wait()
        pre_act = dot(held[...], first[n]) + bias_ref[n].astype(F32)
        weights(n, 1).wait()
        grad_hidden = dot(held_grad[...], second[n], NT)
        value, rise = gelu_pair(pre_act)
        hidden[n] = value.astype(BF)
        back = (grad_hidden * rise).astype(BF)
        grad_pre[n] = back
        bias_out[n] = jnp.sum(back.astype(F32), axis=0, keepdims=True)
        begin([(h.at[n], o.at[n]) for h, o in kept], sem_r.at[pl.ds(2 * n + 2, 2)])
        add_to(total, n, dot(grad_pre[n], first[n], NT))
        return unused

    lax.fori_loop(0, chunks, step, 0)
    low_grad[...] = total[...].astype(BF)
    leaving += begin(back_pairs(grad_outs, low_grad), sem_p)

    def forward(n, unused):
        add_to(total, n, dot(hidden[n], second[n]))
        return unused

    lax.fori_loop(0, chunks, forward, 0)
    low[...] = total[...].astype(BF)
    logit_ref[...] = scalar_lanes(
        jnp.sum(cot[...].astype(F32) * total[...], axis=1, keepdims=True)
    )
    outs = [(h, w) for w, h in spread_pairs(me_ref, out_ref, low, count)]
    finish(leaving + begin(outs, sem_o))
    for n in range(chunks):
        finish(copies_of([(h.at[n], o.at[n]) for h, o in kept], sem_r.at[pl.ds(2 * n + 2, 2)]))


def expert_second(pieces, gates, cot, sub, w_in, w_back, bias, me):
    count = len(pieces)
    rows, width = pieces[0].shape
    rows = rows * count
    ff = w_in.shape[3]
    chunk = min(CHUNK, ff)
    chunks = ff // chunk
    out = pl.pallas_call(
        functools.partial(expert_second_kernel, sub, count),
        in_specs=[SMEM, VMEM] + [ANY] * (2 + 2 * count + count // 2),
        out_specs=[ANY] * (count + 5) + [VMEM] * 2,
        out_shape=[shape((rows // count, width), BF)] * count
        + [shape((rows, width), BF)] * 3
        + [shape((chunks, rows, chunk), BF)] * 2
        + [shape((chunks, 1, chunk), F32), shape((rows, LANES), BF)],
        scratch_shapes=[
            pltpu.VMEM((rows, width), BF),
            pltpu.VMEM((rows, width), BF),
            pltpu.VMEM((rows, LANES), BF),
            pltpu.VMEM((rows, width), BF),
            pltpu.VMEM((chunks, width, chunk), BF),
            pltpu.VMEM((chunks, chunk, width), BF),
            pltpu.VMEM((chunks, rows, chunk), BF),
            pltpu.VMEM((chunks, rows, chunk), BF),
            pltpu.VMEM((rows, width), F32),
            pltpu.VMEM((rows, width), BF),
            pltpu.VMEM((rows, width), BF),
            pltpu.SemaphoreType.DMA((2 * chunks,)),
            pltpu.SemaphoreType.DMA((count,)),
            pltpu.SemaphoreType.DMA((count,)),
            pltpu.SemaphoreType.DMA((count,)),
            pltpu.SemaphoreType.DMA((count,)),
            pltpu.SemaphoreType.DMA((count,)),
            pltpu.SemaphoreType.DMA((2 * chunks + 2,)),
        ],
        cost_estimate=pl.CostEstimate(
            flops=8 * rows * width * ff, bytes_accessed=12 * rows * width, transcendentals=2 * rows * ff
        ),
        name="expert_second",
    )(me, bias.reshape(chunks, 1, chunk), w_in, w_back, *cot, *pieces, *gates)
    return out[:count], *out[count:]


def expert_back_kernel(sub, count, logit_ref, w_in, w_back, slope_in, *refs):
    grads, refs = refs[:count], refs[count:]
    grad_outs, refs = refs[:count], refs[count:]
    grad_all_ref, pre_ref, bias_out = refs[:3]
    held_grad, first, second, slope, grad_pre, total, low_grad = refs[3:10]
    sem_w, sem_s, sem_g, sem_p, sem_r = refs[10:]
    chunks, unused, chunk = first.shape
    weights = weight_copies(sub, w_in, w_back, first, second, sem_w)
    arriving_grad = begin(piece_pairs(grads, held_grad), sem_g)
    begin([(slope_in.at[n], slope.at[n]) for n in range(chunks)], sem_s)
    low_grad[:, held_grad.shape[1] :] = logit_ref[...]
    finish(arriving_grad)
    leaving = begin([(held_grad, grad_all_ref)], sem_r.at[pl.ds(0, 1)])

    def step(n, unused):
        weights(n, 1).wait()
        grad_hidden = dot(held_grad[...], second[n], NT)
        pltpu.make_async_copy(slope_in.at[n], slope.at[n], sem_s.at[n]).wait()
        back = (grad_hidden * slope[n]).astype(BF)
        grad_pre[n] = back
        bias_out[n] = jnp.sum(back.astype(F32), axis=0, keepdims=True)
        begin([(grad_pre.at[n], pre_ref.at[n])], sem_r.at[pl.ds(n + 1, 1)])
        weights(n, 0).wait()
        add_to(total, n, dot(grad_pre[n], first[n], NT))
        return unused

    lax.fori_loop(0, chunks, step, 0)
    low_grad[:, : total.shape[1]] = total[...].astype(BF)
    finish(leaving + begin(back_pairs(grad_outs, low_grad), sem_p))
    for n in range(chunks):
        finish(copies_of([(grad_pre.at[n], pre_ref.at[n])], sem_r.at[pl.ds(n + 1, 1)]))


def expert_back(grads, slope, logit, sub, w_in, w_back):
    count = len(grads)
    rows, width = grads[0].shape
    rows = rows * count
    ff = w_in.shape[3]
    chunk = min(CHUNK, ff)
    chunks = ff // chunk
    out = pl.pallas_call(
        functools.partial(expert_back_kernel, sub, count),
        in_specs=[VMEM] + [ANY] * (3 + count),
        out_specs=[ANY] * (count + 2) + [VMEM],
        out_shape=[shape((rows // count, width + LANES), BF)] * count
        + [shape((rows, width), BF), shape((chunks, rows, chunk), BF), shape((chunks, 1, chunk), F32)],
        scratch_shapes=[
            pltpu.VMEM((rows, width), BF),
            pltpu.VMEM((chunks, width, chunk), BF),
            pltpu.VMEM((chunks, chunk, width), BF),
            pltpu.VMEM((chunks, rows, chunk), F32),
            pltpu.VMEM((chunks, rows, chunk), BF),
            pltpu.VMEM((rows, width), F32),
            pltpu.VMEM((rows, width + LANES), BF),
            pltpu.SemaphoreType.DMA((2 * chunks,)),
            pltpu.SemaphoreType.DMA((chunks,)),
            pltpu.SemaphoreType.DMA((count,)),
            pltpu.SemaphoreType.DMA((count,)),
            pltpu.SemaphoreType.DMA((chunks + 1,)),
        ],
        cost_estimate=pl.CostEstimate(
            flops=4 * rows * width * ff, bytes_accessed=10 * rows * width, transcendentals=0
        ),
        name="expert_back",
    )(logit, w_in, w_back, slope, *grads)
    return out[:count], *out[count:]


def weight_grads_kernel(chunked_left, left_ref, right_ref, *refs):
    out_ref = refs[-1]
    if chunked_left:
        left, right = left_ref[0], right_ref[...]
    else:
        left, right = left_ref[...], right_ref[0]
    out_ref[0, 0] = lax.dot_general(left, right, (((0,), (0,)), ((), ())), preferred_element_type=F32)


def weight_grads(left, right, sub, held, chunked_left):
    chunked, plain = (left, right) if chunked_left else (right, left)
    chunks, rows, chunk = chunked.shape
    width = plain.shape[1]
    pieces = pl.BlockSpec((1, rows, chunk), lambda n: (n, 0, 0))
    whole = pl.BlockSpec((rows, width), lambda n: (0, 0))
    if chunked_left:
        in_specs = [pieces, whole]
        out_spec = pl.BlockSpec((1, 1, chunk, width), lambda n: (0, sub, n, 0))
        dims = (1, 2, chunks * chunk, width)
    else:
        in_specs = [whole, pieces]
        out_spec = pl.BlockSpec((1, 1, width, chunk), lambda n: (0, sub, 0, n))
        dims = (1, 2, width, chunks * chunk)
    more = [] if held is None else [held]
    return pl.pallas_call(
        functools.partial(weight_grads_kernel, chunked_left),
        grid=(chunks,),
        in_specs=in_specs + [ANY] * len(more),
        out_specs=out_spec,
        out_shape=shape(dims, F32),
        input_output_aliases={2: 0} if more else {},
        cost_estimate=pl.CostEstimate(
            flops=2 * rows * width * chunks * chunk,
            bytes_accessed=4 * width * chunks * chunk + 2 * rows * (width + chunks * chunk),
            transcendentals=0,
        ),
        name="weight_grads",
    )(left, right, *more)


def stack_gather(value, axis, size):
    for bit in bits_of(size):
        value = jnp.concatenate([value, send_xor(value, axis, size, 1 << bit)])
    return value


def stack_scatter(value, axis, size):
    for bit in bits_of(size)[::-1]:
        half = value.shape[0] // 2
        value = value[:half] + send_xor(value[half:], axis, size, 1 << bit)
    return value


def together(*values):
    return lax.optimization_barrier(values)


def after(value, *earlier):
    return lax.optimization_barrier((value, *earlier))[0]


def gather_pieces(first, second, axis, size):
    bits = bits_of(size)
    return gather_path(first, axis, size, bits) + gather_path(second, axis, size, bits[::-1])


def scatter_pieces(pieces, axis, size):
    bits = bits_of(size)
    return scatter_path(pieces[:size], axis, size, bits) + scatter_path(
        pieces[size:], axis, size, bits[::-1]
    )


def shards(
    tokens,
    block_ids,
    expert_ids,
    cotangent,
    norm_gain,
    norm_shift,
    w_query,
    w_key,
    w_value,
    w_output,
    centroids,
    expert_gain,
    expert_shift,
    w_in,
    b_in,
    w_back,
    b_back,
):
    rows_n = lax.axis_size("row")
    cols_n = lax.axis_size("col")
    r = lax.axis_index("row")
    c = lax.axis_index("col")
    me = jnp.stack([r, c]).astype(jnp.int32)
    tok, width = tokens.shape
    fw = width // cols_n
    heads = HEADS // cols_n
    scale = float(width // HEADS) ** (-0.5)
    part = width // rows_n
    own = norm_gain.shape[0]
    slot = tok // cols_n

    count = 2 * own + part
    w_cat = jnp.concatenate([w_query, w_key, w_value], axis=1)
    order = jnp.stack(col_order(c, cols_n)).astype(jnp.int32)

    def gather_tiles(value):
        return lax.all_gather(value, ("row", "col"), axis=0, tiled=True).reshape(
            rows_n, cols_n, part, fw
        )

    def matrix_sums(part_qkv, part_output):
        parts = jnp.concatenate([part_qkv, part_output], axis=1).reshape(rows_n, part, 4 * fw)
        parts = reorder(parts, r, rows_n)
        return direct_exchange([parts[m] for m in range(rows_n)], "row", rows_n)

    def exchange(rows):
        return lax.all_to_all(
            rows.reshape(cols_n, -1, rows.shape[-1]), "col", split_axis=0, concat_axis=0, tiled=True
        ).reshape(rows.shape)

    onehot = expert_ids[:, None] == jnp.arange(LANES, dtype=jnp.int32)[None, :]
    onehot_low = onehot.astype(BF)
    below = (jnp.arange(tok)[:, None] > jnp.arange(tok)[None, :]).astype(BF)
    before = dot(below, onehot_low)
    rank = jnp.sum(jnp.where(onehot, before, 0.0), axis=1).astype(jnp.int32)
    place = expert_ids * slot + rank
    route = (jnp.arange(tok, dtype=jnp.int32)[:, None] == place[None, :]).astype(BF)
    unroute = (place[:, None] == jnp.arange(tok, dtype=jnp.int32)[None, :]).astype(BF)
    moved_cot = dot(route, cotangent).astype(BF)
    small_experts = jnp.concatenate([expert_gain[0], expert_shift[0], b_back[0]])

    if cols_n == 8:
        chips = cols_n // 2
        z, core = c // 2, c % 2
        lane = jnp.arange(width, dtype=jnp.int32)
        mine = lane // own == r * cols_n + c
        cent_row = jnp.where(lane // part == r, jnp.tile(centroids[0], rows_n), 0)
        ids_row = jnp.pad(block_ids[0].astype(BF), (0, width - tok))
        packet = jnp.stack(
            [
                jnp.where(mine, jnp.tile(norm_gain, width // own), 0),
                jnp.where(mine, jnp.tile(norm_shift, width // own), 0),
                jnp.where(core == 0, cent_row, 0),
                jnp.where(core == 1, cent_row, 0),
                jnp.where(core == 0, ids_row, 0),
                jnp.where(core == 1, ids_row, 0),
                jnp.zeros_like(ids_row),
                jnp.zeros_like(ids_row),
            ]
        )
        packet = packet + swap_core(packet, cols_n)
        top = direct_gather(packet[:4], "row", rows_n)
        block = jnp.concatenate(
            [tokens, sum(top[1:], top[0]), packet[4:], jnp.zeros((8, width), BF)]
        )
        move_right = lambda v, s: lax.ppermute(v, "col", right_pairs(s - 1, chips - 2, cols_n))
        move_left = lambda v, s: lax.ppermute(v, "col", left_pairs(1, chips - s, cols_n))
        swap = lambda v: swap_core(v, cols_n)
        right_1, left_1 = move_right(block, 1), move_left(block, 1)
        w_pieces = direct_gather(after(w_cat, block), "row", rows_n)
        small_experts = direct_gather(after(small_experts, block), "row", rows_n)
        cot_own = exchange(moved_cot)
        right_1, left_1, cot_own, *rest = together(
            right_1, left_1, cot_own, *w_pieces, *small_experts
        )
        w_pieces, small_experts = rest[:rows_n], rest[rows_n:]
        right_2, left_2 = move_right(right_1, 2), move_left(left_1, 2)
        swapped, right_1s, left_1s = swap(block), swap(right_1), swap(left_1)
        w_cat = arrange_rows(w_pieces, part, me)
        right_2, left_2, swapped, right_1s, left_1s, w_cat = together(
            right_2, left_2, swapped, right_1s, left_1s, w_cat
        )
        right_3, left_3 = move_right(right_2, 3), move_left(left_2, 3)
        right_2s, left_2s = swap(right_2), swap(left_2)
        cot_pieces = direct_gather(after(cot_own, right_1), "row", rows_n)
        right_3, left_3, right_2s, left_2s, *cot_pieces = together(
            right_3, left_3, right_2s, left_2s, *cot_pieces
        )
        right_3s, left_3s = swap(right_3), swap(left_3)
        tiles = gather_tiles(after(w_output, right_3))
        nothing = jnp.zeros((1, width), F32)
        *early, packets, gain_attn, shift_attn = project(
            [
                (block,),
                (swapped,),
                (left_1, right_3),
                (left_2, right_2),
                (left_2s, right_2s),
                (left_3, right_1),
            ],
            nothing, nothing, w_cat, tok, scale, (0, 2, 3, 5),
        )
        late = project(
            [(left_1s, right_3s), (left_3s, right_1s)], gain_attn, shift_attn, w_cat, tok, scale
        )
        places = (0, 1, 2, 4, 5, 6, 3, 7)
        order = order[jnp.array(places)]
        projected = list(zip(early, late))
        ids, lead = packets, 4
        group = (jnp.arange(cols_n, dtype=jnp.int32) // 2 - z) % chips
        cents = packets[:, 2:4]
        turned = (jnp.arange(chips) - z) % chips
        centroids_of = lambda held: jnp.take(held, turned, axis=0).reshape(cols_n, width)
    else:
        w_pieces = direct_gather(w_cat, "row", rows_n)
        small_experts = direct_gather(small_experts, "row", rows_n)
        cot_own = exchange(moved_cot)
        cot_pieces = direct_gather(cot_own, "row", rows_n)
        w_cat = arrange_rows(w_pieces, part, me)
        gain_attn, shift_attn = [
            lax.all_gather(v, ("row", "col"), axis=0, tiled=True).reshape(1, width).astype(F32)
            for v in (norm_gain, norm_shift)
        ]
        cents = lax.all_gather(
            lax.all_gather(centroids, "row", axis=1, tiled=True), "col", axis=0, tiled=True
        )
        centroids_of = lambda held: held
        tiles = gather_tiles(w_output)
        blocks = [(v,) for v in col_gather(tokens, cols_n)]
        projected = [(p,) for p in project(blocks, gain_attn, shift_attn, w_cat, tok, scale)]
        ids = lax.all_gather(block_ids[0].astype(BF), "col", axis=0, tiled=True)
        ids, lead = ids.reshape(cols_n, 1, tok).astype(F32), 0
        group = jnp.arange(cols_n, dtype=jnp.int32)
    normed, q, k, v, kt, vt = projected

    ctx, ctx_low, lse, ends = attend(q, k, vt, ids, lead, group, order, heads)
    small_experts, cents, ctx_low = together(jnp.stack(small_experts), cents, ctx_low)
    ctx_low = exchange(ctx_low.reshape(width, tok))
    experts = reorder(small_experts, r, rows_n).transpose(1, 0, 2).reshape(6, width).astype(F32)
    full_centroids = jnp.pad(centroids_of(cents), ((0, LANES - cols_n), (0, 0)))
    residual, gate, moved = forward_rows(ctx_low, tiles, tokens, full_centroids, onehot_low, route)

    stream_0, grad_2, half_1, half_2 = enter_expert(exchange(moved), experts, cot_own)
    wide_pieces = gather_pieces(half_1, half_2, "row", rows_n)
    partial, normed_all_0, hidden_0, slope_0 = expert_first(wide_pieces, 0, w_in, w_back, b_in[0, 0])
    stream_1, half_1, half_2 = between_experts(
        experts, stream_0, scatter_pieces(partial, "row", rows_n)
    )
    pieces = gather_pieces(half_1, half_2, "row", rows_n)
    partial, branch, normed_all_1, grad_all_1, hidden_1, grad_pre_1, bias_1, logit = expert_second(
        pieces, wide_pieces, cot_pieces, 1, w_in, w_back, b_in[0, 1], me
    )
    sums = scatter_pieces(partial, "row", rows_n)
    w_in_grad = weight_grads(normed_all_1, grad_pre_1, 1, None, False)
    w_in_grad, *sums = together(w_in_grad, *sums)
    grad_1, half_1, half_2, sums_1 = middle_back(experts, stream_1, grad_2, sums)
    pieces = gather_pieces(half_1, half_2, "row", rows_n)
    w_back_grad = weight_grads(hidden_1, after(grad_all_1, grad_1), 1, None, True)
    w_back_grad, *pieces = together(w_back_grad, *pieces)
    partial, grad_all_0, grad_pre_0, bias_0 = expert_back(pieces, slope_0, logit, 0, w_in, w_back)
    sums = together(*scatter_pieces(partial, "row", rows_n))
    branch = lax.psum_scatter(after(branch, sums[0]), "row", scatter_dimension=0, tiled=True)
    leaving, sums_0 = leave_back(experts, stream_0, grad_1, cot_own, stream_1, sums)
    returned = exchange(leaving)
    w_in_grad = weight_grads(normed_all_0, after(grad_pre_0, sums_0), 0, w_in_grad, False)
    w_in_grad, returned = together(w_in_grad, returned)
    grad_residual, grad_attended, part_cent, grad_ctx = backward_rows(
        returned, tiles, unroute, cotangent, full_centroids, onehot_low, gate, residual
    )

    grad_ctx = exchange(grad_ctx)
    part_output = output_grads(ctx_low, grad_attended, rows_n, cols_n)
    w_back_grad = weight_grads(hidden_0, after(grad_all_0, grad_attended), 0, w_back_grad, True)
    expert_low = finish_rows(stream_1, branch, experts)
    part_output, w_back_grad, expert_low, grad_ctx = together(
        part_output, w_back_grad, expert_low, grad_ctx
    )
    expert_low = exchange(expert_low)
    part_output = lax.psum_scatter(
        part_output.reshape(cols_n * width, fw), "col", scatter_dimension=0, tiled=True
    )
    partial, dq, dk, dv = attend_back(
        q, k, v, kt, normed, grad_ctx.reshape(cols_n, fw, tok), ctx, lse, w_cat, gain_attn, shift_attn,
        part_cent, ends, order, heads, scale,
    )
    dq, expert_low, *partial = together(dq, expert_low, *partial)
    if cols_n == 8:
        partial = [partial[places.index(n)] for n in range(cols_n)]
        halves = [
            add_low(partial[2 * turn], swap(partial[2 * turn + 1])) for turn in range(chips)
        ]
        into_right = lambda v, s: lax.ppermute(
            v, "col", right_pairs(0, min(s - 1, chips - 2), cols_n)
        )
        into_left = lambda v, s: lax.ppermute(
            v, "col", left_pairs(max(chips - s, 1), chips - 1, cols_n)
        )
        from_left, from_right = into_right(halves[3], 1), into_left(halves[1], 1)
        part_qkv = project_grads(after(dq, halves[3]), dk, dv, normed, order, rows_n)
        from_left, from_right, part_qkv, part_output = together(
            from_left, from_right, part_qkv, part_output
        )
        from_left = into_right(add_low(from_left, halves[2]), 2)
        from_right = into_left(add_low(from_right, halves[2]), 2)
        output = (residual + gate * dot(unroute, expert_low)).astype(BF)
        grad_sums = matrix_sums(part_qkv, part_output)
        from_left, from_right, output, *grad_sums = together(from_left, from_right, output, *grad_sums)
        from_left = into_right(add_low(from_left, halves[1]), 3)
        from_right = into_left(add_low(from_right, halves[3]), 3)
        summed = halves[0].astype(F32) + from_left.astype(F32) + from_right.astype(F32)
    else:
        part_qkv = project_grads(dq, dk, dv, normed, order, rows_n)
        output = (residual + gate * dot(unroute, expert_low)).astype(BF)
        grad_sums = matrix_sums(part_qkv, part_output)
        summed = col_scatter(partial, cols_n)
    grad_matrices = sum(v.astype(F32) for v in grad_sums)
    grad_qkv, grad_output = grad_matrices[:, : 3 * fw], grad_matrices[:, 3 * fw :]
    grad_normed_attn = summed[:tok]

    norm_rows = summed[tok : tok + 2].reshape(2, rows_n, cols_n, own)
    norm_rows = lax.dynamic_index_in_dim(norm_rows, c, 2, keepdims=False).transpose(1, 0, 2)
    expert_rows = jnp.concatenate([sums_0, sums_1]).reshape(6, rows_n, part).transpose(1, 0, 2)
    packed = jnp.concatenate(
        [
            norm_rows.reshape(rows_n, 2 * own),
            summed[tok + 2].reshape(rows_n, part),
            expert_rows.reshape(rows_n, 6 * part),
        ],
        axis=1,
    )[:, None]
    packed = reorder(packed, r, rows_n)
    packed = sum(direct_exchange([packed[m] for m in range(rows_n)], "row", rows_n))[0]
    expert_sums = packed[count:].reshape(2, 3, part).transpose(1, 0, 2)

    inputs = tokens.astype(F32)
    unit_attn, inv_attn = layer_stats(inputs)
    tokens_grad = grad_residual + norm_back(grad_normed_attn, unit_attn, inv_attn, gain_attn)
    return (
        output,
        tokens_grad,
        packed[:own],
        packed[own : 2 * own],
        grad_qkv[:, :fw],
        grad_qkv[:, fw : 2 * fw],
        grad_qkv[:, 2 * fw :],
        grad_output,
        packed[None, 2 * own : count],
        expert_sums[None, 0],
        expert_sums[None, 1],
        w_in_grad,
        jnp.stack([bias_0.reshape(-1), bias_1.reshape(-1)])[None],
        w_back_grad,
        expert_sums[None, 2],
    )


def solution(mesh):
    placed = (
        P(("row", "col"), None),
        P("row", "col"),
        P(("row", "col")),
        P(("row", "col"), None),
        P(("row", "col")),
        P(("row", "col")),
        P("row", "col"),
        P("row", "col"),
        P("row", "col"),
        P("row", "col"),
        P("col", "row"),
        P("col", None, "row"),
        P("col", None, "row"),
        P("col", None, None, "row"),
        P("col", None, "row"),
        P("col", None, "row", None),
        P("col", None, "row"),
    )
    return jax.shard_map(
        shards,
        mesh=mesh,
        in_specs=placed,
        out_specs=(
            P(("row", "col"), None),
            P(("row", "col"), None),
            P(("row", "col")),
            P(("row", "col")),
            P("row", "col"),
            P("row", "col"),
            P("row", "col"),
            P("row", "col"),
            P("col", "row"),
            P("col", None, "row"),
            P("col", None, "row"),
            P("col", None, None, "row"),
            P("col", None, "row"),
            P("col", None, "row", None),
            P("col", None, "row"),
        ),
        check_vma=False,
    )
```

```python
import functools

import jax
import jax.numpy as jnp
from jax import lax
from jax.experimental import pallas as pl
from jax.experimental.pallas import tpu as pltpu
from jax.sharding import PartitionSpec as P

HEADS = 16
EPS = 1e-05
NEG = -1e30
BF = jnp.bfloat16
F32 = jnp.float32
NT = (((1,), (1,)), ((), ()))
NN = (((1,), (0,)), ((), ()))
LANES = 128


def dot(left, right, dims=NN):
    return lax.dot_general(left, right, dims, preferred_element_type=F32)


def add_low(left, right):
    return (left.astype(F32) + right.astype(F32)).astype(BF)


def send_xor(value, axis, size, mask):
    return lax.ppermute(value, axis, [(i, i ^ mask) for i in range(size)])


def bits_of(size):
    return list(range(size.bit_length() - 1))


def gather_path(values, axis, size, bits, done=()):
    if not done:
        values = [values]
    held = dict(zip([0] + [1 << bit for bit in done], values))
    for bit in bits:
        held.update({m | (1 << bit): send_xor(v, axis, size, 1 << bit) for m, v in list(held.items())})
    return [held[m] for m in sorted(held)]


def scatter_path(blocks, axis, size, bits):
    held = {m: [v] for m, v in enumerate(blocks)}
    for bit in bits:
        leaving = {m: v for m, v in held.items() if (m >> bit) & 1}
        held = {m: v for m, v in held.items() if not (m >> bit) & 1}
        for m, v in leaving.items():
            total = v[0] if len(v) == 1 else sum(n.astype(F32) for n in v).astype(BF)
            held[m & ~(1 << bit)].append(send_xor(total, axis, size, 1 << bit))
    return held[0]


def direct_gather(value, axis, size):
    return [value] + [send_xor(value, axis, size, m) for m in range(1, size)]


def direct_exchange(blocks, axis, size):
    return [blocks[0]] + [send_xor(blocks[m], axis, size, m) for m in range(1, size)]


def reorder(stacked, mine, size):
    return jnp.concatenate(
        [lax.dynamic_index_in_dim(stacked, mine ^ j, 0, keepdims=True) for j in range(size)]
    )


def swap_core(value, size):
    return send_xor(value, "col", size, 1)


def right_pairs(first, last, size):
    return [(i, i + 2) for i in range(size) if first <= i // 2 <= last]


def left_pairs(first, last, size):
    return [(i, i - 2) for i in range(size) if first <= i // 2 <= last]


def line_order(mine, size):
    chips = size // 2
    return [
        ((mine // 2 + turn) % chips) * 2 + ((mine % 2) ^ core)
        for turn in range(chips)
        for core in range(2)
    ]


def col_order(mine, size):
    return line_order(mine, size) if size == 8 else [mine ^ m for m in range(size)]


def col_gather(value, size):
    return gather_path(value, "col", size, bits_of(size))


def col_scatter(blocks, size):
    return sum(v.astype(F32) for v in scatter_path(blocks, "col", size, bits_of(size)))


def layer_stats(stream):
    center = stream - jnp.mean(stream, axis=-1, keepdims=True)
    inv_root = lax.rsqrt(jnp.mean(center * center, axis=-1, keepdims=True) + EPS)
    return (center * inv_root, inv_root)


def norm_back(grad_normed, unit_rows, inv_root, gain_full):
    grad_unit = grad_normed * gain_full
    mean_first = jnp.mean(grad_unit, axis=-1, keepdims=True)
    mean_second = jnp.mean(grad_unit * unit_rows, axis=-1, keepdims=True)
    return inv_root * (grad_unit - mean_first - unit_rows * mean_second)


ANY = pl.BlockSpec(memory_space=pl.ANY)
HBM = pl.BlockSpec(memory_space=pltpu.HBM)
VMEM = pl.BlockSpec(memory_space=pltpu.VMEM)
SMEM = pl.BlockSpec(memory_space=pltpu.SMEM)


def shape(dims, kind):
    return jax.ShapeDtypeStruct(dims, kind)


def params(mib):
    return pltpu.CompilerParams(vmem_limit_bytes=mib * 1024 * 1024)


def copies_of(pairs, sems):
    return [pltpu.make_async_copy(s, d, sems.at[n]) for n, (s, d) in enumerate(pairs)]


def begin(pairs, sems):
    copies = copies_of(pairs, sems)
    for copy in copies:
        copy.start()
    return copies


def finish(copies):
    for copy in copies:
        copy.wait()


def arrange_kernel(count, me_ref, *refs):
    outs, rest = refs[count:-1], refs[-1]
    rows = outs[0].shape[0] // count
    for m in range(count):
        owner = me_ref[0] ^ m
        at = pl.ds(pl.multiple_of(owner * rows, rows), rows)
        done = 0
        for out in outs:
            out[at, :] = refs[m][:rows, done : done + out.shape[1]]
            done += out.shape[1]
        rest[owner] = refs[m][rows:, :]


def arrange_rows(pieces, rows, widths, me):
    count = len(pieces)
    kind = pieces[0].dtype
    return pl.pallas_call(
        functools.partial(arrange_kernel, count),
        in_specs=[SMEM] + [VMEM] * count,
        out_specs=[VMEM] * (len(widths) + 1),
        out_shape=[shape((count * rows, w), kind) for w in widths]
        + [shape((count, pieces[0].shape[0] - rows, pieces[0].shape[1]), kind)],
        name="arrange_rows",
    )(me, *pieces)


def tile_rows(tiles_ref, block):
    return jnp.concatenate([tiles_ref[col, block] for col in range(tiles_ref.shape[0])], axis=1)


def scalar_lanes(values):
    high = values.astype(BF).astype(F32)
    lane = lax.broadcasted_iota(jnp.int32, (values.shape[0], LANES), 1)
    return jnp.where(lane == 0, high, jnp.where(lane == 1, values - high, 0.0)).astype(BF)


def forward_kernel(total, me_ref, tiles_ref, tokens_ref, cent_ref, onehot_ref, route_ref, *refs):
    pieces, refs = refs[:total], refs[total:]
    moved, (ctx_ref, residual_ref, gate_ref, sent) = refs[:total], refs[total:]
    unused, rows_n, part, unused = tiles_ref.shape
    place_pieces(pieces, me_ref, ctx_ref)
    held = tokens_ref[...].astype(F32)
    for n in range(rows_n):
        held = held + lax.dot_general(
            ctx_ref[n * part : (n + 1) * part, :],
            tile_rows(tiles_ref, n),
            (((0,), (0,)), ((), ())),
            preferred_element_type=F32,
        )
    residual_ref[...] = held
    shared = held.astype(BF)
    cent_rows = dot(onehot_ref[...], cent_ref[...])
    gate = jax.nn.sigmoid(jnp.sum(shared.astype(F32) * cent_rows, axis=1, keepdims=True))
    gate_ref[...] = gate
    leaving = jnp.concatenate([shared, scalar_lanes(gate)], axis=1)
    sent[...] = dot(route_ref[...], leaving).astype(BF)
    slot = moved[0].shape[0]
    for m in range(total):
        moved[m][...] = sent[pl.ds(pl.multiple_of((me_ref[1] ^ m) * slot, slot), slot), :]


def forward_rows(pieces, tiles, tokens, cent, onehot, route, me):
    total = len(pieces)
    tok, width = tokens.shape
    out = pl.pallas_call(
        functools.partial(forward_kernel, total),
        in_specs=[SMEM] + [VMEM] * (5 + total),
        out_specs=[VMEM] * (total + 3),
        out_shape=[shape((tok // total, width + LANES), BF)] * total
        + [shape((width, tok), BF), shape((tok, width), F32), shape((tok, 1), F32)],
        scratch_shapes=[pltpu.VMEM((tok, width + LANES), BF)],
        cost_estimate=pl.CostEstimate(
            flops=3 * tok * width * width, bytes_accessed=2 * width * width + 8 * tok * width, transcendentals=0
        ),
        name="forward_rows",
    )(me, tiles, tokens, cent, onehot, route, *pieces)
    return out[:total], *out[total:]


def enter_kernel(total, me_ref, experts_ref, cot_ref, *refs):
    pieces, (stream_ref, grad_ref, first_ref, second_ref, rows_ref) = refs[:total], refs[total:]
    width = stream_ref.shape[1]
    half = first_ref.shape[0]
    place_pieces(pieces, me_ref, rows_ref)
    stream = rows_ref[:, :width]
    lanes = rows_ref[:, width:]
    gate = jnp.sum(lanes.astype(F32), axis=1, keepdims=True)
    stream_ref[...] = stream
    unit_rows, unused = layer_stats(stream.astype(F32))
    normed = (unit_rows * experts_ref[0:1] + experts_ref[2:3]).astype(BF)
    first_ref[:, :width] = normed[:half]
    first_ref[:, width:] = lanes[:half]
    second_ref[:, :width] = normed[half:]
    second_ref[:, width:] = lanes[half:]
    grad_ref[...] = (cot_ref[...].astype(F32) * gate).astype(BF)


def enter_expert(pieces, experts, cot, me):
    total = len(pieces)
    tok, width = cot.shape
    wide = (tok // 2, width + LANES)
    return pl.pallas_call(
        functools.partial(enter_kernel, total),
        in_specs=[SMEM] + [VMEM] * (2 + total),
        out_specs=[VMEM] * 4,
        out_shape=[shape((tok, width), BF)] * 2 + [shape(wide, BF)] * 2,
        scratch_shapes=[pltpu.VMEM((tok, width + LANES), BF)],
        cost_estimate=pl.CostEstimate(flops=20 * tok * width, bytes_accessed=10 * tok * width, transcendentals=0),
        name="enter_expert",
    )(me, experts, cot, *pieces)


def add_up(refs, lanes):
    return sum(ref[:, lanes].astype(F32) for ref in refs)


def halves_of(refs):
    return refs[: len(refs) // 2], refs[len(refs) // 2 :]


def between_kernel(experts_ref, stream_ref, *refs):
    sums, (out_ref, first_ref, second_ref) = refs[:-3], refs[-3:]
    half = first_ref.shape[0]
    for n, (parts, low) in enumerate(zip(halves_of(sums), (first_ref, second_ref))):
        at = slice(n * half, (n + 1) * half)
        stream = stream_ref[at, :].astype(F32) + add_up(parts, slice(None)) + experts_ref[4:5]
        out_ref[at, :] = stream
        unit_rows, unused = layer_stats(stream)
        low[...] = (unit_rows * experts_ref[1:2] + experts_ref[3:4]).astype(BF)


def between_experts(experts, stream, sums):
    tok, width = stream.shape
    return pl.pallas_call(
        between_kernel,
        in_specs=[VMEM] * (2 + len(sums)),
        out_specs=[VMEM] * 3,
        out_shape=[shape((tok, width), F32)] + [shape((tok // 2, width), BF)] * 2,
        cost_estimate=pl.CostEstimate(flops=20 * tok * width, bytes_accessed=12 * tok * width, transcendentals=0),
        name="between_experts",
    )(experts, stream, *sums)


def norm_grads(half, sub, experts_ref, stream_ref, upper_ref, sums, sums_ref):
    width = stream_ref.shape[1]
    grads = []
    for n, parts in enumerate(halves_of(sums)):
        at = slice(n * half, (n + 1) * half)
        grad_normed = add_up(parts, slice(0, width))
        unit_rows, inv_root = layer_stats(stream_ref[at, :].astype(F32))
        upper = upper_ref[at, :].astype(F32)
        for row, values in enumerate((grad_normed * unit_rows, grad_normed, upper)):
            total = jnp.sum(values, axis=0, keepdims=True)
            if n == 0:
                sums_ref[row : row + 1, :] = total
            else:
                sums_ref[row : row + 1, :] += total
        grads.append(upper + norm_back(grad_normed, unit_rows, inv_root, experts_ref[sub : sub + 1]))
    return grads


def middle_back_kernel(experts_ref, stream_ref, upper_ref, *refs):
    sums, (out_ref, first_ref, second_ref, sums_ref) = refs[:-4], refs[-4:]
    half = first_ref.shape[0]
    grads = norm_grads(half, 1, experts_ref, stream_ref, upper_ref, sums, sums_ref)
    for n, low in enumerate((first_ref, second_ref)):
        out_ref[n * half : (n + 1) * half, :] = grads[n]
        low[...] = grads[n].astype(BF)


def middle_back(experts, stream, upper, sums):
    tok, width = stream.shape
    return pl.pallas_call(
        middle_back_kernel,
        in_specs=[VMEM] * (3 + len(sums)),
        out_specs=[VMEM] * 4,
        out_shape=[shape((tok, width), F32)] + [shape((tok // 2, width), BF)] * 2 + [shape((3, width), F32)],
        cost_estimate=pl.CostEstimate(flops=40 * tok * width, bytes_accessed=16 * tok * width, transcendentals=0),
        name="middle_back",
    )(experts, stream, upper, *sums)


def leave_back_kernel(total, me_ref, experts_ref, stream_ref, upper_ref, cot_ref, later_ref, *refs):
    sums, refs = refs[: -total - 2], refs[-total - 2 :]
    outs, sums_ref, held = refs[:total], refs[total], refs[total + 1]
    width = stream_ref.shape[1]
    slot = outs[0].shape[0]
    half = stream_ref.shape[0] // 2
    grads = norm_grads(half, 0, experts_ref, stream_ref, upper_ref, sums, sums_ref)
    for n, parts in enumerate(halves_of(sums)):
        at = slice(n * half, (n + 1) * half)
        kept = cot_ref[at, :].astype(F32) * (later_ref[at, :] + experts_ref[5:6])
        logit = jnp.sum(add_up(parts, slice(width, None)), axis=1, keepdims=True)
        logit = logit + jnp.sum(kept, axis=1, keepdims=True)
        held[at, :width] = grads[n].astype(BF)
        held[at, width:] = scalar_lanes(logit)
    for m in range(total):
        outs[m][...] = held[pl.ds(pl.multiple_of((me_ref[1] ^ m) * slot, slot), slot), :]


def leave_back(experts, stream, upper, cot, later, sums, me, total):
    tok, width = stream.shape
    return pl.pallas_call(
        functools.partial(leave_back_kernel, total),
        in_specs=[SMEM] + [VMEM] * (5 + len(sums)),
        out_specs=[VMEM] * (total + 1),
        out_shape=[shape((tok // total, width + LANES), BF)] * total + [shape((3, width), F32)],
        scratch_shapes=[pltpu.VMEM((tok, width + LANES), BF)],
        cost_estimate=pl.CostEstimate(flops=40 * tok * width, bytes_accessed=20 * tok * width, transcendentals=0),
        name="leave_back",
    )(me, experts, stream, upper, cot, later, *sums)


def place_pieces(pieces, me_ref, held):
    rows = pieces[0].shape[0]
    for m, piece in enumerate(pieces):
        held[pl.ds(pl.multiple_of((me_ref[1] ^ m) * rows, rows), rows), :] = piece[...]


def backward_kernel(total, me_ref, tiles_ref, unroute_ref, cot_ref, cent_ref, onehot_ref, turned_ref, gate_ref, residual_ref, *refs):
    pieces, (out_ref, low_ref, cent_out, ctx_ref, back_ref) = refs[:total], refs[total:]
    place_pieces(pieces, me_ref, back_ref)
    width = cot_ref.shape[1]
    unused, rows_n, part, unused = tiles_ref.shape
    back = dot(unroute_ref[...], back_ref[...])
    gate = gate_ref[...]
    grad_logit = jnp.sum(back[:, width:], axis=1, keepdims=True) * gate * (1.0 - gate)
    cent_rows = dot(onehot_ref[...], cent_ref[...])
    grad = cot_ref[...].astype(F32) + (back[:, :width] + grad_logit * cent_rows)
    out_ref[...] = grad
    low = grad.astype(BF)
    low_ref[...] = low
    for n in range(rows_n):
        ctx_ref[n * part : (n + 1) * part, :] = dot(tile_rows(tiles_ref, n), low, NT).astype(BF)
    cent_out[...] = lax.dot_general(
        turned_ref[...].astype(F32),
        grad_logit * residual_ref[...].astype(BF).astype(F32),
        NN,
        precision=lax.Precision.HIGHEST,
        preferred_element_type=F32,
    )


def backward_rows(pieces, tiles, unroute, cot, cent, onehot, gate, residual, me):
    tok, width = cot.shape
    total = len(pieces)
    return pl.pallas_call(
        functools.partial(backward_kernel, total),
        in_specs=[SMEM] + [VMEM] * (8 + total),
        out_specs=[VMEM] * 4,
        out_shape=[
            shape((tok, width), F32),
            shape((tok, width), BF),
            shape((LANES, width), F32),
            shape((width, tok), BF),
        ],
        scratch_shapes=[pltpu.VMEM((tok, width + LANES), BF)],
        cost_estimate=pl.CostEstimate(
            flops=3 * tok * width * width, bytes_accessed=2 * width * width + 12 * tok * width, transcendentals=0
        ),
        name="backward_rows",
    )(me, tiles, unroute, cot, cent, onehot, onehot.T, gate, residual, *pieces)


def finish_kernel(stream_ref, branch_ref, experts_ref, out_ref):
    out_ref[...] = (stream_ref[...] + branch_ref[...].astype(F32) + experts_ref[5:6]).astype(BF)


def finish_rows(stream, branch, experts):
    return pl.pallas_call(
        finish_kernel,
        in_specs=[VMEM] * 3,
        out_specs=VMEM,
        out_shape=shape(stream.shape, BF),
        name="finish_rows",
    )(stream, branch, experts)


def project_kernel(scale, count, gain_ref, shift_ref, w_ref, *refs):
    blocks, outs, refs = refs[:count], refs[count : count + 6], refs[count + 6 :]
    x_all, held, sems, out_sems = refs[0], refs[1:7], refs[7], refs[8]
    fw = w_ref.shape[1] // 3
    copies = begin([(b, x_all.at[n]) for n, b in enumerate(blocks)], sems)
    leaving = []
    for n in range(count):
        copies[n].wait()
        unit_rows, unused = layer_stats(x_all[n].astype(F32))
        normed = (unit_rows * gain_ref[...] + shift_ref[...]).astype(BF)
        held[0][n] = normed
        out = dot(normed, w_ref[...])
        keys = out[:, fw : 2 * fw]
        values = out[:, 2 * fw :]
        held[1][n] = (out[:, :fw].astype(BF).astype(F32) * scale).astype(BF)
        held[2][n] = keys.astype(BF)
        held[3][n] = values.astype(BF)
        held[4][n] = keys.T.astype(BF)
        held[5][n] = values.T.astype(BF)
        leaving += begin(
            [(h.at[n], o.at[n]) for h, o in zip(held, outs)], out_sems.at[pl.ds(6 * n, 6)]
        )
    finish(leaving)


def project(blocks, gain, shift, w, scale):
    count = len(blocks)
    rows, width = blocks[0].shape
    fw = w.shape[1] // 3
    kinds = [(count, rows, width)] + [(count, rows, fw)] * 3 + [(count, fw, rows)] * 2
    return pl.pallas_call(
        functools.partial(project_kernel, scale, count),
        in_specs=[VMEM] * 3 + [ANY] * count,
        out_specs=[ANY] * 6,
        out_shape=[shape(k, BF) for k in kinds],
        scratch_shapes=[pltpu.VMEM((count, rows, width), BF)]
        + [pltpu.VMEM(k, BF) for k in kinds]
        + [pltpu.SemaphoreType.DMA((count,)), pltpu.SemaphoreType.DMA((6 * count,))],
        cost_estimate=pl.CostEstimate(
            flops=count * (2 * rows * width * fw * 3 + 10 * rows * width),
            bytes_accessed=2 * count * (2 * rows * width + 5 * rows * fw) + 6 * width * fw,
            transcendentals=0,
        ),
        name="project",
    )(gain, shift, w, *blocks)


def views(refs):
    return [ref.at[n] for ref in refs for n in range(ref.shape[0])]


def split_lanes(rows, count):
    width = rows.shape[1] // count
    if count == 1:
        return rows
    head_of = lax.broadcasted_iota(jnp.int32, rows.shape, 1) // width
    return jnp.concatenate(
        [jnp.where(head_of == h, rows, jnp.zeros_like(rows)) for h in range(count)], axis=0
    )


def split_rows(cols, count):
    width = cols.shape[0] // count
    if count == 1:
        return cols
    head_of = lax.broadcasted_iota(jnp.int32, cols.shape, 0) // width
    return jnp.concatenate(
        [jnp.where(head_of == h, cols, jnp.zeros_like(cols)) for h in range(count)], axis=1
    )


QB = 2
KB = 2


QB = 2
KB = 2


QB = 2
KB = 2


def attend_kernel(heads, total, groups, qb, kb, me_ref, order_ref, ids_ref, *refs):
    q_in, k_in, vt_in = [views(refs[n * groups : (n + 1) * groups]) for n in range(3)]
    refs = refs[3 * groups :]
    low_refs, refs = refs[:total], refs[total:]
    ctx_ref, lse_ref, ends_ref, q_all, k_all, vt_all, low_all, count_ref, sems, out_sems = refs
    rows = low_all.shape[2]
    fw = q_all.shape[2]
    head = fw // heads
    span = qb * rows
    key_rows = kb * rows
    pairs = []
    for n in range(total):
        at = order_ref[n]
        q_at = pl.ds(pl.multiple_of(lax.rem(at, qb) * rows, rows), rows)
        k_at = pl.ds(pl.multiple_of(lax.rem(at, kb) * rows, rows), rows)
        pairs += [
            (q_in[n], q_all.at[lax.div(at, qb), q_at, :]),
            (k_in[n], k_all.at[lax.div(at, kb), k_at, :]),
            (vt_in[n], vt_all.at[lax.div(at, kb), :, k_at]),
        ]
    copies = begin(pairs, sems)

    ids = ids_ref[...]
    ends = jnp.zeros((total, rows), F32)
    for n in range(total):
        members = jnp.sum(jnp.where(ids == n, 1.0, 0.0))
        ends = ends + jnp.where(ids >= n, members, 0.0)
    for i in range(total // qb):
        ends_ref[i] = jnp.concatenate([ends[i * qb + b : i * qb + b + 1] for b in range(qb)], axis=1)
        last = jnp.max(ends[i * qb + qb - 1 : i * qb + qb]).astype(jnp.int32)
        count_ref[i] = lax.div(last + (key_rows - 1), key_rows)
    finish(copies)
    spots = lax.broadcasted_iota(jnp.int32, (key_rows, heads * span), 0).astype(F32)

    def block(i, unused):
        queries = split_lanes(q_all[i], heads)
        ends = jnp.concatenate([ends_ref[i]] * heads, axis=1)

        def step(j, state):
            run_max, run_sum, held = state
            scores = dot(k_all[j], queries, NT)
            scores = jnp.where(spots < ends - (j * key_rows).astype(F32), scores, NEG)
            new_max = jnp.maximum(run_max, jnp.max(scores, axis=0, keepdims=True))
            weights = jnp.exp(scores - new_max)
            factor = jnp.exp(run_max - new_max)
            new_sum = run_sum * factor + jnp.sum(weights, axis=0, keepdims=True)
            low = weights.astype(BF)
            values = vt_all[j]
            new_held = tuple(
                held[h] * factor[:, h * span : (h + 1) * span]
                + dot(values[h * head : (h + 1) * head], low[:, h * span : (h + 1) * span])
                for h in range(heads)
            )
            return new_max, new_sum, new_held

        start = (
            jnp.full((1, heads * span), NEG, F32),
            jnp.zeros((1, heads * span), F32),
            tuple(jnp.zeros((head, span), F32) for h in range(heads)),
        )
        run_max, run_sum, held = lax.fori_loop(0, count_ref[i], step, start)
        for h in range(heads):
            result = held[h] / run_sum[:, h * span : (h + 1) * span]
            ctx_ref[i, h * head : (h + 1) * head, :] = result
            for b in range(qb):
                low_all[i * qb + b, h * head : (h + 1) * head, :] = result[
                    :, b * rows : (b + 1) * rows
                ].astype(BF)
        lse_ref[i] = run_max + jnp.log(run_sum)
        return unused

    lax.fori_loop(0, total // qb, block, 0)
    finish(begin([(low_all.at[me_ref[1] ^ m], low_refs[m]) for m in range(total)], out_sems))


def attend(q, k, vt, ids, order, heads, me):
    total = len(order)
    groups = len(q)
    rows, fw = q[0].shape[1:]
    qb, kb = QB, KB
    pairs = total * rows * total * rows * heads
    out = pl.pallas_call(
        functools.partial(attend_kernel, heads, total, groups, qb, kb),
        in_specs=[SMEM] * 2 + [VMEM] + [ANY] * (3 * groups),
        out_specs=[ANY] * total + [VMEM] * 3,
        out_shape=[shape((fw, rows), BF)] * total
        + [
            shape((total // qb, fw, qb * rows), F32),
            shape((total // qb, 1, heads * qb * rows), F32),
            shape((total // qb, 1, qb * rows), F32),
        ],
        scratch_shapes=[
            pltpu.VMEM((total // qb, qb * rows, fw), BF),
            pltpu.VMEM((total // kb, kb * rows, fw), BF),
            pltpu.VMEM((total // kb, fw, kb * rows), BF),
            pltpu.VMEM((total, fw, rows), BF),
            pltpu.SMEM((total // qb,), jnp.int32),
            pltpu.SemaphoreType.DMA((3 * total,)),
            pltpu.SemaphoreType.DMA((total,)),
        ],
        cost_estimate=pl.CostEstimate(
            flops=2 * pairs * 128, bytes_accessed=10 * total * rows * fw, transcendentals=pairs // 2
        ),
        name="attend",
    )(me, order, ids, *q, *k, *vt)
    return out[:total], *out[total:]


def attend_back_kernel(heads, scale, total, groups, qb, kb, order_ref, out_order_ref, ends_ref, ctx_ref, lse_ref, w_ref, gain_ref, shift_ref, cent_ref, *refs):
    q_in, k_in, v_in, kt_in, normed_in = [views(refs[n * groups : (n + 1) * groups]) for n in range(5)]
    refs = refs[5 * groups :]
    grad_in, refs = refs[0], refs[1:]
    out_refs, refs = refs[:total], refs[total:]
    dq_ref, dk_ref, dv_ref = refs[:3]
    q_raw, k_all, v_all, kt_all, g_raw, q_all, grad_all, delta_all, dq_all, out_all, normed_all, small_all, first_ref = refs[3:16]
    sems, normed_sems, out_sems, small_sems = refs[16:]
    unused, rows, width = out_all.shape
    normed_copies = begin([(normed_in[n], normed_all.at[order_ref[n]]) for n in range(total)], normed_sems)
    fw = q_raw.shape[2]
    head = fw // heads
    span = qb * rows
    pairs = []
    for n in range(total):
        at = order_ref[n]
        q_at = pl.ds(pl.multiple_of(lax.rem(at, qb) * rows, rows), rows)
        k_at = pl.ds(pl.multiple_of(lax.rem(at, kb) * rows, rows), rows)
        pairs += [
            (q_in[n], q_raw.at[lax.div(at, qb), q_at, :]),
            (k_in[n], k_all.at[lax.div(at, kb), k_at, :]),
            (v_in[n], v_all.at[lax.div(at, kb), k_at, :]),
            (kt_in[n], kt_all.at[lax.div(at, kb), :, k_at]),
            (grad_in.at[n], g_raw.at[n // qb, :, pl.ds((n % qb) * rows, rows)]),
        ]
    copies = begin(pairs, sems)
    lasts = [jnp.max(ends_ref[i]).astype(jnp.int32) for i in range(total // qb)]
    for j in range(total // kb):
        first_ref[j] = sum((last <= j * kb * rows).astype(jnp.int32) for last in lasts)
    finish(copies)

    def prepare(i, unused):
        q_all[i] = split_lanes(q_raw[i], heads)
        grad = g_raw[i]
        grad_all[i] = split_rows(grad, heads)
        product = grad.astype(F32) * ctx_ref[i]
        delta_all[i] = jnp.concatenate(
            [
                jnp.sum(product[h * head : (h + 1) * head], axis=0, keepdims=True)
                for h in range(heads)
            ],
            axis=1,
        )
        dq_all[i] = jnp.zeros((fw, span), F32)
        return unused

    lax.fori_loop(0, total // qb, prepare, 0)

    spots = lax.broadcasted_iota(jnp.int32, (kb * rows, span), 0).astype(F32)

    def key_block(j, unused):
        keys = k_all[j]
        values = v_all[j]
        keys_t = kt_all[j]

        def step(i, state):
            dk, dv = state
            ends = ends_ref[i] - (j * (kb * rows)).astype(F32)
            for h in range(heads):
                at = slice(h * span, (h + 1) * span)
                queries = q_all[i, at, :]
                grads = grad_all[i, :, at]
                scores = dot(keys, queries, NT) - lse_ref[i, :, at]
                probs = jnp.exp(jnp.where(spots < ends, scores, NEG))
                grad_probs = dot(values, grads) - delta_all[i, :, at]
                grad_scores = (probs * grad_probs).astype(BF)
                dv = dv + dot(probs.astype(BF), grads, NT)
                dk = dk + dot(grad_scores, queries)
                dq_all[i, h * head : (h + 1) * head, :] += dot(
                    keys_t[h * head : (h + 1) * head], grad_scores
                )
            return dk, dv

        zero = jnp.zeros((kb * rows, fw), F32)
        dk, dv = lax.fori_loop(first_ref[j], total // qb, step, (zero, zero))
        dk_ref[pl.ds(j * kb, kb)] = dk.astype(BF).reshape(kb, rows, fw)
        dv_ref[pl.ds(j * kb, kb)] = dv.astype(BF).reshape(kb, rows, fw)
        return unused

    lax.fori_loop(0, total // kb, key_block, 0)

    def turn(i, unused):
        dq_ref[pl.ds(i * qb, qb)] = (dq_all[i] * scale).T.astype(BF).reshape(qb, rows, fw)
        return unused

    lax.fori_loop(0, total // qb, turn, 0)

    leaving = []
    lifted = jnp.zeros((1, width), F32)
    shifted = jnp.zeros((1, width), F32)
    finish(normed_copies)
    for n in range(total):
        at = out_order_ref[n]
        grad = dot(jnp.concatenate([dq_ref[at], dk_ref[at], dv_ref[at]], axis=1), w_ref[...], NT)
        out_all[n] = grad.astype(BF)
        leaving += begin(
            [(out_all.at[n], out_refs[n].at[pl.ds(0, rows), :])], out_sems.at[pl.ds(n, 1)]
        )
        shifted = shifted + jnp.sum(grad, axis=0, keepdims=True)
        lifted = lifted + jnp.sum(grad * normed_all[at].astype(F32), axis=0, keepdims=True)
    lifted = (lifted - shift_ref[...] * shifted) / gain_ref[...]
    for n in range(total):
        rest = jnp.zeros((small_all.shape[1] - 3, width), F32)
        cent = cent_ref[pl.ds(out_order_ref[n], 1), :]
        small_all[n] = jnp.concatenate([lifted, shifted, cent, rest], axis=0).astype(BF)
    finish(
        leaving
        + begin(
            [(small_all.at[n], out_refs[n].at[pl.ds(rows, small_all.shape[1]), :]) for n in range(total)],
            small_sems,
        )
    )


def attend_back(q, k, v, kt, normed, grads, ctx, lse, w, gain, shift, cent, ends, order, out_order, heads, scale):
    total = len(order)
    groups = len(q)
    rows, fw = q[0].shape[1:]
    width = w.shape[0]
    qb, kb = QB, KB
    pairs = total * rows * total * rows * heads
    out = pl.pallas_call(
        functools.partial(attend_back_kernel, heads, scale, total, groups, qb, kb),
        in_specs=[SMEM] * 2 + [VMEM] * 7 + [ANY] * (5 * groups + 1),
        out_specs=[ANY] * total + [VMEM] * 3,
        out_shape=[shape((rows + 16, width), BF)] * total + [shape((total, rows, fw), BF)] * 3,
        scratch_shapes=[
            pltpu.VMEM((total // qb, qb * rows, fw), BF),
            pltpu.VMEM((total // kb, kb * rows, fw), BF),
            pltpu.VMEM((total // kb, kb * rows, fw), BF),
            pltpu.VMEM((total // kb, fw, kb * rows), BF),
            pltpu.VMEM((total // qb, fw, qb * rows), BF),
            pltpu.VMEM((total // qb, heads * qb * rows, fw), BF),
            pltpu.VMEM((total // qb, fw, heads * qb * rows), BF),
            pltpu.VMEM((total // qb, 1, heads * qb * rows), F32),
            pltpu.VMEM((total // qb, fw, qb * rows), F32),
            pltpu.VMEM((total, rows, width), BF),
            pltpu.VMEM((total, rows, width), BF),
            pltpu.VMEM((total, 16, width), BF),
            pltpu.SMEM((total // kb,), jnp.int32),
            pltpu.SemaphoreType.DMA((5 * total,)),
            pltpu.SemaphoreType.DMA((total,)),
            pltpu.SemaphoreType.DMA((total,)),
            pltpu.SemaphoreType.DMA((total,)),
        ],
        cost_estimate=pl.CostEstimate(
            flops=5 * pairs * 128, bytes_accessed=20 * total * rows * fw, transcendentals=pairs // 2
        ),
        name="attend_back",
    )(order, out_order, ends, ctx, lse, w, gain, shift, cent, *q, *k, *v, *kt, *normed, grads)
    return out[:total], out[total], out[total + 1], out[total + 2]


def project_grads_kernel(total, groups, parts, order_ref, dq_ref, dk_ref, dv_ref, *refs):
    normed_in, (out_ref, normed_all, sems) = views(refs[:groups]), refs[groups:]
    rows = dq_ref.shape[1]
    copies = begin(
        [
            (normed_in[n], normed_all.at[pl.ds(pl.multiple_of(order_ref[n] * rows, rows), rows)])
            for n in range(total)
        ],
        sems,
    )
    grads = jnp.concatenate(
        [ref[...].reshape(total * rows, ref.shape[2]) for ref in (dq_ref, dk_ref, dv_ref)], axis=1
    )
    finish(copies)
    step = out_ref.shape[0] // parts
    for n in range(parts):
        out_ref[n * step : (n + 1) * step, :] = lax.dot_general(
            normed_all[:, n * step : (n + 1) * step],
            grads,
            (((0,), (0,)), ((), ())),
            preferred_element_type=F32,
        ).astype(BF)


def project_grads(dq, dk, dv, normed, order, parts):
    total, rows, fw = dq.shape
    width = normed[0].shape[2]
    return pl.pallas_call(
        functools.partial(project_grads_kernel, total, len(normed), parts),
        in_specs=[SMEM] + [VMEM] * 3 + [ANY] * len(normed),
        out_specs=VMEM,
        out_shape=shape((width, 3 * fw), BF),
        scratch_shapes=[pltpu.VMEM((total * rows, width), BF), pltpu.SemaphoreType.DMA((total,))],
        cost_estimate=pl.CostEstimate(
            flops=2 * total * rows * width * 3 * fw,
            bytes_accessed=2 * total * rows * (width + 3 * fw) + 2 * width * 3 * fw,
            transcendentals=0,
        ),
        name="project_grads",
    )(order, dq, dk, dv, *normed)


def output_grads_kernel(ctx_ref, grad_ref, out_ref):
    cols_n, rows_n, part, fw = out_ref.shape
    for n in range(rows_n):
        result = dot(ctx_ref[n * part : (n + 1) * part, :], grad_ref[...]).astype(BF)
        for col in range(cols_n):
            out_ref[col, n] = result[:, col * fw : (col + 1) * fw]


def output_grads(ctx, grad, rows_n, cols_n):
    tok, width = grad.shape
    return pl.pallas_call(
        output_grads_kernel,
        in_specs=[VMEM] * 2,
        out_specs=VMEM,
        out_shape=shape((cols_n, rows_n, width // rows_n, width // cols_n), BF),
        cost_estimate=pl.CostEstimate(
            flops=2 * tok * width * width, bytes_accessed=2 * width * width, transcendentals=0
        ),
        name="output_grads",
    )(ctx, grad)


CHUNK = 512


def gelu_pair(pre_act):
    below = 0.5 * (1.0 + lax.erf(pre_act * 0.7071067811865476))
    bell = jnp.exp(-0.5 * pre_act * pre_act) * 0.3989422804014327
    return pre_act * below, below + pre_act * bell


def weight_copies(sub, w_in, w_back, first, second, sems):
    count, unused, chunk = first.shape

    def copy(n, which):
        at = pl.ds(pl.multiple_of(n * chunk, chunk), chunk)
        if which == 0:
            return pltpu.make_async_copy(w_in.at[0, sub, :, at], first.at[n], sems.at[2 * n])
        return pltpu.make_async_copy(w_back.at[0, sub, at, :], second.at[n], sems.at[2 * n + 1])

    for n in range(count):
        copy(n, 0).start()
        copy(n, 1).start()
    return copy


def add_to(total, n, more):
    @pl.when(n == 0)
    def begin_sum():
        total[...] = more

    @pl.when(n > 0)
    def add_sum():
        total[...] += more


def piece_pairs(pieces, held, first_lane=0):
    rows = held.shape[0] // len(pieces)
    lanes = pl.ds(first_lane, held.shape[1])
    return [(piece.at[:, lanes], held.at[pl.ds(m * rows, rows), :]) for m, piece in enumerate(pieces)]


def back_pairs(pieces, held):
    rows = held.shape[0] // len(pieces)
    return [(held.at[pl.ds(m * rows, rows), :], piece) for m, piece in enumerate(pieces)]


def spread_pairs(me_ref, whole, held, count):
    rows = held.shape[0] // count
    size = count // 2
    pairs = []
    for m in range(count):
        at = ((me_ref[0] ^ (m % size)) * 2 + m // size) * rows
        pairs.append((whole.at[pl.ds(pl.multiple_of(at, rows), rows), :], held.at[pl.ds(m * rows, rows), :]))
    return pairs


def expert_first_kernel(sub, count, bias_ref, w_in, w_back, *refs):
    pieces, refs = refs[:count], refs[count:]
    outs, refs = refs[:count], refs[count:]
    all_ref, hidden_ref, slope_ref = refs[:3]
    held, first, second, hidden, slope, total, low, sem_w, sem_x, sem_o, sem_r = refs[3:]
    chunks, unused, chunk = first.shape
    arriving = begin(piece_pairs(pieces, held), sem_x)
    weights = weight_copies(sub, w_in, w_back, first, second, sem_w)
    finish(arriving)
    leaving = begin([(held, all_ref)], sem_r.at[pl.ds(0, 1)])
    kept = [(hidden, hidden_ref), (slope, slope_ref)]

    def step(n, unused):
        weights(n, 0).wait()
        value, rise = gelu_pair(dot(held[...], first[n]) + bias_ref[n].astype(F32))
        hidden[n] = value.astype(BF)
        slope[n] = rise
        begin([(h.at[n], o.at[n]) for h, o in kept], sem_r.at[pl.ds(2 * n + 1, 2)])
        weights(n, 1).wait()
        add_to(total, n, dot(hidden[n], second[n]))
        return unused

    lax.fori_loop(0, chunks, step, 0)
    low[...] = total[...].astype(BF)
    leaving += begin(back_pairs(outs, low), sem_o)
    finish(leaving)
    for n in range(chunks):
        finish(copies_of([(h.at[n], o.at[n]) for h, o in kept], sem_r.at[pl.ds(2 * n + 1, 2)]))


def expert_first(pieces, sub, w_in, w_back, bias):
    count = len(pieces)
    rows, width = pieces[0].shape[0] * count, w_in.shape[2]
    ff = w_in.shape[3]
    chunk = min(CHUNK, ff)
    chunks = ff // chunk
    out = pl.pallas_call(
        functools.partial(expert_first_kernel, sub, count),
        in_specs=[VMEM, ANY, ANY] + [ANY] * count,
        out_specs=[ANY] * (count + 3),
        out_shape=[shape((rows // count, width), BF)] * count
        + [
            shape((rows, width), BF),
            shape((chunks, rows, chunk), BF),
            shape((chunks, rows, chunk), F32),
        ],
        scratch_shapes=[
            pltpu.VMEM((rows, width), BF),
            pltpu.VMEM((chunks, width, chunk), BF),
            pltpu.VMEM((chunks, chunk, width), BF),
            pltpu.VMEM((chunks, rows, chunk), BF),
            pltpu.VMEM((chunks, rows, chunk), F32),
            pltpu.VMEM((rows, width), F32),
            pltpu.VMEM((rows, width), BF),
            pltpu.SemaphoreType.DMA((2 * chunks,)),
            pltpu.SemaphoreType.DMA((count,)),
            pltpu.SemaphoreType.DMA((count,)),
            pltpu.SemaphoreType.DMA((2 * chunks + 1,)),
        ],
        cost_estimate=pl.CostEstimate(
            flops=4 * rows * width * ff, bytes_accessed=8 * rows * width, transcendentals=2 * rows * ff
        ),
        name="expert_first",
    )(bias.reshape(chunks, 1, chunk), w_in, w_back, *pieces)
    return out[:count], out[count], out[count + 1], out[count + 2]


def expert_second_kernel(sub, count, bias_ref, w_in, w_back, *refs):
    cot_in, refs = refs[:count], refs[count:]
    pieces, refs = refs[:count], refs[count:]
    gates, refs = refs[:count], refs[count:]
    grad_outs, refs = refs[:count], refs[count:]
    all_ref, grad_all_ref, hidden_ref, pre_ref, bias_out = refs[:5]
    held, cot, gate, held_grad, first, second, hidden, grad_pre, total, low_grad = refs[5:15]
    sem_w, sem_x, sem_c, sem_g, sem_p, sem_r = refs[15:]
    chunks, unused, chunk = first.shape
    weights = weight_copies(sub, w_in, w_back, first, second, sem_w)
    arriving = begin(piece_pairs(pieces, held), sem_x)
    width = held.shape[1]
    early = begin(piece_pairs(cot_in, cot), sem_c)
    early += begin(piece_pairs(gates, gate, width), sem_g)
    finish(early)
    held_grad[...] = (
        cot[...].astype(F32) * jnp.sum(gate[...].astype(F32), axis=1, keepdims=True)
    ).astype(BF)
    finish(arriving)
    leaving = begin([(held, all_ref), (held_grad, grad_all_ref)], sem_r.at[pl.ds(0, 2)])
    kept = [(hidden, hidden_ref), (grad_pre, pre_ref)]

    def step(n, unused):
        weights(n, 0).wait()
        pre_act = dot(held[...], first[n]) + bias_ref[n].astype(F32)
        weights(n, 1).wait()
        grad_hidden = dot(held_grad[...], second[n], NT)
        value, rise = gelu_pair(pre_act)
        hidden[n] = value.astype(BF)
        back = (grad_hidden * rise).astype(BF)
        grad_pre[n] = back
        bias_out[n] = jnp.sum(back.astype(F32), axis=0, keepdims=True)
        begin([(h.at[n], o.at[n]) for h, o in kept], sem_r.at[pl.ds(2 * n + 2, 2)])
        add_to(total, n, dot(grad_pre[n], first[n], NT))
        return unused

    lax.fori_loop(0, chunks, step, 0)
    low_grad[...] = total[...].astype(BF)
    leaving += begin(back_pairs(grad_outs, low_grad), sem_p)

    finish(leaving)
    for n in range(chunks):
        finish(copies_of([(h.at[n], o.at[n]) for h, o in kept], sem_r.at[pl.ds(2 * n + 2, 2)]))


def expert_branch_kernel(sub, count, me_ref, hidden_in, w_back, *refs):
    cot_in, (out_ref, logit_ref, hidden, second, cot, total, low, sem_h, sem_w, sem_c, sem_o) = (
        refs[:count],
        refs[count:],
    )
    chunks, unused, chunk = hidden.shape

    def copy(n, which):
        at = pl.ds(pl.multiple_of(n * chunk, chunk), chunk)
        if which == 0:
            return pltpu.make_async_copy(hidden_in.at[n], hidden.at[n], sem_h.at[n])
        return pltpu.make_async_copy(w_back.at[0, sub, at, :], second.at[n], sem_w.at[n])

    for n in range(chunks):
        copy(n, 0).start()
        copy(n, 1).start()
    early = begin(piece_pairs(cot_in, cot), sem_c)

    def step(n, unused):
        copy(n, 0).wait()
        copy(n, 1).wait()
        add_to(total, n, dot(hidden[n], second[n]))
        return unused

    lax.fori_loop(0, chunks, step, 0)
    low[...] = total[...].astype(BF)
    leaving = begin([(h, w) for w, h in spread_pairs(me_ref, out_ref, low, count)], sem_o)
    finish(early)
    logit_ref[...] = scalar_lanes(
        jnp.sum(cot[...].astype(F32) * total[...], axis=1, keepdims=True)
    )
    finish(leaving)


def expert_branch(hidden, cot, sub, w_back, me):
    count = len(cot)
    chunks, rows, chunk = hidden.shape
    width = cot[0].shape[1]
    return pl.pallas_call(
        functools.partial(expert_branch_kernel, sub, count),
        in_specs=[SMEM] + [ANY] * (2 + count),
        out_specs=[ANY, VMEM],
        out_shape=[shape((rows, width), BF), shape((rows, LANES), BF)],
        scratch_shapes=[
            pltpu.VMEM((chunks, rows, chunk), BF),
            pltpu.VMEM((chunks, chunk, width), BF),
            pltpu.VMEM((rows, width), BF),
            pltpu.VMEM((rows, width), F32),
            pltpu.VMEM((rows, width), BF),
            pltpu.SemaphoreType.DMA((chunks,)),
            pltpu.SemaphoreType.DMA((chunks,)),
            pltpu.SemaphoreType.DMA((count,)),
            pltpu.SemaphoreType.DMA((count,)),
        ],
        cost_estimate=pl.CostEstimate(
            flops=2 * rows * width * chunks * chunk, bytes_accessed=8 * rows * width, transcendentals=0
        ),
        name="expert_branch",
    )(me, hidden, w_back, *cot)


def expert_second(pieces, gates, cot, sub, w_in, w_back, bias):
    count = len(pieces)
    rows, width = pieces[0].shape
    rows = rows * count
    ff = w_in.shape[3]
    chunk = min(CHUNK, ff)
    chunks = ff // chunk
    out = pl.pallas_call(
        functools.partial(expert_second_kernel, sub, count),
        in_specs=[VMEM] + [ANY] * (2 + 3 * count),
        out_specs=[ANY] * (count + 4) + [VMEM],
        out_shape=[shape((rows // count, width), BF)] * count
        + [shape((rows, width), BF)] * 2
        + [shape((chunks, rows, chunk), BF)] * 2
        + [shape((chunks, 1, chunk), F32)],
        scratch_shapes=[
            pltpu.VMEM((rows, width), BF),
            pltpu.VMEM((rows, width), BF),
            pltpu.VMEM((rows, LANES), BF),
            pltpu.VMEM((rows, width), BF),
            pltpu.VMEM((chunks, width, chunk), BF),
            pltpu.VMEM((chunks, chunk, width), BF),
            pltpu.VMEM((chunks, rows, chunk), BF),
            pltpu.VMEM((chunks, rows, chunk), BF),
            pltpu.VMEM((rows, width), F32),
            pltpu.VMEM((rows, width), BF),
            pltpu.SemaphoreType.DMA((2 * chunks,)),
            pltpu.SemaphoreType.DMA((count,)),
            pltpu.SemaphoreType.DMA((count,)),
            pltpu.SemaphoreType.DMA((count,)),
            pltpu.SemaphoreType.DMA((count,)),
            pltpu.SemaphoreType.DMA((2 * chunks + 2,)),
        ],
        cost_estimate=pl.CostEstimate(
            flops=6 * rows * width * ff, bytes_accessed=12 * rows * width, transcendentals=2 * rows * ff
        ),
        name="expert_second",
    )(bias.reshape(chunks, 1, chunk), w_in, w_back, *cot, *pieces, *gates)
    return out[:count], *out[count:]


def expert_back_kernel(sub, count, logit_ref, w_in, w_back, slope_in, *refs):
    grads, refs = refs[:count], refs[count:]
    grad_outs, refs = refs[:count], refs[count:]
    grad_all_ref, pre_ref, bias_out = refs[:3]
    held_grad, first, second, slope, grad_pre, total, low_grad = refs[3:10]
    sem_w, sem_s, sem_g, sem_p, sem_r = refs[10:]
    chunks, unused, chunk = first.shape
    arriving_grad = begin(piece_pairs(grads, held_grad), sem_g)
    weights = weight_copies(sub, w_in, w_back, first, second, sem_w)
    begin([(slope_in.at[n], slope.at[n]) for n in range(chunks)], sem_s)
    low_grad[:, held_grad.shape[1] :] = logit_ref[...]
    finish(arriving_grad)
    leaving = begin([(held_grad, grad_all_ref)], sem_r.at[pl.ds(0, 1)])

    def step(n, unused):
        weights(n, 1).wait()
        grad_hidden = dot(held_grad[...], second[n], NT)
        pltpu.make_async_copy(slope_in.at[n], slope.at[n], sem_s.at[n]).wait()
        back = (grad_hidden * slope[n]).astype(BF)
        grad_pre[n] = back
        bias_out[n] = jnp.sum(back.astype(F32), axis=0, keepdims=True)
        begin([(grad_pre.at[n], pre_ref.at[n])], sem_r.at[pl.ds(n + 1, 1)])
        weights(n, 0).wait()
        add_to(total, n, dot(grad_pre[n], first[n], NT))
        return unused

    lax.fori_loop(0, chunks, step, 0)
    low_grad[:, : total.shape[1]] = total[...].astype(BF)
    finish(leaving + begin(back_pairs(grad_outs, low_grad), sem_p))
    for n in range(chunks):
        finish(copies_of([(grad_pre.at[n], pre_ref.at[n])], sem_r.at[pl.ds(n + 1, 1)]))


def expert_back(grads, slope, logit, sub, w_in, w_back):
    count = len(grads)
    rows, width = grads[0].shape
    rows = rows * count
    ff = w_in.shape[3]
    chunk = min(CHUNK, ff)
    chunks = ff // chunk
    out = pl.pallas_call(
        functools.partial(expert_back_kernel, sub, count),
        in_specs=[VMEM] + [ANY] * (3 + count),
        out_specs=[ANY] * (count + 2) + [VMEM],
        out_shape=[shape((rows // count, width + LANES), BF)] * count
        + [shape((rows, width), BF), shape((chunks, rows, chunk), BF), shape((chunks, 1, chunk), F32)],
        scratch_shapes=[
            pltpu.VMEM((rows, width), BF),
            pltpu.VMEM((chunks, width, chunk), BF),
            pltpu.VMEM((chunks, chunk, width), BF),
            pltpu.VMEM((chunks, rows, chunk), F32),
            pltpu.VMEM((chunks, rows, chunk), BF),
            pltpu.VMEM((rows, width), F32),
            pltpu.VMEM((rows, width + LANES), BF),
            pltpu.SemaphoreType.DMA((2 * chunks,)),
            pltpu.SemaphoreType.DMA((chunks,)),
            pltpu.SemaphoreType.DMA((count,)),
            pltpu.SemaphoreType.DMA((count,)),
            pltpu.SemaphoreType.DMA((chunks + 1,)),
        ],
        cost_estimate=pl.CostEstimate(
            flops=4 * rows * width * ff, bytes_accessed=10 * rows * width, transcendentals=0
        ),
        name="expert_back",
    )(logit, w_in, w_back, slope, *grads)
    return out[:count], *out[count:]


def weight_grads_kernel(chunked_left, left_ref, right_ref, *refs):
    out_ref = refs[-1]
    if chunked_left:
        left, right = left_ref[0], right_ref[...]
    else:
        left, right = left_ref[...], right_ref[0]
    out_ref[0, 0] = lax.dot_general(left, right, (((0,), (0,)), ((), ())), preferred_element_type=F32)


def weight_grads(left, right, sub, held, chunked_left):
    chunked, plain = (left, right) if chunked_left else (right, left)
    chunks, rows, chunk = chunked.shape
    width = plain.shape[1]
    pieces = pl.BlockSpec((1, rows, chunk), lambda n: (n, 0, 0))
    whole = pl.BlockSpec((rows, width), lambda n: (0, 0))
    if chunked_left:
        in_specs = [pieces, whole]
        out_spec = pl.BlockSpec((1, 1, chunk, width), lambda n: (0, sub, n, 0))
        dims = (1, 2, chunks * chunk, width)
    else:
        in_specs = [whole, pieces]
        out_spec = pl.BlockSpec((1, 1, width, chunk), lambda n: (0, sub, 0, n))
        dims = (1, 2, width, chunks * chunk)
    more = [] if held is None else [held]
    return pl.pallas_call(
        functools.partial(weight_grads_kernel, chunked_left),
        grid=(chunks,),
        in_specs=in_specs + [ANY] * len(more),
        out_specs=out_spec,
        out_shape=shape(dims, F32),
        input_output_aliases={2: 0} if more else {},
        cost_estimate=pl.CostEstimate(
            flops=2 * rows * width * chunks * chunk,
            bytes_accessed=4 * width * chunks * chunk + 2 * rows * (width + chunks * chunk),
            transcendentals=0,
        ),
        name="weight_grads",
    )(left, right, *more)


def stack_gather(value, axis, size):
    for bit in bits_of(size):
        value = jnp.concatenate([value, send_xor(value, axis, size, 1 << bit)])
    return value


def stack_scatter(value, axis, size):
    for bit in bits_of(size)[::-1]:
        half = value.shape[0] // 2
        value = value[:half] + send_xor(value[half:], axis, size, 1 << bit)
    return value


def together(*values):
    return lax.optimization_barrier(values)


def after(value, *earlier):
    return lax.optimization_barrier((value, *earlier))[0]


def gather_pieces(first, second, axis, size):
    bits = bits_of(size)
    return gather_path(first, axis, size, bits) + gather_path(second, axis, size, bits[::-1])


def scatter_pieces(pieces, axis, size):
    bits = bits_of(size)
    return scatter_path(pieces[:size], axis, size, bits) + scatter_path(
        pieces[size:], axis, size, bits[::-1]
    )


def shards(
    tokens,
    block_ids,
    expert_ids,
    cotangent,
    norm_gain,
    norm_shift,
    w_query,
    w_key,
    w_value,
    w_output,
    centroids,
    expert_gain,
    expert_shift,
    w_in,
    b_in,
    w_back,
    b_back,
):
    rows_n = lax.axis_size("row")
    cols_n = lax.axis_size("col")
    r = lax.axis_index("row")
    c = lax.axis_index("col")
    me = jnp.stack([r, c]).astype(jnp.int32)
    tok, width = tokens.shape
    fw = width // cols_n
    heads = HEADS // cols_n
    scale = float(width // HEADS) ** (-0.5)
    part = width // rows_n
    own = norm_gain.shape[0]
    slot = tok // cols_n

    count = 2 * own + part
    small_experts = jnp.concatenate([expert_gain[0], expert_shift[0], b_back[0]]).reshape(-1)
    more = 16 * -(-small_experts.shape[0] // (64 * fw))
    small_experts = jnp.pad(small_experts, (0, more * 4 * fw - small_experts.shape[0]))
    w_cat = jnp.concatenate(
        [
            jnp.concatenate([w_query, w_key, w_value, w_output], axis=1),
            small_experts.reshape(more, 4 * fw),
        ]
    )
    out_order = jnp.stack(col_order(c, cols_n)).astype(jnp.int32)

    def gather_tiles(value):
        return lax.all_gather(value, "col", axis=0, tiled=True).reshape(cols_n, rows_n, part, fw)

    def matrix_sums(part_qkv, part_output):
        parts = jnp.concatenate([part_qkv, part_output], axis=1).reshape(rows_n, part, 4 * fw)
        parts = reorder(parts, r, rows_n)
        return direct_exchange([parts[m] for m in range(rows_n)], "row", rows_n)

    def exchange(rows):
        return lax.all_to_all(
            rows.reshape(cols_n, -1, rows.shape[-1]), "col", split_axis=0, concat_axis=0, tiled=True
        ).reshape(rows.shape)

    onehot = expert_ids[:, None] == jnp.arange(LANES, dtype=jnp.int32)[None, :]
    onehot_low = onehot.astype(BF)
    below = (jnp.arange(tok)[:, None] > jnp.arange(tok)[None, :]).astype(BF)
    before = dot(below, onehot_low)
    rank = jnp.sum(jnp.where(onehot, before, 0.0), axis=1).astype(jnp.int32)
    place = expert_ids * slot + rank
    route = (jnp.arange(tok, dtype=jnp.int32)[:, None] == place[None, :]).astype(BF)
    unroute = (place[:, None] == jnp.arange(tok, dtype=jnp.int32)[None, :]).astype(BF)
    moved_cot = dot(route, cotangent).astype(BF)

    small = jnp.concatenate([norm_gain, norm_shift, centroids[0], block_ids[0].astype(BF)])[None]

    def small_params(small):
        small = small.reshape(cols_n, rows_n, count + tok)
        small = reorder(small.transpose(1, 0, 2), r, rows_n).transpose(1, 0, 2)
        gain, shift = [
            small[:, :, n * own : (n + 1) * own].transpose(1, 0, 2).reshape(1, width).astype(F32)
            for n in range(2)
        ]
        cents = small[:, :, 2 * own : count].reshape(cols_n, width)
        ids = lax.dynamic_index_in_dim(small[:, :, count:], r, 1, keepdims=False)
        return gain, shift, jnp.pad(cents, ((0, LANES - cols_n), (0, 0))), ids.astype(F32)

    if cols_n == 8:
        chips = cols_n // 2
        z, core = c // 2, c % 2
        move_right = lambda v, s: lax.ppermute(v, "col", right_pairs(s - 1, chips - 2, cols_n))
        move_left = lambda v, s: lax.ppermute(v, "col", left_pairs(1, chips - s, cols_n))
        swap = lambda v: swap_core(v, cols_n)
        right_1, left_1 = move_right(tokens, 1), move_left(tokens, 1)
        tokens_s, small_s = swap(tokens), swap(small)
        right_1, left_1, tokens_s, small_s = together(right_1, left_1, tokens_s, small_s)
        right_2, left_2 = move_right(right_1, 2), move_left(left_1, 2)
        near = jnp.where(z < 2, left_1, right_1)
        near_s = swap(near)
        small = jnp.concatenate(direct_gather(jnp.stack([small, small_s]), "row", rows_n), axis=1)
        right_2, left_2, near, near_s, small = together(right_2, left_2, near, near_s, small)
        right_3, left_3 = move_right(right_2, 3), move_left(left_2, 3)
        middle = jnp.where(
            z < 2, jnp.where(z == 0, left_2, right_1), jnp.where(z == 2, left_1, right_2)
        )
        middle_s = swap(middle)
        small = [small] + [send_xor(small, "col", cols_n, 2 * m) for m in range(1, chips)]
        w_pieces = direct_gather(after(w_cat, right_2), "row", rows_n)
        joined = together(
            right_3, left_3, middle, middle_s, onehot_low, route, unroute, moved_cot, *small, *w_pieces
        )
        right_3, left_3, middle, middle_s, onehot_low, route, unroute, moved_cot = joined[:8]
        small, w_pieces = joined[8 : 8 + chips], joined[8 + chips :]
        far = jnp.where(z < 2, jnp.where(z == 0, left_3, left_2), jnp.where(z == 2, right_2, right_3))
        far_s = swap(far)
        w_cat, tile_rows_own, small_experts = arrange_rows(w_pieces, part, (3 * fw, fw), me)
        small = reorder(reorder(jnp.stack(small), z, chips).transpose(1, 0, 2, 3), core, 2)
        gain_attn, shift_attn, full_centroids, ids = small_params(small.transpose(1, 0, 2, 3))
        tiles = gather_tiles(after(tile_rows_own, far))
        early = project(
            [tokens, tokens_s, near, near_s, middle, middle_s], gain_attn, shift_attn, w_cat, scale
        )
        cot_own = exchange(after(moved_cot, early[1]))
        late = project([far, far_s], gain_attn, shift_attn, w_cat, scale)
        from_z = [
            z,
            jnp.where(z % 2 == 0, 1, 2),
            jnp.where(z < 2, jnp.where(z == 0, 2, 0), jnp.where(z == 2, 3, 1)),
            jnp.where(z < 2, 3, 0),
        ]
        order = jnp.stack([at * 2 + (core ^ n) for at in from_z for n in range(2)]).astype(jnp.int32)
        projected = list(zip(early, late))
    else:
        small = jnp.concatenate(direct_gather(small, "row", rows_n))
        small = lax.all_gather(small, "col", axis=0, tiled=True)
        gain_attn, shift_attn, full_centroids, ids = small_params(small)
        w_pieces = direct_gather(w_cat, "row", rows_n)
        cot_own = exchange(moved_cot)
        w_cat, tile_rows_own, small_experts = arrange_rows(w_pieces, part, (3 * fw, fw), me)
        tiles = gather_tiles(tile_rows_own)
        order = out_order
        blocks = col_gather(tokens, cols_n)
        projected = [(p,) for p in project(blocks, gain_attn, shift_attn, w_cat, scale)]
    normed, q, k, v, kt, vt = projected

    ctx_low, ctx, lse, ends = attend(q, k, vt, ids, order, heads, me)
    cot_own, small_experts, *ctx_low = together(cot_own, small_experts, *ctx_low)
    bits = bits_of(rows_n)
    near_cot = {
        half: gather_path(cot_own[half * tok // 2 : (half + 1) * tok // 2], "row", rows_n, [bit])
        for half, bit in ((0, bits[0]), (1, bits[-1]))
    }
    ctx_low = direct_exchange(ctx_low, "col", cols_n)
    rest = together(*ctx_low, *near_cot[0], *near_cot[1])
    ctx_low, near_cot = rest[:cols_n], {0: rest[cols_n : cols_n + 2], 1: rest[cols_n + 2 :]}
    cot_pieces = gather_path(near_cot[0], "row", rows_n, bits[1:], [bits[0]]) + gather_path(
        near_cot[1], "row", rows_n, bits[::-1][1:], [bits[-1]]
    )
    experts = small_experts.reshape(rows_n, -1)[:, : 6 * part].reshape(rows_n, 6, part)
    experts = experts.transpose(1, 0, 2).reshape(6, width).astype(F32)
    moved, ctx_low, residual, gate = forward_rows(
        ctx_low, tiles, tokens, full_centroids, onehot_low, route, me
    )

    rest = together(*direct_exchange(moved, "col", cols_n), *cot_pieces)
    arrived, cot_pieces = rest[:cols_n], rest[cols_n:]
    stream_0, grad_2, half_1, half_2 = enter_expert(arrived, experts, cot_own, me)
    wide_pieces = gather_pieces(half_1, half_2, "row", rows_n)
    partial, normed_all_0, hidden_0, slope_0 = expert_first(wide_pieces, 0, w_in, w_back, b_in[0, 0])
    stream_1, half_1, half_2 = between_experts(
        experts, stream_0, scatter_pieces(partial, "row", rows_n)
    )
    pieces = gather_pieces(half_1, half_2, "row", rows_n)
    partial, normed_all_1, grad_all_1, hidden_1, grad_pre_1, bias_1 = expert_second(
        pieces, wide_pieces, cot_pieces, 1, w_in, w_back, b_in[0, 1]
    )
    sums = scatter_pieces(partial, "row", rows_n)
    branch, logit = expert_branch(hidden_1, cot_pieces, 1, w_back, me)
    branch, logit, *sums = together(branch, logit, *sums)
    grad_1, half_1, half_2, sums_1 = middle_back(experts, stream_1, grad_2, sums)
    pieces = gather_pieces(half_1, half_2, "row", rows_n)
    w_back_grad = weight_grads(hidden_1, after(grad_all_1, grad_1), 1, None, True)
    w_back_grad, *pieces = together(w_back_grad, *pieces)
    partial, grad_all_0, grad_pre_0, bias_0 = expert_back(pieces, slope_0, logit, 0, w_in, w_back)
    sums = together(*scatter_pieces(partial, "row", rows_n))
    branch = lax.psum_scatter(after(branch, sums[0]), "row", scatter_dimension=0, tiled=True)
    *leaving, sums_0 = leave_back(experts, stream_0, grad_1, cot_own, stream_1, sums, me, cols_n)
    returned = direct_exchange(leaving, "col", cols_n)
    w_in_grad = weight_grads(normed_all_0, after(grad_pre_0, sums_0), 0, None, False)
    w_in_grad, *returned = together(w_in_grad, *returned)
    grad_residual, grad_attended, part_cent, grad_ctx = backward_rows(
        returned, tiles, unroute, cotangent, full_centroids, onehot_low, gate, residual, me
    )

    grad_ctx = exchange(grad_ctx)
    part_output = output_grads(ctx_low, grad_attended, rows_n, cols_n)
    w_back_grad = weight_grads(hidden_0, after(grad_all_0, grad_attended), 0, w_back_grad, True)
    expert_low = finish_rows(stream_1, branch, experts)
    part_output, w_back_grad, expert_low, grad_ctx = together(
        part_output, w_back_grad, expert_low, grad_ctx
    )
    expert_low = exchange(expert_low)
    part_output = lax.psum_scatter(
        part_output.reshape(cols_n * width, fw), "col", scatter_dimension=0, tiled=True
    )
    partial, dq, dk, dv = attend_back(
        q, k, v, kt, normed, grad_ctx.reshape(cols_n, fw, tok), ctx, lse, w_cat, gain_attn, shift_attn,
        part_cent, ends, order, out_order, heads, scale,
    )
    dq, expert_low, *partial = together(dq, expert_low, *partial)
    if cols_n == 8:
        halves = [
            add_low(partial[2 * turn], swap(partial[2 * turn + 1])) for turn in range(chips)
        ]
        into_right = lambda v, s: lax.ppermute(
            v, "col", right_pairs(0, min(s - 1, chips - 2), cols_n)
        )
        into_left = lambda v, s: lax.ppermute(
            v, "col", left_pairs(max(chips - s, 1), chips - 1, cols_n)
        )
        from_left, from_right = into_right(halves[3], 1), into_left(halves[1], 1)
        part_qkv = project_grads(after(dq, halves[3]), dk, dv, normed, order, rows_n)
        from_left, from_right, part_qkv, part_output = together(
            from_left, from_right, part_qkv, part_output
        )
        from_left = into_right(add_low(from_left, halves[2]), 2)
        from_right = into_left(add_low(from_right, halves[2]), 2)
        output = (residual + gate * dot(unroute, expert_low)).astype(BF)
        grad_sums = matrix_sums(part_qkv, part_output)
        from_left, from_right, output, *grad_sums = together(from_left, from_right, output, *grad_sums)
        normed_all_1, from_left, from_right = together(normed_all_1, from_left, from_right)
        from_left = into_right(add_low(from_left, halves[1]), 3)
        from_right = into_left(add_low(from_right, halves[3]), 3)
        w_in_grad = weight_grads(normed_all_1, grad_pre_1, 1, w_in_grad, False)
        from_left, from_right, w_in_grad = together(from_left, from_right, w_in_grad)
        summed = halves[0].astype(F32) + from_left.astype(F32) + from_right.astype(F32)
    else:
        part_qkv = project_grads(dq, dk, dv, normed, order, rows_n)
        output = (residual + gate * dot(unroute, expert_low)).astype(BF)
        grad_sums = matrix_sums(part_qkv, part_output)
        w_in_grad = weight_grads(normed_all_1, grad_pre_1, 1, w_in_grad, False)
        summed = col_scatter(partial, cols_n)
    grad_matrices = sum(v.astype(F32) for v in grad_sums)
    grad_qkv, grad_output = grad_matrices[:, : 3 * fw], grad_matrices[:, 3 * fw :]
    grad_normed_attn = summed[:tok]

    norm_rows = summed[tok : tok + 2].reshape(2, rows_n, cols_n, own)
    norm_rows = lax.dynamic_index_in_dim(norm_rows, c, 2, keepdims=False).transpose(1, 0, 2)
    expert_rows = jnp.concatenate([sums_0, sums_1]).reshape(6, rows_n, part).transpose(1, 0, 2)
    packed = jnp.concatenate(
        [
            norm_rows.reshape(rows_n, 2 * own),
            summed[tok + 2].reshape(rows_n, part),
            expert_rows.reshape(rows_n, 6 * part),
        ],
        axis=1,
    )[:, None]
    packed = reorder(packed, r, rows_n)
    packed = sum(direct_exchange([packed[m] for m in range(rows_n)], "row", rows_n))[0]
    expert_sums = packed[count:].reshape(2, 3, part).transpose(1, 0, 2)

    inputs = tokens.astype(F32)
    unit_attn, inv_attn = layer_stats(inputs)
    tokens_grad = grad_residual + norm_back(grad_normed_attn, unit_attn, inv_attn, gain_attn)
    return (
        output,
        tokens_grad,
        packed[:own],
        packed[own : 2 * own],
        grad_qkv[:, :fw],
        grad_qkv[:, fw : 2 * fw],
        grad_qkv[:, 2 * fw :],
        grad_output,
        packed[None, 2 * own : count],
        expert_sums[None, 0],
        expert_sums[None, 1],
        w_in_grad,
        jnp.stack([bias_0.reshape(-1), bias_1.reshape(-1)])[None],
        w_back_grad,
        expert_sums[None, 2],
    )


def solution(mesh):
    placed = (
        P(("row", "col"), None),
        P("row", "col"),
        P(("row", "col")),
        P(("row", "col"), None),
        P(("row", "col")),
        P(("row", "col")),
        P("row", "col"),
        P("row", "col"),
        P("row", "col"),
        P("row", "col"),
        P("col", "row"),
        P("col", None, "row"),
        P("col", None, "row"),
        P("col", None, None, "row"),
        P("col", None, "row"),
        P("col", None, "row", None),
        P("col", None, "row"),
    )
    return jax.shard_map(
        shards,
        mesh=mesh,
        in_specs=placed,
        out_specs=(
            P(("row", "col"), None),
            P(("row", "col"), None),
            P(("row", "col")),
            P(("row", "col")),
            P("row", "col"),
            P("row", "col"),
            P("row", "col"),
            P("row", "col"),
            P("col", "row"),
            P("col", None, "row"),
            P("col", None, "row"),
            P("col", None, None, "row"),
            P("col", None, "row"),
            P("col", None, "row", None),
            P("col", None, "row"),
        ),
        check_vma=False,
    )
```

```python
import functools

import jax
import jax.numpy as jnp
from jax import lax
from jax.experimental import pallas as pl
from jax.experimental.pallas import tpu as pltpu
from jax.sharding import PartitionSpec as P

HEADS = 16
EPS = 1e-05
NEG = -1e30
BF = jnp.bfloat16
F32 = jnp.float32
NT = (((1,), (1,)), ((), ()))
NN = (((1,), (0,)), ((), ()))
LANES = 128


def dot(left, right, dims=NN):
    return lax.dot_general(left, right, dims, preferred_element_type=F32)


def add_low(left, right):
    return (left.astype(F32) + right.astype(F32)).astype(BF)


def send_xor(value, axis, size, mask):
    return lax.ppermute(value, axis, [(i, i ^ mask) for i in range(size)])


def bits_of(size):
    return list(range(size.bit_length() - 1))


def gather_path(values, axis, size, bits, done=()):
    if not done:
        values = [values]
    held = dict(zip([0] + [1 << bit for bit in done], values))
    for bit in bits:
        held.update({m | (1 << bit): send_xor(v, axis, size, 1 << bit) for m, v in list(held.items())})
    return [held[m] for m in sorted(held)]


def scatter_path(blocks, axis, size, bits):
    held = {m: [v] for m, v in enumerate(blocks)}
    for bit in bits:
        leaving = {m: v for m, v in held.items() if (m >> bit) & 1}
        held = {m: v for m, v in held.items() if not (m >> bit) & 1}
        for m, v in leaving.items():
            total = v[0] if len(v) == 1 else sum(n.astype(F32) for n in v).astype(BF)
            held[m & ~(1 << bit)].append(send_xor(total, axis, size, 1 << bit))
    return held[0]


def direct_gather(value, axis, size):
    return [value] + [send_xor(value, axis, size, m) for m in range(1, size)]


def direct_exchange(blocks, axis, size):
    return [blocks[0]] + [send_xor(blocks[m], axis, size, m) for m in range(1, size)]


def reorder(stacked, mine, size):
    return jnp.concatenate(
        [lax.dynamic_index_in_dim(stacked, mine ^ j, 0, keepdims=True) for j in range(size)]
    )


def swap_core(value, size):
    return send_xor(value, "col", size, 1)


def right_pairs(first, last, size):
    return [(i, i + 2) for i in range(size) if first <= i // 2 <= last]


def left_pairs(first, last, size):
    return [(i, i - 2) for i in range(size) if first <= i // 2 <= last]


def line_order(mine, size):
    chips = size // 2
    return [
        ((mine // 2 + turn) % chips) * 2 + ((mine % 2) ^ core)
        for turn in range(chips)
        for core in range(2)
    ]


def col_order(mine, size):
    return line_order(mine, size) if size == 8 else [mine ^ m for m in range(size)]


def col_gather(value, size):
    return gather_path(value, "col", size, bits_of(size))


def col_scatter(blocks, size):
    return sum(v.astype(F32) for v in scatter_path(blocks, "col", size, bits_of(size)))


def layer_stats(stream):
    center = stream - jnp.mean(stream, axis=-1, keepdims=True)
    inv_root = lax.rsqrt(jnp.mean(center * center, axis=-1, keepdims=True) + EPS)
    return (center * inv_root, inv_root)


def norm_back(grad_normed, unit_rows, inv_root, gain_full):
    grad_unit = grad_normed * gain_full
    mean_first = jnp.mean(grad_unit, axis=-1, keepdims=True)
    mean_second = jnp.mean(grad_unit * unit_rows, axis=-1, keepdims=True)
    return inv_root * (grad_unit - mean_first - unit_rows * mean_second)


ANY = pl.BlockSpec(memory_space=pl.ANY)
HBM = pl.BlockSpec(memory_space=pltpu.HBM)
VMEM = pl.BlockSpec(memory_space=pltpu.VMEM)
SMEM = pl.BlockSpec(memory_space=pltpu.SMEM)


def shape(dims, kind):
    return jax.ShapeDtypeStruct(dims, kind)


def params(mib):
    return pltpu.CompilerParams(vmem_limit_bytes=mib * 1024 * 1024)


def copies_of(pairs, sems):
    return [pltpu.make_async_copy(s, d, sems.at[n]) for n, (s, d) in enumerate(pairs)]


def begin(pairs, sems):
    copies = copies_of(pairs, sems)
    for copy in copies:
        copy.start()
    return copies


def finish(copies):
    for copy in copies:
        copy.wait()


def arrange_kernel(count, me_ref, *refs):
    outs, rest = refs[count:-1], refs[-1]
    rows = outs[0].shape[0] // count
    for m in range(count):
        owner = me_ref[0] ^ m
        at = pl.ds(pl.multiple_of(owner * rows, rows), rows)
        done = 0
        for out in outs:
            out[at, :] = refs[m][:rows, done : done + out.shape[1]]
            done += out.shape[1]
        rest[owner] = refs[m][rows:, :]


def arrange_rows(pieces, rows, widths, me):
    count = len(pieces)
    kind = pieces[0].dtype
    return pl.pallas_call(
        functools.partial(arrange_kernel, count),
        in_specs=[SMEM] + [VMEM] * count,
        out_specs=[VMEM] * (len(widths) + 1),
        out_shape=[shape((count * rows, w), kind) for w in widths]
        + [shape((count, pieces[0].shape[0] - rows, pieces[0].shape[1]), kind)],
        name="arrange_rows",
    )(me, *pieces)


def tile_rows(tiles_ref, block):
    return jnp.concatenate([tiles_ref[col, block] for col in range(tiles_ref.shape[0])], axis=1)


def scalar_lanes(values):
    high = values.astype(BF).astype(F32)
    lane = lax.broadcasted_iota(jnp.int32, (values.shape[0], LANES), 1)
    return jnp.where(lane == 0, high, jnp.where(lane == 1, values - high, 0.0)).astype(BF)


def forward_kernel(total, me_ref, tiles_ref, tokens_ref, cent_ref, onehot_ref, route_ref, *refs):
    pieces, refs = refs[:total], refs[total:]
    moved, (ctx_ref, residual_ref, gate_ref, sent) = refs[:total], refs[total:]
    unused, rows_n, part, unused = tiles_ref.shape
    place_pieces(pieces, me_ref, ctx_ref)
    held = tokens_ref[...].astype(F32)
    for n in range(rows_n):
        held = held + lax.dot_general(
            ctx_ref[n * part : (n + 1) * part, :],
            tile_rows(tiles_ref, n),
            (((0,), (0,)), ((), ())),
            preferred_element_type=F32,
        )
    residual_ref[...] = held
    shared = held.astype(BF)
    cent_rows = dot(onehot_ref[...], cent_ref[...])
    gate = jax.nn.sigmoid(jnp.sum(shared.astype(F32) * cent_rows, axis=1, keepdims=True))
    gate_ref[...] = gate
    leaving = jnp.concatenate([shared, scalar_lanes(gate)], axis=1)
    sent[...] = dot(route_ref[...], leaving).astype(BF)
    slot = moved[0].shape[0]
    for m in range(total):
        moved[m][...] = sent[pl.ds(pl.multiple_of((me_ref[1] ^ m) * slot, slot), slot), :]


def forward_rows(pieces, tiles, tokens, cent, onehot, route, me):
    total = len(pieces)
    tok, width = tokens.shape
    out = pl.pallas_call(
        functools.partial(forward_kernel, total),
        in_specs=[SMEM] + [VMEM] * (5 + total),
        out_specs=[VMEM] * (total + 3),
        out_shape=[shape((tok // total, width + LANES), BF)] * total
        + [shape((width, tok), BF), shape((tok, width), F32), shape((tok, 1), F32)],
        scratch_shapes=[pltpu.VMEM((tok, width + LANES), BF)],
        cost_estimate=pl.CostEstimate(
            flops=3 * tok * width * width, bytes_accessed=2 * width * width + 8 * tok * width, transcendentals=0
        ),
        name="forward_rows",
    )(me, tiles, tokens, cent, onehot, route, *pieces)
    return out[:total], *out[total:]


def enter_kernel(total, me_ref, experts_ref, cot_ref, *refs):
    pieces, (stream_ref, grad_ref, first_ref, second_ref, rows_ref) = refs[:total], refs[total:]
    width = stream_ref.shape[1]
    half = first_ref.shape[0]
    place_pieces(pieces, me_ref, rows_ref)
    stream = rows_ref[:, :width]
    lanes = rows_ref[:, width:]
    gate = jnp.sum(lanes.astype(F32), axis=1, keepdims=True)
    stream_ref[...] = stream
    unit_rows, unused = layer_stats(stream.astype(F32))
    normed = (unit_rows * experts_ref[0:1] + experts_ref[2:3]).astype(BF)
    first_ref[:, :width] = normed[:half]
    first_ref[:, width:] = lanes[:half]
    second_ref[:, :width] = normed[half:]
    second_ref[:, width:] = lanes[half:]
    grad_ref[...] = (cot_ref[...].astype(F32) * gate).astype(BF)


def enter_expert(pieces, experts, cot, me):
    total = len(pieces)
    tok, width = cot.shape
    wide = (tok // 2, width + LANES)
    return pl.pallas_call(
        functools.partial(enter_kernel, total),
        in_specs=[SMEM] + [VMEM] * (2 + total),
        out_specs=[VMEM] * 4,
        out_shape=[shape((tok, width), BF)] * 2 + [shape(wide, BF)] * 2,
        scratch_shapes=[pltpu.VMEM((tok, width + LANES), BF)],
        cost_estimate=pl.CostEstimate(flops=20 * tok * width, bytes_accessed=10 * tok * width, transcendentals=0),
        name="enter_expert",
    )(me, experts, cot, *pieces)


def add_up(refs, lanes):
    return sum(ref[:, lanes].astype(F32) for ref in refs)


def halves_of(refs):
    return refs[: len(refs) // 2], refs[len(refs) // 2 :]


def between_kernel(experts_ref, stream_ref, *refs):
    sums, (out_ref, first_ref, second_ref) = refs[:-3], refs[-3:]
    half = first_ref.shape[0]
    for n, (parts, low) in enumerate(zip(halves_of(sums), (first_ref, second_ref))):
        at = slice(n * half, (n + 1) * half)
        stream = stream_ref[at, :].astype(F32) + add_up(parts, slice(None)) + experts_ref[4:5]
        out_ref[at, :] = stream
        unit_rows, unused = layer_stats(stream)
        low[...] = (unit_rows * experts_ref[1:2] + experts_ref[3:4]).astype(BF)


def between_experts(experts, stream, sums):
    tok, width = stream.shape
    return pl.pallas_call(
        between_kernel,
        in_specs=[VMEM] * (2 + len(sums)),
        out_specs=[VMEM] * 3,
        out_shape=[shape((tok, width), F32)] + [shape((tok // 2, width), BF)] * 2,
        cost_estimate=pl.CostEstimate(flops=20 * tok * width, bytes_accessed=12 * tok * width, transcendentals=0),
        compiler_params=params(20),
        name="between_experts",
    )(experts, stream, *sums)


def norm_grads(half, sub, experts_ref, stream_ref, upper_ref, sums, sums_ref):
    width = stream_ref.shape[1]
    grads = []
    for n, parts in enumerate(halves_of(sums)):
        at = slice(n * half, (n + 1) * half)
        grad_normed = add_up(parts, slice(0, width))
        unit_rows, inv_root = layer_stats(stream_ref[at, :].astype(F32))
        upper = upper_ref[at, :].astype(F32)
        for row, values in enumerate((grad_normed * unit_rows, grad_normed, upper)):
            total = jnp.sum(values, axis=0, keepdims=True)
            if n == 0:
                sums_ref[row : row + 1, :] = total
            else:
                sums_ref[row : row + 1, :] += total
        grads.append(upper + norm_back(grad_normed, unit_rows, inv_root, experts_ref[sub : sub + 1]))
    return grads


def middle_back_kernel(experts_ref, stream_ref, upper_ref, *refs):
    sums, (out_ref, first_ref, second_ref, sums_ref) = refs[:-4], refs[-4:]
    half = first_ref.shape[0]
    grads = norm_grads(half, 1, experts_ref, stream_ref, upper_ref, sums, sums_ref)
    for n, low in enumerate((first_ref, second_ref)):
        out_ref[n * half : (n + 1) * half, :] = grads[n]
        low[...] = grads[n].astype(BF)


def middle_back(experts, stream, upper, sums):
    tok, width = stream.shape
    return pl.pallas_call(
        middle_back_kernel,
        in_specs=[VMEM] * (3 + len(sums)),
        out_specs=[VMEM] * 4,
        out_shape=[shape((tok, width), F32)] + [shape((tok // 2, width), BF)] * 2 + [shape((3, width), F32)],
        cost_estimate=pl.CostEstimate(flops=40 * tok * width, bytes_accessed=16 * tok * width, transcendentals=0),
        name="middle_back",
    )(experts, stream, upper, *sums)


def leave_back_kernel(total, me_ref, experts_ref, stream_ref, upper_ref, cot_ref, later_ref, *refs):
    sums, refs = refs[: -total - 2], refs[-total - 2 :]
    outs, sums_ref, held = refs[:total], refs[total], refs[total + 1]
    width = stream_ref.shape[1]
    slot = outs[0].shape[0]
    half = stream_ref.shape[0] // 2
    grads = norm_grads(half, 0, experts_ref, stream_ref, upper_ref, sums, sums_ref)
    for n, parts in enumerate(halves_of(sums)):
        at = slice(n * half, (n + 1) * half)
        kept = cot_ref[at, :].astype(F32) * (later_ref[at, :] + experts_ref[5:6])
        logit = jnp.sum(add_up(parts, slice(width, None)), axis=1, keepdims=True)
        logit = logit + jnp.sum(kept, axis=1, keepdims=True)
        held[at, :width] = grads[n].astype(BF)
        held[at, width:] = scalar_lanes(logit)
    for m in range(total):
        outs[m][...] = held[pl.ds(pl.multiple_of((me_ref[1] ^ m) * slot, slot), slot), :]


def leave_back(experts, stream, upper, cot, later, sums, me, total):
    tok, width = stream.shape
    return pl.pallas_call(
        functools.partial(leave_back_kernel, total),
        in_specs=[SMEM] + [VMEM] * (5 + len(sums)),
        out_specs=[VMEM] * (total + 1),
        out_shape=[shape((tok // total, width + LANES), BF)] * total + [shape((3, width), F32)],
        scratch_shapes=[pltpu.VMEM((tok, width + LANES), BF)],
        cost_estimate=pl.CostEstimate(flops=40 * tok * width, bytes_accessed=20 * tok * width, transcendentals=0),
        name="leave_back",
    )(me, experts, stream, upper, cot, later, *sums)


def place_pieces(pieces, me_ref, held):
    rows = pieces[0].shape[0]
    for m, piece in enumerate(pieces):
        held[pl.ds(pl.multiple_of((me_ref[1] ^ m) * rows, rows), rows), :] = piece[...]


def backward_kernel(total, me_ref, tiles_ref, unroute_ref, cot_ref, cent_ref, onehot_ref, gate_ref, residual_ref, *refs):
    pieces, (out_ref, low_ref, cent_out, ctx_ref, back_ref) = refs[:total], refs[total:]
    place_pieces(pieces, me_ref, back_ref)
    width = cot_ref.shape[1]
    unused, rows_n, part, unused = tiles_ref.shape
    back = dot(unroute_ref[...], back_ref[...])
    gate = gate_ref[...]
    grad_logit = jnp.sum(back[:, width:], axis=1, keepdims=True) * gate * (1.0 - gate)
    cent_rows = dot(onehot_ref[...], cent_ref[...])
    grad = cot_ref[...].astype(F32) + (back[:, :width] + grad_logit * cent_rows)
    out_ref[...] = grad
    low = grad.astype(BF)
    low_ref[...] = low
    for n in range(rows_n):
        ctx_ref[n * part : (n + 1) * part, :] = dot(tile_rows(tiles_ref, n), low, NT).astype(BF)
    cent_out[...] = lax.dot_general(
        onehot_ref[...].astype(F32),
        grad_logit * residual_ref[...].astype(BF).astype(F32),
        (((0,), (0,)), ((), ())),
        precision=lax.Precision.HIGHEST,
        preferred_element_type=F32,
    )


def backward_rows(pieces, tiles, unroute, cot, cent, onehot, gate, residual, me):
    tok, width = cot.shape
    total = len(pieces)
    return pl.pallas_call(
        functools.partial(backward_kernel, total),
        in_specs=[SMEM] + [VMEM] * (7 + total),
        out_specs=[VMEM] * 4,
        out_shape=[
            shape((tok, width), F32),
            shape((tok, width), BF),
            shape((LANES, width), F32),
            shape((width, tok), BF),
        ],
        scratch_shapes=[pltpu.VMEM((tok, width + LANES), BF)],
        cost_estimate=pl.CostEstimate(
            flops=3 * tok * width * width, bytes_accessed=2 * width * width + 12 * tok * width, transcendentals=0
        ),
        name="backward_rows",
    )(me, tiles, unroute, cot, cent, onehot, gate, residual, *pieces)


def finish_kernel(stream_ref, branch_ref, experts_ref, out_ref):
    out_ref[...] = (stream_ref[...] + branch_ref[...].astype(F32) + experts_ref[5:6]).astype(BF)


def finish_rows(stream, branch, experts):
    return pl.pallas_call(
        finish_kernel,
        in_specs=[VMEM] * 3,
        out_specs=VMEM,
        out_shape=shape(stream.shape, BF),
        name="finish_rows",
    )(stream, branch, experts)


def project_kernel(scale, count, gain_ref, shift_ref, w_ref, *refs):
    blocks, outs, refs = refs[:count], refs[count : count + 6], refs[count + 6 :]
    x_all, held, sems, out_sems = refs[0], refs[1:7], refs[7], refs[8]
    fw = w_ref.shape[1] // 3
    copies = begin([(b, x_all.at[n]) for n, b in enumerate(blocks)], sems)
    leaving = []
    for n in range(count):
        copies[n].wait()
        unit_rows, unused = layer_stats(x_all[n].astype(F32))
        normed = (unit_rows * gain_ref[...] + shift_ref[...]).astype(BF)
        held[0][n] = normed
        out = dot(normed, w_ref[...])
        keys = out[:, fw : 2 * fw]
        values = out[:, 2 * fw :]
        held[1][n] = (out[:, :fw].astype(BF).astype(F32) * scale).astype(BF)
        held[2][n] = keys.astype(BF)
        held[3][n] = values.astype(BF)
        held[4][n] = keys.T.astype(BF)
        held[5][n] = values.T.astype(BF)
        leaving += begin(
            [(h.at[n], o.at[n]) for h, o in zip(held, outs)], out_sems.at[pl.ds(6 * n, 6)]
        )
    finish(leaving)


def project(blocks, gain, shift, w, scale):
    count = len(blocks)
    rows, width = blocks[0].shape
    fw = w.shape[1] // 3
    kinds = [(count, rows, width)] + [(count, rows, fw)] * 3 + [(count, fw, rows)] * 2
    return pl.pallas_call(
        functools.partial(project_kernel, scale, count),
        in_specs=[VMEM] * 3 + [ANY] * count,
        out_specs=[ANY] * 6,
        out_shape=[shape(k, BF) for k in kinds],
        scratch_shapes=[pltpu.VMEM((count, rows, width), BF)]
        + [pltpu.VMEM(k, BF) for k in kinds]
        + [pltpu.SemaphoreType.DMA((count,)), pltpu.SemaphoreType.DMA((6 * count,))],
        cost_estimate=pl.CostEstimate(
            flops=count * (2 * rows * width * fw * 3 + 10 * rows * width),
            bytes_accessed=2 * count * (2 * rows * width + 5 * rows * fw) + 6 * width * fw,
            transcendentals=0,
        ),
        name="project",
    )(gain, shift, w, *blocks)


def views(refs):
    return [ref.at[n] for ref in refs for n in range(ref.shape[0])]


def split_lanes(rows, count):
    width = rows.shape[1] // count
    if count == 1:
        return rows
    head_of = lax.broadcasted_iota(jnp.int32, rows.shape, 1) // width
    return jnp.concatenate(
        [jnp.where(head_of == h, rows, jnp.zeros_like(rows)) for h in range(count)], axis=0
    )


def split_rows(cols, count):
    width = cols.shape[0] // count
    if count == 1:
        return cols
    head_of = lax.broadcasted_iota(jnp.int32, cols.shape, 0) // width
    return jnp.concatenate(
        [jnp.where(head_of == h, cols, jnp.zeros_like(cols)) for h in range(count)], axis=1
    )


QB = 2
KB = 2


QB = 2
KB = 2


QB = 2
KB = 2


def attend_kernel(heads, total, groups, qb, kb, me_ref, order_ref, ids_ref, *refs):
    q_in, k_in, vt_in = [views(refs[n * groups : (n + 1) * groups]) for n in range(3)]
    refs = refs[3 * groups :]
    low_refs, refs = refs[:total], refs[total:]
    ctx_ref, lse_ref, ends_ref, q_all, k_all, vt_all, low_all, count_ref, sems, out_sems = refs
    rows = low_all.shape[2]
    fw = q_all.shape[2]
    head = fw // heads
    span = qb * rows
    key_rows = kb * rows
    pairs = []
    for n in range(total):
        at = order_ref[n]
        q_at = pl.ds(pl.multiple_of(lax.rem(at, qb) * rows, rows), rows)
        k_at = pl.ds(pl.multiple_of(lax.rem(at, kb) * rows, rows), rows)
        pairs += [
            (q_in[n], q_all.at[lax.div(at, qb), q_at, :]),
            (k_in[n], k_all.at[lax.div(at, kb), k_at, :]),
            (vt_in[n], vt_all.at[lax.div(at, kb), :, k_at]),
        ]
    copies = begin(pairs, sems)

    ids = ids_ref[...]
    ends = jnp.zeros((total, rows), F32)
    for n in range(total):
        members = jnp.sum(jnp.where(ids == n, 1.0, 0.0))
        ends = ends + jnp.where(ids >= n, members, 0.0)
    for i in range(total // qb):
        ends_ref[i] = jnp.concatenate([ends[i * qb + b : i * qb + b + 1] for b in range(qb)], axis=1)
        last = jnp.max(ends[i * qb + qb - 1 : i * qb + qb]).astype(jnp.int32)
        count_ref[i] = lax.div(last + (key_rows - 1), key_rows)
    finish(copies)
    spots = lax.broadcasted_iota(jnp.int32, (key_rows, heads * span), 0).astype(F32)

    def block(i, unused):
        queries = split_lanes(q_all[i], heads)
        ends = jnp.concatenate([ends_ref[i]] * heads, axis=1)

        def step(j, state):
            run_max, run_sum, held = state
            scores = dot(k_all[j], queries, NT)
            scores = jnp.where(spots < ends - (j * key_rows).astype(F32), scores, NEG)
            new_max = jnp.maximum(run_max, jnp.max(scores, axis=0, keepdims=True))
            weights = jnp.exp(scores - new_max)
            factor = jnp.exp(run_max - new_max)
            new_sum = run_sum * factor + jnp.sum(weights, axis=0, keepdims=True)
            low = weights.astype(BF)
            values = vt_all[j]
            new_held = tuple(
                held[h] * factor[:, h * span : (h + 1) * span]
                + dot(values[h * head : (h + 1) * head], low[:, h * span : (h + 1) * span])
                for h in range(heads)
            )
            return new_max, new_sum, new_held

        start = (
            jnp.full((1, heads * span), NEG, F32),
            jnp.zeros((1, heads * span), F32),
            tuple(jnp.zeros((head, span), F32) for h in range(heads)),
        )
        run_max, run_sum, held = lax.fori_loop(0, count_ref[i], step, start)
        for h in range(heads):
            result = held[h] / run_sum[:, h * span : (h + 1) * span]
            ctx_ref[i, h * head : (h + 1) * head, :] = result
            for b in range(qb):
                low_all[i * qb + b, h * head : (h + 1) * head, :] = result[
                    :, b * rows : (b + 1) * rows
                ].astype(BF)
        lse_ref[i] = run_max + jnp.log(run_sum)
        return unused

    lax.fori_loop(0, total // qb, block, 0)
    finish(begin([(low_all.at[me_ref[1] ^ m], low_refs[m]) for m in range(total)], out_sems))


def attend(q, k, vt, ids, order, heads, me):
    total = len(order)
    groups = len(q)
    rows, fw = q[0].shape[1:]
    qb, kb = QB, KB
    pairs = total * rows * total * rows * heads
    out = pl.pallas_call(
        functools.partial(attend_kernel, heads, total, groups, qb, kb),
        in_specs=[SMEM] * 2 + [VMEM] + [ANY] * (3 * groups),
        out_specs=[ANY] * total + [VMEM] * 3,
        out_shape=[shape((fw, rows), BF)] * total
        + [
            shape((total // qb, fw, qb * rows), F32),
            shape((total // qb, 1, heads * qb * rows), F32),
            shape((total // qb, 1, qb * rows), F32),
        ],
        scratch_shapes=[
            pltpu.VMEM((total // qb, qb * rows, fw), BF),
            pltpu.VMEM((total // kb, kb * rows, fw), BF),
            pltpu.VMEM((total // kb, fw, kb * rows), BF),
            pltpu.VMEM((total, fw, rows), BF),
            pltpu.SMEM((total // qb,), jnp.int32),
            pltpu.SemaphoreType.DMA((3 * total,)),
            pltpu.SemaphoreType.DMA((total,)),
        ],
        cost_estimate=pl.CostEstimate(
            flops=2 * pairs * 128, bytes_accessed=10 * total * rows * fw, transcendentals=pairs // 2
        ),
        name="attend",
    )(me, order, ids, *q, *k, *vt)
    return out[:total], *out[total:]


def attend_back_kernel(heads, scale, total, groups, qb, kb, order_ref, out_order_ref, ends_ref, ctx_ref, lse_ref, w_ref, gain_ref, shift_ref, cent_ref, *refs):
    q_in, k_in, v_in, kt_in, normed_in = [views(refs[n * groups : (n + 1) * groups]) for n in range(5)]
    refs = refs[5 * groups :]
    grad_in, refs = refs[0], refs[1:]
    out_refs, refs = refs[:total], refs[total:]
    dq_ref, dk_ref, dv_ref = refs[:3]
    q_raw, k_all, v_all, kt_all, g_raw, q_all, grad_all, delta_all, dq_all, out_all, normed_all, small_all, first_ref = refs[3:16]
    sems, normed_sems, out_sems, small_sems = refs[16:]
    unused, rows, width = out_all.shape
    fw = q_raw.shape[2]
    head = fw // heads
    span = qb * rows
    pairs = []
    for n in range(total):
        at = order_ref[n]
        q_at = pl.ds(pl.multiple_of(lax.rem(at, qb) * rows, rows), rows)
        k_at = pl.ds(pl.multiple_of(lax.rem(at, kb) * rows, rows), rows)
        pairs += [
            (q_in[n], q_raw.at[lax.div(at, qb), q_at, :]),
            (k_in[n], k_all.at[lax.div(at, kb), k_at, :]),
            (v_in[n], v_all.at[lax.div(at, kb), k_at, :]),
            (kt_in[n], kt_all.at[lax.div(at, kb), :, k_at]),
            (grad_in.at[n], g_raw.at[n // qb, :, pl.ds((n % qb) * rows, rows)]),
        ]
    copies = begin(pairs, sems)
    normed_copies = begin([(normed_in[n], normed_all.at[order_ref[n]]) for n in range(total)], normed_sems)
    lasts = [jnp.max(ends_ref[i]).astype(jnp.int32) for i in range(total // qb)]
    for j in range(total // kb):
        first_ref[j] = sum((last <= j * kb * rows).astype(jnp.int32) for last in lasts)
    finish(copies)

    def prepare(i, unused):
        q_all[i] = split_lanes(q_raw[i], heads)
        grad = g_raw[i]
        grad_all[i] = split_rows(grad, heads)
        product = grad.astype(F32) * ctx_ref[i]
        delta_all[i] = jnp.concatenate(
            [
                jnp.sum(product[h * head : (h + 1) * head], axis=0, keepdims=True)
                for h in range(heads)
            ],
            axis=1,
        )
        dq_all[i] = jnp.zeros((fw, span), F32)
        return unused

    lax.fori_loop(0, total // qb, prepare, 0)

    spots = lax.broadcasted_iota(jnp.int32, (kb * rows, span), 0).astype(F32)

    def key_block(j, unused):
        keys = k_all[j]
        values = v_all[j]
        keys_t = kt_all[j]

        def step(i, state):
            dk, dv = state
            ends = ends_ref[i] - (j * (kb * rows)).astype(F32)
            for h in range(heads):
                at = slice(h * span, (h + 1) * span)
                queries = q_all[i, at, :]
                grads = grad_all[i, :, at]
                scores = dot(keys, queries, NT) - lse_ref[i, :, at]
                probs = jnp.exp(jnp.where(spots < ends, scores, NEG))
                grad_probs = dot(values, grads) - delta_all[i, :, at]
                grad_scores = (probs * grad_probs).astype(BF)
                dv = dv + dot(probs.astype(BF), grads, NT)
                dk = dk + dot(grad_scores, queries)
                dq_all[i, h * head : (h + 1) * head, :] += dot(
                    keys_t[h * head : (h + 1) * head], grad_scores
                )
            return dk, dv

        zero = jnp.zeros((kb * rows, fw), F32)
        dk, dv = lax.fori_loop(first_ref[j], total // qb, step, (zero, zero))
        dk_ref[pl.ds(j * kb, kb)] = dk.astype(BF).reshape(kb, rows, fw)
        dv_ref[pl.ds(j * kb, kb)] = dv.astype(BF).reshape(kb, rows, fw)
        return unused

    lax.fori_loop(0, total // kb, key_block, 0)

    def turn(i, unused):
        dq_ref[pl.ds(i * qb, qb)] = (dq_all[i] * scale).T.astype(BF).reshape(qb, rows, fw)
        return unused

    lax.fori_loop(0, total // qb, turn, 0)

    leaving = []
    lifted = jnp.zeros((1, width), F32)
    shifted = jnp.zeros((1, width), F32)
    finish(normed_copies)
    for n in range(total):
        at = out_order_ref[n]
        grad = dot(jnp.concatenate([dq_ref[at], dk_ref[at], dv_ref[at]], axis=1), w_ref[...], NT)
        out_all[n] = grad.astype(BF)
        leaving += begin(
            [(out_all.at[n], out_refs[n].at[pl.ds(0, rows), :])], out_sems.at[pl.ds(n, 1)]
        )
        shifted = shifted + jnp.sum(grad, axis=0, keepdims=True)
        lifted = lifted + jnp.sum(grad * normed_all[at].astype(F32), axis=0, keepdims=True)
    lifted = (lifted - shift_ref[...] * shifted) / gain_ref[...]
    for n in range(total):
        rest = jnp.zeros((small_all.shape[1] - 3, width), F32)
        cent = cent_ref[pl.ds(out_order_ref[n], 1), :]
        small_all[n] = jnp.concatenate([lifted, shifted, cent, rest], axis=0).astype(BF)
    finish(
        leaving
        + begin(
            [(small_all.at[n], out_refs[n].at[pl.ds(rows, small_all.shape[1]), :]) for n in range(total)],
            small_sems,
        )
    )


def attend_back(q, k, v, kt, normed, grads, ctx, lse, w, gain, shift, cent, ends, order, out_order, heads, scale):
    total = len(order)
    groups = len(q)
    rows, fw = q[0].shape[1:]
    width = w.shape[0]
    qb, kb = QB, KB
    pairs = total * rows * total * rows * heads
    out = pl.pallas_call(
        functools.partial(attend_back_kernel, heads, scale, total, groups, qb, kb),
        in_specs=[SMEM] * 2 + [VMEM] * 7 + [ANY] * (5 * groups + 1),
        out_specs=[ANY] * total + [VMEM] * 3,
        out_shape=[shape((rows + 16, width), BF)] * total + [shape((total, rows, fw), BF)] * 3,
        scratch_shapes=[
            pltpu.VMEM((total // qb, qb * rows, fw), BF),
            pltpu.VMEM((total // kb, kb * rows, fw), BF),
            pltpu.VMEM((total // kb, kb * rows, fw), BF),
            pltpu.VMEM((total // kb, fw, kb * rows), BF),
            pltpu.VMEM((total // qb, fw, qb * rows), BF),
            pltpu.VMEM((total // qb, heads * qb * rows, fw), BF),
            pltpu.VMEM((total // qb, fw, heads * qb * rows), BF),
            pltpu.VMEM((total // qb, 1, heads * qb * rows), F32),
            pltpu.VMEM((total // qb, fw, qb * rows), F32),
            pltpu.VMEM((total, rows, width), BF),
            pltpu.VMEM((total, rows, width), BF),
            pltpu.VMEM((total, 16, width), BF),
            pltpu.SMEM((total // kb,), jnp.int32),
            pltpu.SemaphoreType.DMA((5 * total,)),
            pltpu.SemaphoreType.DMA((total,)),
            pltpu.SemaphoreType.DMA((total,)),
            pltpu.SemaphoreType.DMA((total,)),
        ],
        cost_estimate=pl.CostEstimate(
            flops=5 * pairs * 128, bytes_accessed=20 * total * rows * fw, transcendentals=pairs // 2
        ),
        name="attend_back",
    )(order, out_order, ends, ctx, lse, w, gain, shift, cent, *q, *k, *v, *kt, *normed, grads)
    return out[:total], out[total], out[total + 1], out[total + 2]


def project_grads_kernel(total, groups, parts, order_ref, dq_ref, dk_ref, dv_ref, *refs):
    normed_in, (out_ref, normed_all, sems) = views(refs[:groups]), refs[groups:]
    rows = dq_ref.shape[1]
    copies = begin(
        [
            (normed_in[n], normed_all.at[pl.ds(pl.multiple_of(order_ref[n] * rows, rows), rows)])
            for n in range(total)
        ],
        sems,
    )
    grads = jnp.concatenate(
        [ref[...].reshape(total * rows, ref.shape[2]) for ref in (dq_ref, dk_ref, dv_ref)], axis=1
    )
    finish(copies)
    step = out_ref.shape[0] // parts
    for n in range(parts):
        out_ref[n * step : (n + 1) * step, :] = lax.dot_general(
            normed_all[:, n * step : (n + 1) * step],
            grads,
            (((0,), (0,)), ((), ())),
            preferred_element_type=F32,
        ).astype(BF)


def project_grads(dq, dk, dv, normed, order, parts):
    total, rows, fw = dq.shape
    width = normed[0].shape[2]
    return pl.pallas_call(
        functools.partial(project_grads_kernel, total, len(normed), parts),
        in_specs=[SMEM] + [VMEM] * 3 + [ANY] * len(normed),
        out_specs=VMEM,
        out_shape=shape((width, 3 * fw), BF),
        scratch_shapes=[pltpu.VMEM((total * rows, width), BF), pltpu.SemaphoreType.DMA((total,))],
        cost_estimate=pl.CostEstimate(
            flops=2 * total * rows * width * 3 * fw,
            bytes_accessed=2 * total * rows * (width + 3 * fw) + 2 * width * 3 * fw,
            transcendentals=0,
        ),
        name="project_grads",
    )(order, dq, dk, dv, *normed)


def output_grads_kernel(ctx_ref, grad_ref, out_ref):
    cols_n, rows_n, part, fw = out_ref.shape
    for n in range(rows_n):
        result = dot(ctx_ref[n * part : (n + 1) * part, :], grad_ref[...]).astype(BF)
        for col in range(cols_n):
            out_ref[col, n] = result[:, col * fw : (col + 1) * fw]


def output_grads(ctx, grad, rows_n, cols_n):
    tok, width = grad.shape
    return pl.pallas_call(
        output_grads_kernel,
        in_specs=[VMEM] * 2,
        out_specs=VMEM,
        out_shape=shape((cols_n, rows_n, width // rows_n, width // cols_n), BF),
        cost_estimate=pl.CostEstimate(
            flops=2 * tok * width * width, bytes_accessed=2 * width * width, transcendentals=0
        ),
        name="output_grads",
    )(ctx, grad)


CHUNK = 512


def gelu_pair(pre_act):
    below = 0.5 * (1.0 + lax.erf(pre_act * 0.7071067811865476))
    bell = jnp.exp(-0.5 * pre_act * pre_act) * 0.3989422804014327
    return pre_act * below, below + pre_act * bell


def weight_copies(sub, w_in, w_back, first, second, sems, between=lambda n: None, turns=(0, 1)):
    count, unused, chunk = first.shape

    def copy(n, which):
        at = pl.ds(pl.multiple_of(n * chunk, chunk), chunk)
        if which == 0:
            return pltpu.make_async_copy(w_in.at[0, sub, :, at], first.at[n], sems.at[2 * n])
        return pltpu.make_async_copy(w_back.at[0, sub, at, :], second.at[n], sems.at[2 * n + 1])

    for n in range(count):
        copy(n, turns[0]).start()
        between(n)
        copy(n, turns[1]).start()
    return copy


def add_to(total, n, more):
    @pl.when(n == 0)
    def begin_sum():
        total[...] = more

    @pl.when(n > 0)
    def add_sum():
        total[...] += more


def piece_pairs(pieces, held, first_lane=0):
    rows = held.shape[0] // len(pieces)
    lanes = pl.ds(first_lane, held.shape[1])
    return [(piece.at[:, lanes], held.at[pl.ds(m * rows, rows), :]) for m, piece in enumerate(pieces)]


def back_pairs(pieces, held):
    rows = held.shape[0] // len(pieces)
    return [(held.at[pl.ds(m * rows, rows), :], piece) for m, piece in enumerate(pieces)]


def spread_pairs(me_ref, whole, held, count):
    rows = held.shape[0] // count
    size = count // 2
    pairs = []
    for m in range(count):
        at = ((me_ref[0] ^ (m % size)) * 2 + m // size) * rows
        pairs.append((whole.at[pl.ds(pl.multiple_of(at, rows), rows), :], held.at[pl.ds(m * rows, rows), :]))
    return pairs


def expert_first_kernel(sub, count, bias_ref, w_in, w_back, *refs):
    pieces, refs = refs[:count], refs[count:]
    outs, refs = refs[:count], refs[count:]
    all_ref, hidden_ref, slope_ref = refs[:3]
    held, first, second, hidden, slope, total, low, sem_w, sem_x, sem_o, sem_r = refs[3:]
    chunks, unused, chunk = first.shape
    arriving = begin(piece_pairs(pieces, held), sem_x)
    weights = weight_copies(sub, w_in, w_back, first, second, sem_w)
    finish(arriving)
    leaving = begin([(held, all_ref)], sem_r.at[pl.ds(0, 1)])
    kept = [(hidden, hidden_ref), (slope, slope_ref)]

    def step(n, unused):
        weights(n, 0).wait()
        value, rise = gelu_pair(dot(held[...], first[n]) + bias_ref[n].astype(F32))
        hidden[n] = value.astype(BF)
        slope[n] = rise
        begin([(h.at[n], o.at[n]) for h, o in kept], sem_r.at[pl.ds(2 * n + 1, 2)])
        weights(n, 1).wait()
        add_to(total, n, dot(hidden[n], second[n]))
        return unused

    lax.fori_loop(0, chunks, step, 0)
    low[...] = total[...].astype(BF)
    leaving += begin(back_pairs(outs, low), sem_o)
    finish(leaving)
    for n in range(chunks):
        finish(copies_of([(h.at[n], o.at[n]) for h, o in kept], sem_r.at[pl.ds(2 * n + 1, 2)]))


def expert_first(pieces, sub, w_in, w_back, bias):
    count = len(pieces)
    rows, width = pieces[0].shape[0] * count, w_in.shape[2]
    ff = w_in.shape[3]
    chunk = min(CHUNK, ff)
    chunks = ff // chunk
    out = pl.pallas_call(
        functools.partial(expert_first_kernel, sub, count),
        in_specs=[VMEM, ANY, ANY] + [ANY] * count,
        out_specs=[ANY] * (count + 3),
        out_shape=[shape((rows // count, width), BF)] * count
        + [
            shape((rows, width), BF),
            shape((chunks, rows, chunk), BF),
            shape((chunks, rows, chunk), F32),
        ],
        scratch_shapes=[
            pltpu.VMEM((rows, width), BF),
            pltpu.VMEM((chunks, width, chunk), BF),
            pltpu.VMEM((chunks, chunk, width), BF),
            pltpu.VMEM((chunks, rows, chunk), BF),
            pltpu.VMEM((chunks, rows, chunk), F32),
            pltpu.VMEM((rows, width), F32),
            pltpu.VMEM((rows, width), BF),
            pltpu.SemaphoreType.DMA((2 * chunks,)),
            pltpu.SemaphoreType.DMA((count,)),
            pltpu.SemaphoreType.DMA((count,)),
            pltpu.SemaphoreType.DMA((2 * chunks + 1,)),
        ],
        cost_estimate=pl.CostEstimate(
            flops=4 * rows * width * ff, bytes_accessed=8 * rows * width, transcendentals=2 * rows * ff
        ),
        name="expert_first",
    )(bias.reshape(chunks, 1, chunk), w_in, w_back, *pieces)
    return out[:count], out[count], out[count + 1], out[count + 2]


def expert_second_kernel(sub, count, bias_ref, w_in, w_back, *refs):
    cot_in, refs = refs[:count], refs[count:]
    pieces, refs = refs[:count], refs[count:]
    gates, refs = refs[:count], refs[count:]
    grad_outs, refs = refs[:count], refs[count:]
    all_ref, grad_all_ref, hidden_ref, pre_ref, bias_out = refs[:5]
    held, cot, gate, held_grad, first, second, hidden, grad_pre, total, low_grad = refs[5:15]
    sem_w, sem_x, sem_c, sem_g, sem_p, sem_r = refs[15:]
    chunks, unused, chunk = first.shape
    arriving = begin(piece_pairs(pieces, held), sem_x)
    width = held.shape[1]
    early = []

    def load_early(n):
        if n == 0:
            early.extend(begin(piece_pairs(cot_in, cot), sem_c))
            early.extend(begin(piece_pairs(gates, gate, width), sem_g))

    weights = weight_copies(sub, w_in, w_back, first, second, sem_w, load_early)
    finish(arriving)
    leaving = begin([(held, all_ref)], sem_r.at[pl.ds(0, 1)])
    scaled = [(held_grad, grad_all_ref)]
    kept = [(hidden, hidden_ref), (grad_pre, pre_ref)]

    def step(n, unused):
        weights(n, 0).wait()
        pre_act = dot(held[...], first[n]) + bias_ref[n].astype(F32)

        @pl.when(n == 0)
        def scale_grads():
            finish(early)
            held_grad[...] = (
                cot[...].astype(F32) * jnp.sum(gate[...].astype(F32), axis=1, keepdims=True)
            ).astype(BF)
            begin(scaled, sem_r.at[pl.ds(1, 1)])

        weights(n, 1).wait()
        grad_hidden = dot(held_grad[...], second[n], NT)
        value, rise = gelu_pair(pre_act)
        hidden[n] = value.astype(BF)
        back = (grad_hidden * rise).astype(BF)
        grad_pre[n] = back
        bias_out[n] = jnp.sum(back.astype(F32), axis=0, keepdims=True)
        begin([(h.at[n], o.at[n]) for h, o in kept], sem_r.at[pl.ds(2 * n + 2, 2)])
        add_to(total, n, dot(grad_pre[n], first[n], NT))
        return unused

    lax.fori_loop(0, chunks, step, 0)
    low_grad[...] = total[...].astype(BF)
    leaving += begin(back_pairs(grad_outs, low_grad), sem_p)

    finish(leaving + copies_of(scaled, sem_r.at[pl.ds(1, 1)]))
    for n in range(chunks):
        finish(copies_of([(h.at[n], o.at[n]) for h, o in kept], sem_r.at[pl.ds(2 * n + 2, 2)]))


def expert_branch_kernel(sub, count, me_ref, hidden_in, w_back, *refs):
    cot_in, (out_ref, logit_ref, hidden, second, cot, total, low, sem_h, sem_w, sem_c, sem_o) = (
        refs[:count],
        refs[count:],
    )
    chunks, unused, chunk = hidden.shape

    def copy(n, which):
        at = pl.ds(pl.multiple_of(n * chunk, chunk), chunk)
        if which == 0:
            return pltpu.make_async_copy(hidden_in.at[n], hidden.at[n], sem_h.at[n])
        return pltpu.make_async_copy(w_back.at[0, sub, at, :], second.at[n], sem_w.at[n])

    for n in range(chunks):
        copy(n, 0).start()
        copy(n, 1).start()
    early = begin(piece_pairs(cot_in, cot), sem_c)

    def step(n, unused):
        copy(n, 0).wait()
        copy(n, 1).wait()
        add_to(total, n, dot(hidden[n], second[n]))
        return unused

    lax.fori_loop(0, chunks, step, 0)
    low[...] = total[...].astype(BF)
    leaving = begin([(h, w) for w, h in spread_pairs(me_ref, out_ref, low, count)], sem_o)
    finish(early)
    logit_ref[...] = scalar_lanes(
        jnp.sum(cot[...].astype(F32) * total[...], axis=1, keepdims=True)
    )
    finish(leaving)


def expert_branch(hidden, cot, sub, w_back, me):
    count = len(cot)
    chunks, rows, chunk = hidden.shape
    width = cot[0].shape[1]
    return pl.pallas_call(
        functools.partial(expert_branch_kernel, sub, count),
        in_specs=[SMEM] + [ANY] * (2 + count),
        out_specs=[ANY, VMEM],
        out_shape=[shape((rows, width), BF), shape((rows, LANES), BF)],
        scratch_shapes=[
            pltpu.VMEM((chunks, rows, chunk), BF),
            pltpu.VMEM((chunks, chunk, width), BF),
            pltpu.VMEM((rows, width), BF),
            pltpu.VMEM((rows, width), F32),
            pltpu.VMEM((rows, width), BF),
            pltpu.SemaphoreType.DMA((chunks,)),
            pltpu.SemaphoreType.DMA((chunks,)),
            pltpu.SemaphoreType.DMA((count,)),
            pltpu.SemaphoreType.DMA((count,)),
        ],
        cost_estimate=pl.CostEstimate(
            flops=2 * rows * width * chunks * chunk, bytes_accessed=8 * rows * width, transcendentals=0
        ),
        name="expert_branch",
    )(me, hidden, w_back, *cot)


def expert_second(pieces, gates, cot, sub, w_in, w_back, bias):
    count = len(pieces)
    rows, width = pieces[0].shape
    rows = rows * count
    ff = w_in.shape[3]
    chunk = min(CHUNK, ff)
    chunks = ff // chunk
    out = pl.pallas_call(
        functools.partial(expert_second_kernel, sub, count),
        in_specs=[VMEM] + [ANY] * (2 + 3 * count),
        out_specs=[ANY] * (count + 4) + [VMEM],
        out_shape=[shape((rows // count, width), BF)] * count
        + [shape((rows, width), BF)] * 2
        + [shape((chunks, rows, chunk), BF)] * 2
        + [shape((chunks, 1, chunk), F32)],
        scratch_shapes=[
            pltpu.VMEM((rows, width), BF),
            pltpu.VMEM((rows, width), BF),
            pltpu.VMEM((rows, LANES), BF),
            pltpu.VMEM((rows, width), BF),
            pltpu.VMEM((chunks, width, chunk), BF),
            pltpu.VMEM((chunks, chunk, width), BF),
            pltpu.VMEM((chunks, rows, chunk), BF),
            pltpu.VMEM((chunks, rows, chunk), BF),
            pltpu.VMEM((rows, width), F32),
            pltpu.VMEM((rows, width), BF),
            pltpu.SemaphoreType.DMA((2 * chunks,)),
            pltpu.SemaphoreType.DMA((count,)),
            pltpu.SemaphoreType.DMA((count,)),
            pltpu.SemaphoreType.DMA((count,)),
            pltpu.SemaphoreType.DMA((count,)),
            pltpu.SemaphoreType.DMA((2 * chunks + 2,)),
        ],
        cost_estimate=pl.CostEstimate(
            flops=6 * rows * width * ff, bytes_accessed=12 * rows * width, transcendentals=2 * rows * ff
        ),
        name="expert_second",
    )(bias.reshape(chunks, 1, chunk), w_in, w_back, *cot, *pieces, *gates)
    return out[:count], *out[count:]


def expert_back_kernel(sub, count, logit_ref, w_in, w_back, slope_in, *refs):
    grads, refs = refs[:count], refs[count:]
    grad_outs, refs = refs[:count], refs[count:]
    grad_all_ref, pre_ref, bias_out = refs[:3]
    held_grad, first, second, slope, grad_pre, total, low_grad = refs[3:10]
    sem_w, sem_s, sem_g, sem_p, sem_r = refs[10:]
    chunks, unused, chunk = first.shape
    arriving_grad = begin(piece_pairs(grads, held_grad), sem_g)
    slopes = lambda n: pltpu.make_async_copy(slope_in.at[n], slope.at[n], sem_s.at[n])
    weights = weight_copies(
        sub, w_in, w_back, first, second, sem_w, lambda n: slopes(n).start(), (1, 0)
    )
    low_grad[:, held_grad.shape[1] :] = logit_ref[...]
    finish(arriving_grad)
    leaving = begin([(held_grad, grad_all_ref)], sem_r.at[pl.ds(0, 1)])

    def step(n, unused):
        weights(n, 1).wait()
        grad_hidden = dot(held_grad[...], second[n], NT)
        slopes(n).wait()
        back = (grad_hidden * slope[n]).astype(BF)
        grad_pre[n] = back
        bias_out[n] = jnp.sum(back.astype(F32), axis=0, keepdims=True)
        begin([(grad_pre.at[n], pre_ref.at[n])], sem_r.at[pl.ds(n + 1, 1)])
        weights(n, 0).wait()
        add_to(total, n, dot(grad_pre[n], first[n], NT))
        return unused

    lax.fori_loop(0, chunks, step, 0)
    low_grad[:, : total.shape[1]] = total[...].astype(BF)
    finish(leaving + begin(back_pairs(grad_outs, low_grad), sem_p))
    for n in range(chunks):
        finish(copies_of([(grad_pre.at[n], pre_ref.at[n])], sem_r.at[pl.ds(n + 1, 1)]))


def expert_back(grads, slope, logit, sub, w_in, w_back):
    count = len(grads)
    rows, width = grads[0].shape
    rows = rows * count
    ff = w_in.shape[3]
    chunk = min(CHUNK, ff)
    chunks = ff // chunk
    out = pl.pallas_call(
        functools.partial(expert_back_kernel, sub, count),
        in_specs=[VMEM] + [ANY] * (3 + count),
        out_specs=[ANY] * (count + 2) + [VMEM],
        out_shape=[shape((rows // count, width + LANES), BF)] * count
        + [shape((rows, width), BF), shape((chunks, rows, chunk), BF), shape((chunks, 1, chunk), F32)],
        scratch_shapes=[
            pltpu.VMEM((rows, width), BF),
            pltpu.VMEM((chunks, width, chunk), BF),
            pltpu.VMEM((chunks, chunk, width), BF),
            pltpu.VMEM((chunks, rows, chunk), F32),
            pltpu.VMEM((chunks, rows, chunk), BF),
            pltpu.VMEM((rows, width), F32),
            pltpu.VMEM((rows, width + LANES), BF),
            pltpu.SemaphoreType.DMA((2 * chunks,)),
            pltpu.SemaphoreType.DMA((chunks,)),
            pltpu.SemaphoreType.DMA((count,)),
            pltpu.SemaphoreType.DMA((count,)),
            pltpu.SemaphoreType.DMA((chunks + 1,)),
        ],
        cost_estimate=pl.CostEstimate(
            flops=4 * rows * width * ff, bytes_accessed=10 * rows * width, transcendentals=0
        ),
        name="expert_back",
    )(logit, w_in, w_back, slope, *grads)
    return out[:count], *out[count:]


def weight_grads_kernel(chunked_left, left_ref, right_ref, *refs):
    out_ref = refs[-1]
    if chunked_left:
        left, right = left_ref[0], right_ref[...]
    else:
        left, right = left_ref[...], right_ref[0]
    out_ref[0, 0] = lax.dot_general(left, right, (((0,), (0,)), ((), ())), preferred_element_type=F32)


def weight_grads(left, right, sub, held, chunked_left):
    chunked, plain = (left, right) if chunked_left else (right, left)
    chunks, rows, chunk = chunked.shape
    width = plain.shape[1]
    pieces = pl.BlockSpec((1, rows, chunk), lambda n: (n, 0, 0))
    whole = pl.BlockSpec((rows, width), lambda n: (0, 0))
    if chunked_left:
        in_specs = [pieces, whole]
        out_spec = pl.BlockSpec((1, 1, chunk, width), lambda n: (0, sub, n, 0))
        dims = (1, 2, chunks * chunk, width)
    else:
        in_specs = [whole, pieces]
        out_spec = pl.BlockSpec((1, 1, width, chunk), lambda n: (0, sub, 0, n))
        dims = (1, 2, width, chunks * chunk)
    more = [] if held is None else [held]
    return pl.pallas_call(
        functools.partial(weight_grads_kernel, chunked_left),
        grid=(chunks,),
        in_specs=in_specs + [ANY] * len(more),
        out_specs=out_spec,
        out_shape=shape(dims, F32),
        input_output_aliases={2: 0} if more else {},
        cost_estimate=pl.CostEstimate(
            flops=2 * rows * width * chunks * chunk,
            bytes_accessed=4 * width * chunks * chunk + 2 * rows * (width + chunks * chunk),
            transcendentals=0,
        ),
        name="weight_grads",
    )(left, right, *more)


def stack_gather(value, axis, size):
    for bit in bits_of(size):
        value = jnp.concatenate([value, send_xor(value, axis, size, 1 << bit)])
    return value


def stack_scatter(value, axis, size):
    for bit in bits_of(size)[::-1]:
        half = value.shape[0] // 2
        value = value[:half] + send_xor(value[half:], axis, size, 1 << bit)
    return value


def together(*values):
    return lax.optimization_barrier(values)


def after(value, *earlier):
    return lax.optimization_barrier((value, *earlier))[0]


def gather_pieces(first, second, axis, size):
    bits = bits_of(size)
    return gather_path(first, axis, size, bits) + gather_path(second, axis, size, bits[::-1])


def scatter_pieces(pieces, axis, size):
    bits = bits_of(size)
    return scatter_path(pieces[:size], axis, size, bits) + scatter_path(
        pieces[size:], axis, size, bits[::-1]
    )


def shards(
    tokens,
    block_ids,
    expert_ids,
    cotangent,
    norm_gain,
    norm_shift,
    w_query,
    w_key,
    w_value,
    w_output,
    centroids,
    expert_gain,
    expert_shift,
    w_in,
    b_in,
    w_back,
    b_back,
):
    rows_n = lax.axis_size("row")
    cols_n = lax.axis_size("col")
    r = lax.axis_index("row")
    c = lax.axis_index("col")
    me = jnp.stack([r, c]).astype(jnp.int32)
    tok, width = tokens.shape
    fw = width // cols_n
    heads = HEADS // cols_n
    scale = float(width // HEADS) ** (-0.5)
    part = width // rows_n
    own = norm_gain.shape[0]
    slot = tok // cols_n

    count = 2 * own + part
    small_experts = jnp.concatenate([expert_gain[0], expert_shift[0], b_back[0]]).reshape(-1)
    more = 16 * -(-small_experts.shape[0] // (64 * fw))
    small_experts = jnp.pad(small_experts, (0, more * 4 * fw - small_experts.shape[0]))
    w_cat = jnp.concatenate(
        [
            jnp.concatenate([w_query, w_key, w_value, w_output], axis=1),
            small_experts.reshape(more, 4 * fw),
        ]
    )
    out_order = jnp.stack(col_order(c, cols_n)).astype(jnp.int32)

    def gather_tiles(value):
        return lax.all_gather(value, "col", axis=0, tiled=True).reshape(cols_n, rows_n, part, fw)

    def matrix_sums(part_qkv, part_output):
        parts = jnp.concatenate([part_qkv, part_output], axis=1).reshape(rows_n, part, 4 * fw)
        parts = reorder(parts, r, rows_n)
        return direct_exchange([parts[m] for m in range(rows_n)], "row", rows_n)

    def exchange(rows):
        return lax.all_to_all(
            rows.reshape(cols_n, -1, rows.shape[-1]), "col", split_axis=0, concat_axis=0, tiled=True
        ).reshape(rows.shape)

    onehot = expert_ids[:, None] == jnp.arange(LANES, dtype=jnp.int32)[None, :]
    onehot_low = onehot.astype(BF)
    below = (jnp.arange(tok)[:, None] > jnp.arange(tok)[None, :]).astype(BF)
    before = dot(below, onehot_low)
    rank = jnp.sum(jnp.where(onehot, before, 0.0), axis=1).astype(jnp.int32)
    place = expert_ids * slot + rank
    route = (jnp.arange(tok, dtype=jnp.int32)[:, None] == place[None, :]).astype(BF)
    unroute = (place[:, None] == jnp.arange(tok, dtype=jnp.int32)[None, :]).astype(BF)
    moved_cot = dot(route, cotangent).astype(BF)

    small = jnp.concatenate([norm_gain, norm_shift, centroids[0], block_ids[0].astype(BF)])[None]

    def small_params(small):
        small = small.reshape(cols_n, rows_n, count + tok)
        small = reorder(small.transpose(1, 0, 2), r, rows_n).transpose(1, 0, 2)
        gain, shift = [
            small[:, :, n * own : (n + 1) * own].transpose(1, 0, 2).reshape(1, width).astype(F32)
            for n in range(2)
        ]
        cents = small[:, :, 2 * own : count].reshape(cols_n, width)
        ids = lax.dynamic_index_in_dim(small[:, :, count:], r, 1, keepdims=False)
        return gain, shift, jnp.pad(cents, ((0, LANES - cols_n), (0, 0))), ids.astype(F32)

    if cols_n == 8:
        chips = cols_n // 2
        z, core = c // 2, c % 2
        move_right = lambda v, s: lax.ppermute(v, "col", right_pairs(s - 1, chips - 2, cols_n))
        move_left = lambda v, s: lax.ppermute(v, "col", left_pairs(1, chips - s, cols_n))
        swap = lambda v: swap_core(v, cols_n)
        right_1, left_1 = move_right(tokens, 1), move_left(tokens, 1)
        tokens_s, small_s = swap(tokens), swap(small)
        right_1, left_1, tokens_s, small_s = together(right_1, left_1, tokens_s, small_s)
        right_2, left_2 = move_right(right_1, 2), move_left(left_1, 2)
        near = jnp.where(z < 2, left_1, right_1)
        near_s = swap(near)
        small = jnp.concatenate(direct_gather(jnp.stack([small, small_s]), "row", rows_n), axis=1)
        from_z = [
            z,
            jnp.where(z % 2 == 0, 1, 2),
            jnp.where(z < 2, jnp.where(z == 0, 2, 0), jnp.where(z == 2, 3, 1)),
            jnp.where(z < 2, 3, 0),
        ]
        order = jnp.stack([at * 2 + (core ^ n) for at in from_z for n in range(2)]).astype(jnp.int32)
        right_2, left_2, near, near_s, small, order, out_order, me = together(
            right_2, left_2, near, near_s, small, order, out_order, me
        )
        right_3, left_3 = move_right(right_2, 3), move_left(left_2, 3)
        middle = jnp.where(
            z < 2, jnp.where(z == 0, left_2, right_1), jnp.where(z == 2, left_1, right_2)
        )
        middle_s = swap(middle)
        small = [small] + [send_xor(small, "col", cols_n, 2 * m) for m in range(1, chips)]
        w_pieces = direct_gather(after(w_cat, right_2), "row", rows_n)
        joined = together(
            right_3, left_3, middle, middle_s, onehot_low, route, unroute, moved_cot, *small, *w_pieces
        )
        right_3, left_3, middle, middle_s, onehot_low, route, unroute, moved_cot = joined[:8]
        small, w_pieces = joined[8 : 8 + chips], joined[8 + chips :]
        far = jnp.where(z < 2, jnp.where(z == 0, left_3, left_2), jnp.where(z == 2, right_2, right_3))
        far_s = swap(far)
        w_cat, tile_rows_own, small_experts = arrange_rows(w_pieces, part, (3 * fw, fw), me)
        small = reorder(reorder(jnp.stack(small), z, chips).transpose(1, 0, 2, 3), core, 2)
        gain_attn, shift_attn, full_centroids, ids = small_params(small.transpose(1, 0, 2, 3))
        tiles = gather_tiles(after(tile_rows_own, far))
        cot_own = exchange(after(moved_cot, far_s))
        projected = project(
            [tokens, tokens_s, near, near_s, middle, middle_s, far, far_s],
            gain_attn, shift_attn, w_cat, scale,
        )
        projected = [(p,) for p in projected]
    else:
        small = jnp.concatenate(direct_gather(small, "row", rows_n))
        small = lax.all_gather(small, "col", axis=0, tiled=True)
        gain_attn, shift_attn, full_centroids, ids = small_params(small)
        w_pieces = direct_gather(w_cat, "row", rows_n)
        cot_own = exchange(moved_cot)
        w_cat, tile_rows_own, small_experts = arrange_rows(w_pieces, part, (3 * fw, fw), me)
        tiles = gather_tiles(tile_rows_own)
        order = out_order
        blocks = col_gather(tokens, cols_n)
        projected = [(p,) for p in project(blocks, gain_attn, shift_attn, w_cat, scale)]
    normed, q, k, v, kt, vt = projected

    ctx_low, ctx, lse, ends = attend(q, k, vt, ids, order, heads, me)
    cot_own, small_experts, *ctx_low = together(cot_own, small_experts, *ctx_low)
    bits = bits_of(rows_n)
    near_cot = {
        half: gather_path(cot_own[half * tok // 2 : (half + 1) * tok // 2], "row", rows_n, [bit])
        for half, bit in ((0, bits[0]), (1, bits[-1]))
    }
    ctx_low = direct_exchange(ctx_low, "col", cols_n)
    rest = together(*ctx_low, *near_cot[0], *near_cot[1])
    ctx_low, near_cot = rest[:cols_n], {0: rest[cols_n : cols_n + 2], 1: rest[cols_n + 2 :]}
    cot_pieces = gather_path(near_cot[0], "row", rows_n, bits[1:], [bits[0]]) + gather_path(
        near_cot[1], "row", rows_n, bits[::-1][1:], [bits[-1]]
    )
    experts = small_experts.reshape(rows_n, -1)[:, : 6 * part].reshape(rows_n, 6, part)
    experts = experts.transpose(1, 0, 2).reshape(6, width).astype(F32)
    moved, ctx_low, residual, gate = forward_rows(
        ctx_low, tiles, tokens, full_centroids, onehot_low, route, me
    )

    rest = together(*direct_exchange(moved, "col", cols_n), *cot_pieces)
    arrived, cot_pieces = rest[:cols_n], rest[cols_n:]
    stream_0, grad_2, half_1, half_2 = enter_expert(arrived, experts, cot_own, me)
    wide_pieces = gather_pieces(half_1, half_2, "row", rows_n)
    partial, normed_all_0, hidden_0, slope_0 = expert_first(wide_pieces, 0, w_in, w_back, b_in[0, 0])
    stream_1, half_1, half_2 = between_experts(
        experts, stream_0, scatter_pieces(partial, "row", rows_n)
    )
    pieces = gather_pieces(half_1, half_2, "row", rows_n)
    partial, normed_all_1, grad_all_1, hidden_1, grad_pre_1, bias_1 = expert_second(
        pieces, wide_pieces, cot_pieces, 1, w_in, w_back, b_in[0, 1]
    )
    sums = scatter_pieces(partial, "row", rows_n)
    branch, logit = expert_branch(hidden_1, cot_pieces, 1, w_back, me)
    branch, logit, *sums = together(branch, logit, *sums)
    grad_1, half_1, half_2, sums_1 = middle_back(experts, stream_1, grad_2, sums)
    pieces = gather_pieces(half_1, half_2, "row", rows_n)
    w_back_grad = weight_grads(hidden_1, after(grad_all_1, grad_1), 1, None, True)
    w_back_grad, *pieces = together(w_back_grad, *pieces)
    partial, grad_all_0, grad_pre_0, bias_0 = expert_back(pieces, slope_0, logit, 0, w_in, w_back)
    sums = together(*scatter_pieces(partial, "row", rows_n))
    branch = lax.psum_scatter(after(branch, sums[0]), "row", scatter_dimension=0, tiled=True)
    *leaving, sums_0 = leave_back(experts, stream_0, grad_1, cot_own, stream_1, sums, me, cols_n)
    returned = direct_exchange(leaving, "col", cols_n)
    w_in_grad = weight_grads(normed_all_0, after(grad_pre_0, sums_0), 0, None, False)
    w_in_grad, *returned = together(w_in_grad, *returned)
    grad_residual, grad_attended, part_cent, grad_ctx = backward_rows(
        returned, tiles, unroute, cotangent, full_centroids, onehot_low, gate, residual, me
    )

    grad_ctx = exchange(grad_ctx)
    part_output = output_grads(ctx_low, grad_attended, rows_n, cols_n)
    w_back_grad = weight_grads(hidden_0, after(grad_all_0, grad_attended), 0, w_back_grad, True)
    expert_low = finish_rows(stream_1, branch, experts)
    part_output, w_back_grad, expert_low, grad_ctx = together(
        part_output, w_back_grad, expert_low, grad_ctx
    )
    expert_low = exchange(expert_low)
    part_output = lax.psum_scatter(
        part_output.reshape(cols_n * width, fw), "col", scatter_dimension=0, tiled=True
    )
    partial, dq, dk, dv = attend_back(
        q, k, v, kt, normed, grad_ctx.reshape(cols_n, fw, tok), ctx, lse, w_cat, gain_attn, shift_attn,
        part_cent, ends, order, out_order, heads, scale,
    )
    dq, expert_low, *partial = together(dq, expert_low, *partial)
    if cols_n == 8:
        halves = [
            add_low(partial[2 * turn], swap(partial[2 * turn + 1])) for turn in range(chips)
        ]
        into_right = lambda v, s: lax.ppermute(
            v, "col", right_pairs(0, min(s - 1, chips - 2), cols_n)
        )
        into_left = lambda v, s: lax.ppermute(
            v, "col", left_pairs(max(chips - s, 1), chips - 1, cols_n)
        )
        from_left, from_right = into_right(halves[3], 1), into_left(halves[1], 1)
        part_qkv = project_grads(after(dq, halves[3]), dk, dv, normed, order, rows_n)
        from_left, from_right, part_qkv, part_output = together(
            from_left, from_right, part_qkv, part_output
        )
        from_left = into_right(add_low(from_left, halves[2]), 2)
        from_right = into_left(add_low(from_right, halves[2]), 2)
        output = (residual + gate * dot(unroute, expert_low)).astype(BF)
        grad_sums = matrix_sums(part_qkv, part_output)
        from_left, from_right, output, *grad_sums = together(from_left, from_right, output, *grad_sums)
        normed_all_1, from_left, from_right = together(normed_all_1, from_left, from_right)
        from_left = into_right(add_low(from_left, halves[1]), 3)
        from_right = into_left(add_low(from_right, halves[3]), 3)
        w_in_grad = weight_grads(normed_all_1, grad_pre_1, 1, w_in_grad, False)
        from_left, from_right, w_in_grad = together(from_left, from_right, w_in_grad)
        summed = halves[0].astype(F32) + from_left.astype(F32) + from_right.astype(F32)
    else:
        part_qkv = project_grads(dq, dk, dv, normed, order, rows_n)
        output = (residual + gate * dot(unroute, expert_low)).astype(BF)
        grad_sums = matrix_sums(part_qkv, part_output)
        w_in_grad = weight_grads(normed_all_1, grad_pre_1, 1, w_in_grad, False)
        summed = col_scatter(partial, cols_n)
    grad_matrices = sum(v.astype(F32) for v in grad_sums)
    grad_qkv, grad_output = grad_matrices[:, : 3 * fw], grad_matrices[:, 3 * fw :]
    grad_normed_attn = summed[:tok]

    norm_rows = summed[tok : tok + 2].reshape(2, rows_n, cols_n, own)
    norm_rows = lax.dynamic_index_in_dim(norm_rows, c, 2, keepdims=False).transpose(1, 0, 2)
    expert_rows = jnp.concatenate([sums_0, sums_1]).reshape(6, rows_n, part).transpose(1, 0, 2)
    packed = jnp.concatenate(
        [
            norm_rows.reshape(rows_n, 2 * own),
            summed[tok + 2].reshape(rows_n, part),
            expert_rows.reshape(rows_n, 6 * part),
        ],
        axis=1,
    )[:, None]
    packed = reorder(packed, r, rows_n)
    packed = sum(direct_exchange([packed[m] for m in range(rows_n)], "row", rows_n))[0]
    expert_sums = packed[count:].reshape(2, 3, part).transpose(1, 0, 2)

    inputs = tokens.astype(F32)
    unit_attn, inv_attn = layer_stats(inputs)
    tokens_grad = grad_residual + norm_back(grad_normed_attn, unit_attn, inv_attn, gain_attn)
    return (
        output,
        tokens_grad,
        packed[:own],
        packed[own : 2 * own],
        grad_qkv[:, :fw],
        grad_qkv[:, fw : 2 * fw],
        grad_qkv[:, 2 * fw :],
        grad_output,
        packed[None, 2 * own : count],
        expert_sums[None, 0],
        expert_sums[None, 1],
        w_in_grad,
        jnp.stack([bias_0.reshape(-1), bias_1.reshape(-1)])[None],
        w_back_grad,
        expert_sums[None, 2],
    )


def solution(mesh):
    placed = (
        P(("row", "col"), None),
        P("row", "col"),
        P(("row", "col")),
        P(("row", "col"), None),
        P(("row", "col")),
        P(("row", "col")),
        P("row", "col"),
        P("row", "col"),
        P("row", "col"),
        P("row", "col"),
        P("col", "row"),
        P("col", None, "row"),
        P("col", None, "row"),
        P("col", None, None, "row"),
        P("col", None, "row"),
        P("col", None, "row", None),
        P("col", None, "row"),
    )
    return jax.shard_map(
        shards,
        mesh=mesh,
        in_specs=placed,
        out_specs=(
            P(("row", "col"), None),
            P(("row", "col"), None),
            P(("row", "col")),
            P(("row", "col")),
            P("row", "col"),
            P("row", "col"),
            P("row", "col"),
            P("row", "col"),
            P("col", "row"),
            P("col", None, "row"),
            P("col", None, "row"),
            P("col", None, None, "row"),
            P("col", None, "row"),
            P("col", None, "row", None),
            P("col", None, "row"),
        ),
        check_vma=False,
    )
```

```python
import functools

import jax
import jax.numpy as jnp
from jax import lax
from jax.experimental import pallas as pl
from jax.experimental.pallas import tpu as pltpu
from jax.sharding import PartitionSpec as P

HEADS = 16
EPS = 1e-05
NEG = -1e30
BF = jnp.bfloat16
F32 = jnp.float32
NT = (((1,), (1,)), ((), ()))
NN = (((1,), (0,)), ((), ()))
LANES = 128


def dot(left, right, dims=NN):
    return lax.dot_general(left, right, dims, preferred_element_type=F32)


def add_low(left, right):
    return (left.astype(F32) + right.astype(F32)).astype(BF)


def send_xor(value, axis, size, mask):
    return lax.ppermute(value, axis, [(i, i ^ mask) for i in range(size)])


def bits_of(size):
    return list(range(size.bit_length() - 1))


def gather_path(values, axis, size, bits, done=()):
    if not done:
        values = [values]
    held = dict(zip([0] + [1 << bit for bit in done], values))
    for bit in bits:
        held.update({m | (1 << bit): send_xor(v, axis, size, 1 << bit) for m, v in list(held.items())})
    return [held[m] for m in sorted(held)]


def scatter_path(blocks, axis, size, bits):
    held = {m: [v] for m, v in enumerate(blocks)}
    for bit in bits:
        leaving = {m: v for m, v in held.items() if (m >> bit) & 1}
        held = {m: v for m, v in held.items() if not (m >> bit) & 1}
        for m, v in leaving.items():
            total = v[0] if len(v) == 1 else sum(n.astype(F32) for n in v).astype(BF)
            held[m & ~(1 << bit)].append(send_xor(total, axis, size, 1 << bit))
    return held[0]


def direct_gather(value, axis, size):
    return [value] + [send_xor(value, axis, size, m) for m in range(1, size)]


def direct_exchange(blocks, axis, size):
    return [blocks[0]] + [send_xor(blocks[m], axis, size, m) for m in range(1, size)]


def reorder(stacked, mine, size):
    return jnp.concatenate(
        [lax.dynamic_index_in_dim(stacked, mine ^ j, 0, keepdims=True) for j in range(size)]
    )


def swap_core(value, size):
    return send_xor(value, "col", size, 1)


def right_pairs(first, last, size):
    return [(i, i + 2) for i in range(size) if first <= i // 2 <= last]


def left_pairs(first, last, size):
    return [(i, i - 2) for i in range(size) if first <= i // 2 <= last]


def line_order(mine, size):
    chips = size // 2
    return [
        ((mine // 2 + turn) % chips) * 2 + ((mine % 2) ^ core)
        for turn in range(chips)
        for core in range(2)
    ]


def col_order(mine, size):
    return line_order(mine, size) if size == 8 else [mine ^ m for m in range(size)]


def col_gather(value, size):
    return gather_path(value, "col", size, bits_of(size))


def col_scatter(blocks, size):
    return sum(v.astype(F32) for v in scatter_path(blocks, "col", size, bits_of(size)))


def layer_stats(stream):
    center = stream - jnp.mean(stream, axis=-1, keepdims=True)
    inv_root = lax.rsqrt(jnp.mean(center * center, axis=-1, keepdims=True) + EPS)
    return (center * inv_root, inv_root)


def norm_back(grad_normed, unit_rows, inv_root, gain_full):
    grad_unit = grad_normed * gain_full
    mean_first = jnp.mean(grad_unit, axis=-1, keepdims=True)
    mean_second = jnp.mean(grad_unit * unit_rows, axis=-1, keepdims=True)
    return inv_root * (grad_unit - mean_first - unit_rows * mean_second)


ANY = pl.BlockSpec(memory_space=pl.ANY)
HBM = pl.BlockSpec(memory_space=pltpu.HBM)
VMEM = pl.BlockSpec(memory_space=pltpu.VMEM)
SMEM = pl.BlockSpec(memory_space=pltpu.SMEM)


def shape(dims, kind):
    return jax.ShapeDtypeStruct(dims, kind)


def params(mib):
    return pltpu.CompilerParams(vmem_limit_bytes=mib * 1024 * 1024)


def copies_of(pairs, sems):
    return [pltpu.make_async_copy(s, d, sems.at[n]) for n, (s, d) in enumerate(pairs)]


def begin(pairs, sems):
    copies = copies_of(pairs, sems)
    for copy in copies:
        copy.start()
    return copies


def finish(copies):
    for copy in copies:
        copy.wait()


def arrange_kernel(count, me_ref, *refs):
    outs, rest = refs[count:-1], refs[-1]
    rows = outs[0].shape[0] // count
    for m in range(count):
        owner = me_ref[0] ^ m
        at = pl.ds(pl.multiple_of(owner * rows, rows), rows)
        done = 0
        for out in outs:
            out[at, :] = refs[m][:rows, done : done + out.shape[1]]
            done += out.shape[1]
        rest[owner] = refs[m][rows:, :]


def arrange_rows(pieces, rows, widths, me):
    count = len(pieces)
    kind = pieces[0].dtype
    return pl.pallas_call(
        functools.partial(arrange_kernel, count),
        in_specs=[SMEM] + [VMEM] * count,
        out_specs=[VMEM] * (len(widths) + 1),
        out_shape=[shape((count * rows, w), kind) for w in widths]
        + [shape((count, pieces[0].shape[0] - rows, pieces[0].shape[1]), kind)],
        name="arrange_rows",
    )(me, *pieces)


def tile_rows(tiles_ref, block):
    return jnp.concatenate([tiles_ref[col, block] for col in range(tiles_ref.shape[0])], axis=1)


def scalar_lanes(values):
    high = values.astype(BF).astype(F32)
    lane = lax.broadcasted_iota(jnp.int32, (values.shape[0], LANES), 1)
    return jnp.where(lane == 0, high, jnp.where(lane == 1, values - high, 0.0)).astype(BF)


def forward_kernel(total, me_ref, tiles_ref, tokens_ref, cent_ref, onehot_ref, route_ref, *refs):
    pieces, refs = refs[:total], refs[total:]
    moved, (ctx_ref, residual_ref, gate_ref, sent) = refs[:total], refs[total:]
    unused, rows_n, part, unused = tiles_ref.shape
    place_pieces(pieces, me_ref, ctx_ref)
    held = tokens_ref[...].astype(F32)
    for n in range(rows_n):
        held = held + lax.dot_general(
            ctx_ref[n * part : (n + 1) * part, :],
            tile_rows(tiles_ref, n),
            (((0,), (0,)), ((), ())),
            preferred_element_type=F32,
        )
    residual_ref[...] = held
    shared = held.astype(BF)
    cent_rows = dot(onehot_ref[...], cent_ref[...])
    gate = jax.nn.sigmoid(jnp.sum(shared.astype(F32) * cent_rows, axis=1, keepdims=True))
    gate_ref[...] = gate
    leaving = jnp.concatenate([shared, scalar_lanes(gate)], axis=1)
    sent[...] = dot(route_ref[...], leaving).astype(BF)
    slot = moved[0].shape[0]
    for m in range(total):
        moved[m][...] = sent[pl.ds(pl.multiple_of((me_ref[1] ^ m) * slot, slot), slot), :]


def forward_rows(pieces, tiles, tokens, cent, onehot, route, me):
    total = len(pieces)
    tok, width = tokens.shape
    out = pl.pallas_call(
        functools.partial(forward_kernel, total),
        in_specs=[SMEM] + [VMEM] * (5 + total),
        out_specs=[VMEM] * (total + 3),
        out_shape=[shape((tok // total, width + LANES), BF)] * total
        + [shape((width, tok), BF), shape((tok, width), F32), shape((tok, 1), F32)],
        scratch_shapes=[pltpu.VMEM((tok, width + LANES), BF)],
        cost_estimate=pl.CostEstimate(
            flops=3 * tok * width * width, bytes_accessed=2 * width * width + 8 * tok * width, transcendentals=0
        ),
        name="forward_rows",
    )(me, tiles, tokens, cent, onehot, route, *pieces)
    return out[:total], *out[total:]


def enter_kernel(total, me_ref, experts_ref, cot_ref, *refs):
    pieces, (stream_ref, grad_ref, first_ref, second_ref, rows_ref) = refs[:total], refs[total:]
    width = stream_ref.shape[1]
    half = first_ref.shape[0]
    place_pieces(pieces, me_ref, rows_ref)
    stream = rows_ref[:, :width]
    lanes = rows_ref[:, width:]
    gate = jnp.sum(lanes.astype(F32), axis=1, keepdims=True)
    stream_ref[...] = stream
    unit_rows, unused = layer_stats(stream.astype(F32))
    normed = (unit_rows * experts_ref[0:1] + experts_ref[2:3]).astype(BF)
    first_ref[:, :width] = normed[:half]
    first_ref[:, width:] = lanes[:half]
    second_ref[:, :width] = normed[half:]
    second_ref[:, width:] = lanes[half:]
    grad_ref[...] = (cot_ref[...].astype(F32) * gate).astype(BF)


def enter_expert(pieces, experts, cot, me):
    total = len(pieces)
    tok, width = cot.shape
    wide = (tok // 2, width + LANES)
    return pl.pallas_call(
        functools.partial(enter_kernel, total),
        in_specs=[SMEM] + [VMEM] * (2 + total),
        out_specs=[VMEM] * 4,
        out_shape=[shape((tok, width), BF)] * 2 + [shape(wide, BF)] * 2,
        scratch_shapes=[pltpu.VMEM((tok, width + LANES), BF)],
        cost_estimate=pl.CostEstimate(flops=20 * tok * width, bytes_accessed=10 * tok * width, transcendentals=0),
        name="enter_expert",
    )(me, experts, cot, *pieces)


def add_up(refs, lanes):
    return sum(ref[:, lanes].astype(F32) for ref in refs)


def halves_of(refs):
    return refs[: len(refs) // 2], refs[len(refs) // 2 :]


def between_kernel(experts_ref, stream_ref, *refs):
    sums, (out_ref, first_ref, second_ref) = refs[:-3], refs[-3:]
    half = first_ref.shape[0]
    for n, (parts, low) in enumerate(zip(halves_of(sums), (first_ref, second_ref))):
        at = slice(n * half, (n + 1) * half)
        stream = stream_ref[at, :].astype(F32) + add_up(parts, slice(None)) + experts_ref[4:5]
        out_ref[at, :] = stream
        unit_rows, unused = layer_stats(stream)
        low[...] = (unit_rows * experts_ref[1:2] + experts_ref[3:4]).astype(BF)


def between_experts(experts, stream, sums):
    tok, width = stream.shape
    return pl.pallas_call(
        between_kernel,
        in_specs=[VMEM] * (2 + len(sums)),
        out_specs=[VMEM] * 3,
        out_shape=[shape((tok, width), F32)] + [shape((tok // 2, width), BF)] * 2,
        cost_estimate=pl.CostEstimate(flops=20 * tok * width, bytes_accessed=12 * tok * width, transcendentals=0),
        compiler_params=params(20),
        name="between_experts",
    )(experts, stream, *sums)


def norm_grads(half, sub, experts_ref, stream_ref, upper_ref, sums, sums_ref):
    width = stream_ref.shape[1]
    grads = []
    for n, parts in enumerate(halves_of(sums)):
        at = slice(n * half, (n + 1) * half)
        grad_normed = add_up(parts, slice(0, width))
        unit_rows, inv_root = layer_stats(stream_ref[at, :].astype(F32))
        upper = upper_ref[at, :].astype(F32)
        for row, values in enumerate((grad_normed * unit_rows, grad_normed, upper)):
            total = jnp.sum(values, axis=0, keepdims=True)
            if n == 0:
                sums_ref[row : row + 1, :] = total
            else:
                sums_ref[row : row + 1, :] += total
        grads.append(upper + norm_back(grad_normed, unit_rows, inv_root, experts_ref[sub : sub + 1]))
    return grads


def middle_back_kernel(experts_ref, stream_ref, upper_ref, *refs):
    sums, (out_ref, first_ref, second_ref, sums_ref) = refs[:-4], refs[-4:]
    half = first_ref.shape[0]
    grads = norm_grads(half, 1, experts_ref, stream_ref, upper_ref, sums, sums_ref)
    for n, low in enumerate((first_ref, second_ref)):
        out_ref[n * half : (n + 1) * half, :] = grads[n]
        low[...] = grads[n].astype(BF)


def middle_back(experts, stream, upper, sums):
    tok, width = stream.shape
    return pl.pallas_call(
        middle_back_kernel,
        in_specs=[VMEM] * (3 + len(sums)),
        out_specs=[VMEM] * 4,
        out_shape=[shape((tok, width), F32)] + [shape((tok // 2, width), BF)] * 2 + [shape((3, width), F32)],
        cost_estimate=pl.CostEstimate(flops=40 * tok * width, bytes_accessed=16 * tok * width, transcendentals=0),
        name="middle_back",
    )(experts, stream, upper, *sums)


def leave_back_kernel(total, me_ref, experts_ref, stream_ref, upper_ref, cot_ref, later_ref, *refs):
    sums, refs = refs[: -total - 2], refs[-total - 2 :]
    outs, sums_ref, held = refs[:total], refs[total], refs[total + 1]
    width = stream_ref.shape[1]
    slot = outs[0].shape[0]
    half = stream_ref.shape[0] // 2
    grads = norm_grads(half, 0, experts_ref, stream_ref, upper_ref, sums, sums_ref)
    for n, parts in enumerate(halves_of(sums)):
        at = slice(n * half, (n + 1) * half)
        kept = cot_ref[at, :].astype(F32) * (later_ref[at, :] + experts_ref[5:6])
        logit = jnp.sum(add_up(parts, slice(width, None)), axis=1, keepdims=True)
        logit = logit + jnp.sum(kept, axis=1, keepdims=True)
        held[at, :width] = grads[n].astype(BF)
        held[at, width:] = scalar_lanes(logit)
    for m in range(total):
        outs[m][...] = held[pl.ds(pl.multiple_of((me_ref[1] ^ m) * slot, slot), slot), :]


def leave_back(experts, stream, upper, cot, later, sums, me, total):
    tok, width = stream.shape
    return pl.pallas_call(
        functools.partial(leave_back_kernel, total),
        in_specs=[SMEM] + [VMEM] * (5 + len(sums)),
        out_specs=[VMEM] * (total + 1),
        out_shape=[shape((tok // total, width + LANES), BF)] * total + [shape((3, width), F32)],
        scratch_shapes=[pltpu.VMEM((tok, width + LANES), BF)],
        cost_estimate=pl.CostEstimate(flops=40 * tok * width, bytes_accessed=20 * tok * width, transcendentals=0),
        name="leave_back",
    )(me, experts, stream, upper, cot, later, *sums)


def place_pieces(pieces, me_ref, held):
    rows = pieces[0].shape[0]
    for m, piece in enumerate(pieces):
        held[pl.ds(pl.multiple_of((me_ref[1] ^ m) * rows, rows), rows), :] = piece[...]


def backward_kernel(total, me_ref, tiles_ref, unroute_ref, cot_ref, cent_ref, onehot_ref, gate_ref, residual_ref, *refs):
    pieces, (out_ref, low_ref, cent_out, ctx_ref, back_ref) = refs[:total], refs[total:]
    place_pieces(pieces, me_ref, back_ref)
    width = cot_ref.shape[1]
    unused, rows_n, part, unused = tiles_ref.shape
    back = dot(unroute_ref[...], back_ref[...])
    gate = gate_ref[...]
    grad_logit = jnp.sum(back[:, width:], axis=1, keepdims=True) * gate * (1.0 - gate)
    cent_rows = dot(onehot_ref[...], cent_ref[...])
    grad = cot_ref[...].astype(F32) + (back[:, :width] + grad_logit * cent_rows)
    out_ref[...] = grad
    low = grad.astype(BF)
    low_ref[...] = low
    for n in range(rows_n):
        ctx_ref[n * part : (n + 1) * part, :] = dot(tile_rows(tiles_ref, n), low, NT).astype(BF)
    cent_out[...] = lax.dot_general(
        onehot_ref[...].astype(F32),
        grad_logit * residual_ref[...].astype(BF).astype(F32),
        (((0,), (0,)), ((), ())),
        precision=lax.Precision.HIGHEST,
        preferred_element_type=F32,
    )


def backward_rows(pieces, tiles, unroute, cot, cent, onehot, gate, residual, me):
    tok, width = cot.shape
    total = len(pieces)
    return pl.pallas_call(
        functools.partial(backward_kernel, total),
        in_specs=[SMEM] + [VMEM] * (7 + total),
        out_specs=[VMEM] * 4,
        out_shape=[
            shape((tok, width), F32),
            shape((tok, width), BF),
            shape((LANES, width), F32),
            shape((width, tok), BF),
        ],
        scratch_shapes=[pltpu.VMEM((tok, width + LANES), BF)],
        cost_estimate=pl.CostEstimate(
            flops=3 * tok * width * width, bytes_accessed=2 * width * width + 12 * tok * width, transcendentals=0
        ),
        name="backward_rows",
    )(me, tiles, unroute, cot, cent, onehot, gate, residual, *pieces)


def finish_kernel(stream_ref, branch_ref, experts_ref, out_ref):
    out_ref[...] = (stream_ref[...] + branch_ref[...].astype(F32) + experts_ref[5:6]).astype(BF)


def finish_rows(stream, branch, experts):
    return pl.pallas_call(
        finish_kernel,
        in_specs=[VMEM] * 3,
        out_specs=VMEM,
        out_shape=shape(stream.shape, BF),
        name="finish_rows",
    )(stream, branch, experts)


def project_kernel(scale, count, gain_ref, shift_ref, w_ref, *refs):
    blocks, outs, refs = refs[:count], refs[count : count + 6], refs[count + 6 :]
    x_all, held, sems, out_sems = refs[0], refs[1:7], refs[7], refs[8]
    fw = w_ref.shape[1] // 3
    begin([(b, x_all.at[n]) for n, b in enumerate(blocks)], sems)

    def leaving(n):
        return copies_of([(h.at[n], o.at[n]) for h, o in zip(held, outs)], out_sems.at[pl.ds(6 * n, 6)])

    def one(n, unused):
        pltpu.make_async_copy(blocks[0], x_all.at[n], sems.at[n]).wait()
        unit_rows, unused_root = layer_stats(x_all[n].astype(F32))
        normed = (unit_rows * gain_ref[...] + shift_ref[...]).astype(BF)
        held[0][n] = normed
        out = dot(normed, w_ref[...])
        keys = out[:, fw : 2 * fw]
        values = out[:, 2 * fw :]
        held[1][n] = (out[:, :fw].astype(BF).astype(F32) * scale).astype(BF)
        held[2][n] = keys.astype(BF)
        held[3][n] = values.astype(BF)
        held[4][n] = keys.T.astype(BF)
        held[5][n] = values.T.astype(BF)
        for copy in leaving(n):
            copy.start()
        return unused

    lax.fori_loop(0, count, one, 0)
    for n in range(count):
        finish(leaving(n))


def project(blocks, gain, shift, w, scale):
    count = len(blocks)
    rows, width = blocks[0].shape
    fw = w.shape[1] // 3
    kinds = [(count, rows, width)] + [(count, rows, fw)] * 3 + [(count, fw, rows)] * 2
    return pl.pallas_call(
        functools.partial(project_kernel, scale, count),
        in_specs=[VMEM] * 3 + [ANY] * count,
        out_specs=[ANY] * 6,
        out_shape=[shape(k, BF) for k in kinds],
        scratch_shapes=[pltpu.VMEM((count, rows, width), BF)]
        + [pltpu.VMEM(k, BF) for k in kinds]
        + [pltpu.SemaphoreType.DMA((count,)), pltpu.SemaphoreType.DMA((6 * count,))],
        cost_estimate=pl.CostEstimate(
            flops=count * (2 * rows * width * fw * 3 + 10 * rows * width),
            bytes_accessed=2 * count * (2 * rows * width + 5 * rows * fw) + 6 * width * fw,
            transcendentals=0,
        ),
        name="project",
    )(gain, shift, w, *blocks)


def views(refs):
    return [ref.at[n] for ref in refs for n in range(ref.shape[0])]


def split_lanes(rows, count):
    width = rows.shape[1] // count
    if count == 1:
        return rows
    head_of = lax.broadcasted_iota(jnp.int32, rows.shape, 1) // width
    return jnp.concatenate(
        [jnp.where(head_of == h, rows, jnp.zeros_like(rows)) for h in range(count)], axis=0
    )


def split_rows(cols, count):
    width = cols.shape[0] // count
    if count == 1:
        return cols
    head_of = lax.broadcasted_iota(jnp.int32, cols.shape, 0) // width
    return jnp.concatenate(
        [jnp.where(head_of == h, cols, jnp.zeros_like(cols)) for h in range(count)], axis=1
    )


QB = 2
KB = 2


QB = 2
KB = 2


QB = 2
KB = 2


def attend_kernel(heads, total, groups, qb, kb, me_ref, order_ref, ids_ref, *refs):
    q_in, k_in, vt_in = [views(refs[n * groups : (n + 1) * groups]) for n in range(3)]
    refs = refs[3 * groups :]
    low_refs, refs = refs[:total], refs[total:]
    ctx_ref, lse_ref, ends_ref, q_all, k_all, vt_all, low_all, count_ref, sems, out_sems = refs
    rows = low_all.shape[2]
    fw = q_all.shape[2]
    head = fw // heads
    span = qb * rows
    key_rows = kb * rows
    pairs = []
    for n in range(total):
        at = order_ref[n]
        q_at = pl.ds(pl.multiple_of(lax.rem(at, qb) * rows, rows), rows)
        k_at = pl.ds(pl.multiple_of(lax.rem(at, kb) * rows, rows), rows)
        pairs += [
            (q_in[n], q_all.at[lax.div(at, qb), q_at, :]),
            (k_in[n], k_all.at[lax.div(at, kb), k_at, :]),
            (vt_in[n], vt_all.at[lax.div(at, kb), :, k_at]),
        ]
    copies = begin(pairs, sems)

    ids = ids_ref[...]
    ends = jnp.zeros((total, rows), F32)
    for n in range(total):
        members = jnp.sum(jnp.where(ids == n, 1.0, 0.0))
        ends = ends + jnp.where(ids >= n, members, 0.0)
    for i in range(total // qb):
        ends_ref[i] = jnp.concatenate([ends[i * qb + b : i * qb + b + 1] for b in range(qb)], axis=1)
        last = jnp.max(ends[i * qb + qb - 1 : i * qb + qb]).astype(jnp.int32)
        count_ref[i] = lax.div(last + (key_rows - 1), key_rows)
    finish(copies)
    spots = lax.broadcasted_iota(jnp.int32, (key_rows, heads * span), 0).astype(F32)

    def block(i, unused):
        queries = split_lanes(q_all[i], heads)
        ends = jnp.concatenate([ends_ref[i]] * heads, axis=1)

        def step(j, state):
            run_max, run_sum, held = state
            scores = dot(k_all[j], queries, NT)
            scores = jnp.where(spots < ends - (j * key_rows).astype(F32), scores, NEG)
            new_max = jnp.maximum(run_max, jnp.max(scores, axis=0, keepdims=True))
            weights = jnp.exp(scores - new_max)
            factor = jnp.exp(run_max - new_max)
            new_sum = run_sum * factor + jnp.sum(weights, axis=0, keepdims=True)
            low = weights.astype(BF)
            values = vt_all[j]
            new_held = tuple(
                held[h] * factor[:, h * span : (h + 1) * span]
                + dot(values[h * head : (h + 1) * head], low[:, h * span : (h + 1) * span])
                for h in range(heads)
            )
            return new_max, new_sum, new_held

        start = (
            jnp.full((1, heads * span), NEG, F32),
            jnp.zeros((1, heads * span), F32),
            tuple(jnp.zeros((head, span), F32) for h in range(heads)),
        )
        run_max, run_sum, held = lax.fori_loop(0, count_ref[i], step, start)
        for h in range(heads):
            result = held[h] / run_sum[:, h * span : (h + 1) * span]
            ctx_ref[i, h * head : (h + 1) * head, :] = result
            for b in range(qb):
                low_all[i * qb + b, h * head : (h + 1) * head, :] = result[
                    :, b * rows : (b + 1) * rows
                ].astype(BF)
        lse_ref[i] = run_max + jnp.log(run_sum)
        return unused

    lax.fori_loop(0, total // qb, block, 0)
    finish(begin([(low_all.at[me_ref[1] ^ m], low_refs[m]) for m in range(total)], out_sems))


def attend(q, k, vt, ids, order, heads, me):
    total = len(order)
    groups = len(q)
    rows, fw = q[0].shape[1:]
    qb, kb = QB, KB
    pairs = total * rows * total * rows * heads
    out = pl.pallas_call(
        functools.partial(attend_kernel, heads, total, groups, qb, kb),
        in_specs=[SMEM] * 2 + [VMEM] + [ANY] * (3 * groups),
        out_specs=[ANY] * total + [VMEM] * 3,
        out_shape=[shape((fw, rows), BF)] * total
        + [
            shape((total // qb, fw, qb * rows), F32),
            shape((total // qb, 1, heads * qb * rows), F32),
            shape((total // qb, 1, qb * rows), F32),
        ],
        scratch_shapes=[
            pltpu.VMEM((total // qb, qb * rows, fw), BF),
            pltpu.VMEM((total // kb, kb * rows, fw), BF),
            pltpu.VMEM((total // kb, fw, kb * rows), BF),
            pltpu.VMEM((total, fw, rows), BF),
            pltpu.SMEM((total // qb,), jnp.int32),
            pltpu.SemaphoreType.DMA((3 * total,)),
            pltpu.SemaphoreType.DMA((total,)),
        ],
        cost_estimate=pl.CostEstimate(
            flops=2 * pairs * 128, bytes_accessed=10 * total * rows * fw, transcendentals=pairs // 2
        ),
        name="attend",
    )(me, order, ids, *q, *k, *vt)
    return out[:total], *out[total:]


def attend_back_kernel(heads, scale, total, groups, qb, kb, order_ref, out_order_ref, ends_ref, ctx_ref, lse_ref, w_ref, gain_ref, shift_ref, cent_ref, *refs):
    q_in, k_in, v_in, kt_in, normed_in = [views(refs[n * groups : (n + 1) * groups]) for n in range(5)]
    refs = refs[5 * groups :]
    grad_in, refs = refs[0], refs[1:]
    out_refs, refs = refs[:total], refs[total:]
    dq_ref, dk_ref, dv_ref = refs[:3]
    q_raw, k_all, v_all, kt_all, g_raw, q_all, grad_all, delta_all, dq_all, out_all, normed_all, small_all, first_ref = refs[3:16]
    sems, normed_sems, out_sems, small_sems = refs[16:]
    unused, rows, width = out_all.shape
    fw = q_raw.shape[2]
    head = fw // heads
    span = qb * rows
    pairs = []
    for n in range(total):
        at = order_ref[n]
        q_at = pl.ds(pl.multiple_of(lax.rem(at, qb) * rows, rows), rows)
        k_at = pl.ds(pl.multiple_of(lax.rem(at, kb) * rows, rows), rows)
        pairs += [
            (q_in[n], q_raw.at[lax.div(at, qb), q_at, :]),
            (k_in[n], k_all.at[lax.div(at, kb), k_at, :]),
            (v_in[n], v_all.at[lax.div(at, kb), k_at, :]),
            (kt_in[n], kt_all.at[lax.div(at, kb), :, k_at]),
            (grad_in.at[n], g_raw.at[n // qb, :, pl.ds((n % qb) * rows, rows)]),
        ]
    copies = begin(pairs, sems)
    normed_copies = begin([(normed_in[n], normed_all.at[order_ref[n]]) for n in range(total)], normed_sems)
    lasts = [jnp.max(ends_ref[i]).astype(jnp.int32) for i in range(total // qb)]
    for j in range(total // kb):
        first_ref[j] = sum((last <= j * kb * rows).astype(jnp.int32) for last in lasts)
    finish(copies)

    def prepare(i, unused):
        q_all[i] = split_lanes(q_raw[i], heads)
        grad = g_raw[i]
        grad_all[i] = split_rows(grad, heads)
        product = grad.astype(F32) * ctx_ref[i]
        delta_all[i] = jnp.concatenate(
            [
                jnp.sum(product[h * head : (h + 1) * head], axis=0, keepdims=True)
                for h in range(heads)
            ],
            axis=1,
        )
        dq_all[i] = jnp.zeros((fw, span), F32)
        return unused

    lax.fori_loop(0, total // qb, prepare, 0)

    spots = lax.broadcasted_iota(jnp.int32, (kb * rows, span), 0).astype(F32)

    def key_block(j, unused):
        keys = k_all[j]
        values = v_all[j]
        keys_t = kt_all[j]

        def step(i, state):
            dk, dv = state
            ends = ends_ref[i] - (j * (kb * rows)).astype(F32)
            for h in range(heads):
                at = slice(h * span, (h + 1) * span)
                queries = q_all[i, at, :]
                grads = grad_all[i, :, at]
                scores = dot(keys, queries, NT) - lse_ref[i, :, at]
                probs = jnp.exp(jnp.where(spots < ends, scores, NEG))
                grad_probs = dot(values, grads) - delta_all[i, :, at]
                grad_scores = (probs * grad_probs).astype(BF)
                dv = dv + dot(probs.astype(BF), grads, NT)
                dk = dk + dot(grad_scores, queries)
                dq_all[i, h * head : (h + 1) * head, :] += dot(
                    keys_t[h * head : (h + 1) * head], grad_scores
                )
            return dk, dv

        zero = jnp.zeros((kb * rows, fw), F32)
        dk, dv = lax.fori_loop(first_ref[j], total // qb, step, (zero, zero))
        dk_ref[pl.ds(j * kb, kb)] = dk.astype(BF).reshape(kb, rows, fw)
        dv_ref[pl.ds(j * kb, kb)] = dv.astype(BF).reshape(kb, rows, fw)
        return unused

    lax.fori_loop(0, total // kb, key_block, 0)

    def turn(i, unused):
        dq_ref[pl.ds(i * qb, qb)] = (dq_all[i] * scale).T.astype(BF).reshape(qb, rows, fw)
        return unused

    lax.fori_loop(0, total // qb, turn, 0)

    leaving = []
    lifted = jnp.zeros((1, width), F32)
    shifted = jnp.zeros((1, width), F32)
    finish(normed_copies)
    for n in range(total):
        at = out_order_ref[n]
        grad = dot(jnp.concatenate([dq_ref[at], dk_ref[at], dv_ref[at]], axis=1), w_ref[...], NT)
        out_all[n] = grad.astype(BF)
        leaving += begin(
            [(out_all.at[n], out_refs[n].at[pl.ds(0, rows), :])], out_sems.at[pl.ds(n, 1)]
        )
        shifted = shifted + jnp.sum(grad, axis=0, keepdims=True)
        lifted = lifted + jnp.sum(grad * normed_all[at].astype(F32), axis=0, keepdims=True)
    lifted = (lifted - shift_ref[...] * shifted) / gain_ref[...]
    for n in range(total):
        rest = jnp.zeros((small_all.shape[1] - 3, width), F32)
        cent = cent_ref[pl.ds(out_order_ref[n], 1), :]
        small_all[n] = jnp.concatenate([lifted, shifted, cent, rest], axis=0).astype(BF)
    finish(
        leaving
        + begin(
            [(small_all.at[n], out_refs[n].at[pl.ds(rows, small_all.shape[1]), :]) for n in range(total)],
            small_sems,
        )
    )


def attend_back(q, k, v, kt, normed, grads, ctx, lse, w, gain, shift, cent, ends, order, out_order, heads, scale):
    total = len(order)
    groups = len(q)
    rows, fw = q[0].shape[1:]
    width = w.shape[0]
    qb, kb = QB, KB
    pairs = total * rows * total * rows * heads
    out = pl.pallas_call(
        functools.partial(attend_back_kernel, heads, scale, total, groups, qb, kb),
        in_specs=[SMEM] * 2 + [VMEM] * 7 + [ANY] * (5 * groups + 1),
        out_specs=[ANY] * total + [VMEM] * 3,
        out_shape=[shape((rows + 16, width), BF)] * total + [shape((total, rows, fw), BF)] * 3,
        scratch_shapes=[
            pltpu.VMEM((total // qb, qb * rows, fw), BF),
            pltpu.VMEM((total // kb, kb * rows, fw), BF),
            pltpu.VMEM((total // kb, kb * rows, fw), BF),
            pltpu.VMEM((total // kb, fw, kb * rows), BF),
            pltpu.VMEM((total // qb, fw, qb * rows), BF),
            pltpu.VMEM((total // qb, heads * qb * rows, fw), BF),
            pltpu.VMEM((total // qb, fw, heads * qb * rows), BF),
            pltpu.VMEM((total // qb, 1, heads * qb * rows), F32),
            pltpu.VMEM((total // qb, fw, qb * rows), F32),
            pltpu.VMEM((total, rows, width), BF),
            pltpu.VMEM((total, rows, width), BF),
            pltpu.VMEM((total, 16, width), BF),
            pltpu.SMEM((total // kb,), jnp.int32),
            pltpu.SemaphoreType.DMA((5 * total,)),
            pltpu.SemaphoreType.DMA((total,)),
            pltpu.SemaphoreType.DMA((total,)),
            pltpu.SemaphoreType.DMA((total,)),
        ],
        cost_estimate=pl.CostEstimate(
            flops=5 * pairs * 128, bytes_accessed=20 * total * rows * fw, transcendentals=pairs // 2
        ),
        name="attend_back",
    )(order, out_order, ends, ctx, lse, w, gain, shift, cent, *q, *k, *v, *kt, *normed, grads)
    return out[:total], out[total], out[total + 1], out[total + 2]


def project_grads_kernel(total, groups, parts, order_ref, dq_ref, dk_ref, dv_ref, *refs):
    normed_in, (out_ref, normed_all, grads_all, sems) = views(refs[:groups]), refs[groups:]
    rows = dq_ref.shape[1]
    copies = begin(
        [
            (normed_in[n], normed_all.at[pl.ds(pl.multiple_of(order_ref[n] * rows, rows), rows)])
            for n in range(total)
        ],
        sems,
    )
    grads_all[...] = jnp.concatenate(
        [ref[...].reshape(total * rows, ref.shape[2]) for ref in (dq_ref, dk_ref, dv_ref)], axis=1
    )
    finish(copies)
    step = out_ref.shape[0] // parts

    def one(n, unused):
        at = pl.ds(pl.multiple_of(n * step, step), step)
        out_ref[at, :] = lax.dot_general(
            normed_all[:, at], grads_all[...], (((0,), (0,)), ((), ())), preferred_element_type=F32
        ).astype(BF)
        return unused

    lax.fori_loop(0, parts, one, 0)


def project_grads(dq, dk, dv, normed, order, parts):
    total, rows, fw = dq.shape
    width = normed[0].shape[2]
    return pl.pallas_call(
        functools.partial(project_grads_kernel, total, len(normed), parts),
        in_specs=[SMEM] + [VMEM] * 3 + [ANY] * len(normed),
        out_specs=VMEM,
        out_shape=shape((width, 3 * fw), BF),
        scratch_shapes=[
            pltpu.VMEM((total * rows, width), BF),
            pltpu.VMEM((total * rows, 3 * fw), BF),
            pltpu.SemaphoreType.DMA((total,)),
        ],
        cost_estimate=pl.CostEstimate(
            flops=2 * total * rows * width * 3 * fw,
            bytes_accessed=2 * total * rows * (width + 3 * fw) + 2 * width * 3 * fw,
            transcendentals=0,
        ),
        name="project_grads",
    )(order, dq, dk, dv, *normed)


def output_grads_kernel(ctx_ref, grad_ref, out_ref):
    cols_n, rows_n, part, fw = out_ref.shape
    for n in range(rows_n):
        result = dot(ctx_ref[n * part : (n + 1) * part, :], grad_ref[...]).astype(BF)
        for col in range(cols_n):
            out_ref[col, n] = result[:, col * fw : (col + 1) * fw]


def output_grads(ctx, grad, rows_n, cols_n):
    tok, width = grad.shape
    return pl.pallas_call(
        output_grads_kernel,
        in_specs=[VMEM] * 2,
        out_specs=VMEM,
        out_shape=shape((cols_n, rows_n, width // rows_n, width // cols_n), BF),
        cost_estimate=pl.CostEstimate(
            flops=2 * tok * width * width, bytes_accessed=2 * width * width, transcendentals=0
        ),
        name="output_grads",
    )(ctx, grad)


CHUNK = 512


def gelu_pair(pre_act):
    below = 0.5 * (1.0 + lax.erf(pre_act * 0.7071067811865476))
    bell = jnp.exp(-0.5 * pre_act * pre_act) * 0.3989422804014327
    return pre_act * below, below + pre_act * bell


def weight_copies(sub, w_in, w_back, first, second, sems, between=lambda n: None, turns=(0, 1)):
    count, unused, chunk = first.shape

    def copy(n, which):
        at = pl.ds(pl.multiple_of(n * chunk, chunk), chunk)
        if which == 0:
            return pltpu.make_async_copy(w_in.at[0, sub, :, at], first.at[n], sems.at[2 * n])
        return pltpu.make_async_copy(w_back.at[0, sub, at, :], second.at[n], sems.at[2 * n + 1])

    for n in range(count):
        copy(n, turns[0]).start()
        between(n)
        copy(n, turns[1]).start()
    return copy


def add_to(total, n, more):
    @pl.when(n == 0)
    def begin_sum():
        total[...] = more

    @pl.when(n > 0)
    def add_sum():
        total[...] += more


def piece_pairs(pieces, held, first_lane=0):
    rows = held.shape[0] // len(pieces)
    lanes = pl.ds(first_lane, held.shape[1])
    return [(piece.at[:, lanes], held.at[pl.ds(m * rows, rows), :]) for m, piece in enumerate(pieces)]


def back_pairs(pieces, held):
    rows = held.shape[0] // len(pieces)
    return [(held.at[pl.ds(m * rows, rows), :], piece) for m, piece in enumerate(pieces)]


def spread_pairs(me_ref, whole, held, count):
    rows = held.shape[0] // count
    size = count // 2
    pairs = []
    for m in range(count):
        at = ((me_ref[0] ^ (m % size)) * 2 + m // size) * rows
        pairs.append((whole.at[pl.ds(pl.multiple_of(at, rows), rows), :], held.at[pl.ds(m * rows, rows), :]))
    return pairs


def expert_first_kernel(sub, count, bias_ref, w_in, w_back, *refs):
    pieces, refs = refs[:count], refs[count:]
    outs, refs = refs[:count], refs[count:]
    all_ref, hidden_ref, slope_ref = refs[:3]
    held, first, second, hidden, slope, total, low, sem_w, sem_x, sem_o, sem_r = refs[3:]
    chunks, unused, chunk = first.shape
    arriving = begin(piece_pairs(pieces, held), sem_x)
    weights = weight_copies(sub, w_in, w_back, first, second, sem_w)
    finish(arriving)
    leaving = begin([(held, all_ref)], sem_r.at[pl.ds(0, 1)])
    kept = [(hidden, hidden_ref), (slope, slope_ref)]

    def step(n, unused):
        weights(n, 0).wait()
        value, rise = gelu_pair(dot(held[...], first[n]) + bias_ref[n].astype(F32))
        hidden[n] = value.astype(BF)
        slope[n] = rise
        begin([(h.at[n], o.at[n]) for h, o in kept], sem_r.at[pl.ds(2 * n + 1, 2)])
        weights(n, 1).wait()
        add_to(total, n, dot(hidden[n], second[n]))
        return unused

    lax.fori_loop(0, chunks, step, 0)
    low[...] = total[...].astype(BF)
    leaving += begin(back_pairs(outs, low), sem_o)
    finish(leaving)
    for n in range(chunks):
        finish(copies_of([(h.at[n], o.at[n]) for h, o in kept], sem_r.at[pl.ds(2 * n + 1, 2)]))


def expert_first(pieces, sub, w_in, w_back, bias):
    count = len(pieces)
    rows, width = pieces[0].shape[0] * count, w_in.shape[2]
    ff = w_in.shape[3]
    chunk = min(CHUNK, ff)
    chunks = ff // chunk
    out = pl.pallas_call(
        functools.partial(expert_first_kernel, sub, count),
        in_specs=[VMEM, ANY, ANY] + [ANY] * count,
        out_specs=[ANY] * (count + 3),
        out_shape=[shape((rows // count, width), BF)] * count
        + [
            shape((rows, width), BF),
            shape((chunks, rows, chunk), BF),
            shape((chunks, rows, chunk), F32),
        ],
        scratch_shapes=[
            pltpu.VMEM((rows, width), BF),
            pltpu.VMEM((chunks, width, chunk), BF),
            pltpu.VMEM((chunks, chunk, width), BF),
            pltpu.VMEM((chunks, rows, chunk), BF),
            pltpu.VMEM((chunks, rows, chunk), F32),
            pltpu.VMEM((rows, width), F32),
            pltpu.VMEM((rows, width), BF),
            pltpu.SemaphoreType.DMA((2 * chunks,)),
            pltpu.SemaphoreType.DMA((count,)),
            pltpu.SemaphoreType.DMA((count,)),
            pltpu.SemaphoreType.DMA((2 * chunks + 1,)),
        ],
        cost_estimate=pl.CostEstimate(
            flops=4 * rows * width * ff, bytes_accessed=8 * rows * width, transcendentals=2 * rows * ff
        ),
        name="expert_first",
    )(bias.reshape(chunks, 1, chunk), w_in, w_back, *pieces)
    return out[:count], out[count], out[count + 1], out[count + 2]


def expert_second_kernel(sub, count, bias_ref, w_in, w_back, *refs):
    cot_in, refs = refs[:count], refs[count:]
    pieces, refs = refs[:count], refs[count:]
    gates, refs = refs[:count], refs[count:]
    grad_outs, refs = refs[:count], refs[count:]
    all_ref, grad_all_ref, hidden_ref, pre_ref, bias_out = refs[:5]
    held, cot, gate, held_grad, first, second, hidden, grad_pre, total, low_grad = refs[5:15]
    sem_w, sem_x, sem_c, sem_g, sem_p, sem_r = refs[15:]
    chunks, unused, chunk = first.shape
    arriving = begin(piece_pairs(pieces, held), sem_x)
    width = held.shape[1]
    early = []

    def load_early(n):
        if n == 0:
            early.extend(begin(piece_pairs(cot_in, cot), sem_c))
            early.extend(begin(piece_pairs(gates, gate, width), sem_g))

    weights = weight_copies(sub, w_in, w_back, first, second, sem_w, load_early)
    finish(arriving)
    leaving = begin([(held, all_ref)], sem_r.at[pl.ds(0, 1)])
    scaled = [(held_grad, grad_all_ref)]
    kept = [(hidden, hidden_ref), (grad_pre, pre_ref)]

    def step(n, unused):
        weights(n, 0).wait()
        pre_act = dot(held[...], first[n]) + bias_ref[n].astype(F32)

        @pl.when(n == 0)
        def scale_grads():
            finish(early)
            held_grad[...] = (
                cot[...].astype(F32) * jnp.sum(gate[...].astype(F32), axis=1, keepdims=True)
            ).astype(BF)
            begin(scaled, sem_r.at[pl.ds(1, 1)])

        weights(n, 1).wait()
        grad_hidden = dot(held_grad[...], second[n], NT)
        value, rise = gelu_pair(pre_act)
        hidden[n] = value.astype(BF)
        back = (grad_hidden * rise).astype(BF)
        grad_pre[n] = back
        bias_out[n] = jnp.sum(back.astype(F32), axis=0, keepdims=True)
        begin([(h.at[n], o.at[n]) for h, o in kept], sem_r.at[pl.ds(2 * n + 2, 2)])
        add_to(total, n, dot(grad_pre[n], first[n], NT))
        return unused

    lax.fori_loop(0, chunks, step, 0)
    low_grad[...] = total[...].astype(BF)
    leaving += begin(back_pairs(grad_outs, low_grad), sem_p)

    finish(leaving + copies_of(scaled, sem_r.at[pl.ds(1, 1)]))
    for n in range(chunks):
        finish(copies_of([(h.at[n], o.at[n]) for h, o in kept], sem_r.at[pl.ds(2 * n + 2, 2)]))


def expert_branch_kernel(sub, count, me_ref, hidden_in, w_back, *refs):
    cot_in, (out_ref, logit_ref, hidden, second, cot, total, low, sem_h, sem_w, sem_c, sem_o) = (
        refs[:count],
        refs[count:],
    )
    chunks, unused, chunk = hidden.shape

    def copy(n, which):
        at = pl.ds(pl.multiple_of(n * chunk, chunk), chunk)
        if which == 0:
            return pltpu.make_async_copy(hidden_in.at[n], hidden.at[n], sem_h.at[n])
        return pltpu.make_async_copy(w_back.at[0, sub, at, :], second.at[n], sem_w.at[n])

    for n in range(chunks):
        copy(n, 0).start()
        copy(n, 1).start()
    early = begin(piece_pairs(cot_in, cot), sem_c)

    def step(n, unused):
        copy(n, 0).wait()
        copy(n, 1).wait()
        add_to(total, n, dot(hidden[n], second[n]))
        return unused

    lax.fori_loop(0, chunks, step, 0)
    low[...] = total[...].astype(BF)
    leaving = begin([(h, w) for w, h in spread_pairs(me_ref, out_ref, low, count)], sem_o)
    finish(early)
    logit_ref[...] = scalar_lanes(
        jnp.sum(cot[...].astype(F32) * total[...], axis=1, keepdims=True)
    )
    finish(leaving)


def expert_branch(hidden, cot, sub, w_back, me):
    count = len(cot)
    chunks, rows, chunk = hidden.shape
    width = cot[0].shape[1]
    return pl.pallas_call(
        functools.partial(expert_branch_kernel, sub, count),
        in_specs=[SMEM] + [ANY] * (2 + count),
        out_specs=[ANY, VMEM],
        out_shape=[shape((rows, width), BF), shape((rows, LANES), BF)],
        scratch_shapes=[
            pltpu.VMEM((chunks, rows, chunk), BF),
            pltpu.VMEM((chunks, chunk, width), BF),
            pltpu.VMEM((rows, width), BF),
            pltpu.VMEM((rows, width), F32),
            pltpu.VMEM((rows, width), BF),
            pltpu.SemaphoreType.DMA((chunks,)),
            pltpu.SemaphoreType.DMA((chunks,)),
            pltpu.SemaphoreType.DMA((count,)),
            pltpu.SemaphoreType.DMA((count,)),
        ],
        cost_estimate=pl.CostEstimate(
            flops=2 * rows * width * chunks * chunk, bytes_accessed=8 * rows * width, transcendentals=0
        ),
        name="expert_branch",
    )(me, hidden, w_back, *cot)


def expert_second(pieces, gates, cot, sub, w_in, w_back, bias):
    count = len(pieces)
    rows, width = pieces[0].shape
    rows = rows * count
    ff = w_in.shape[3]
    chunk = min(CHUNK, ff)
    chunks = ff // chunk
    out = pl.pallas_call(
        functools.partial(expert_second_kernel, sub, count),
        in_specs=[VMEM] + [ANY] * (2 + 3 * count),
        out_specs=[ANY] * (count + 4) + [VMEM],
        out_shape=[shape((rows // count, width), BF)] * count
        + [shape((rows, width), BF)] * 2
        + [shape((chunks, rows, chunk), BF)] * 2
        + [shape((chunks, 1, chunk), F32)],
        scratch_shapes=[
            pltpu.VMEM((rows, width), BF),
            pltpu.VMEM((rows, width), BF),
            pltpu.VMEM((rows, LANES), BF),
            pltpu.VMEM((rows, width), BF),
            pltpu.VMEM((chunks, width, chunk), BF),
            pltpu.VMEM((chunks, chunk, width), BF),
            pltpu.VMEM((chunks, rows, chunk), BF),
            pltpu.VMEM((chunks, rows, chunk), BF),
            pltpu.VMEM((rows, width), F32),
            pltpu.VMEM((rows, width), BF),
            pltpu.SemaphoreType.DMA((2 * chunks,)),
            pltpu.SemaphoreType.DMA((count,)),
            pltpu.SemaphoreType.DMA((count,)),
            pltpu.SemaphoreType.DMA((count,)),
            pltpu.SemaphoreType.DMA((count,)),
            pltpu.SemaphoreType.DMA((2 * chunks + 2,)),
        ],
        cost_estimate=pl.CostEstimate(
            flops=6 * rows * width * ff, bytes_accessed=12 * rows * width, transcendentals=2 * rows * ff
        ),
        name="expert_second",
    )(bias.reshape(chunks, 1, chunk), w_in, w_back, *cot, *pieces, *gates)
    return out[:count], *out[count:]


def expert_back_kernel(sub, count, logit_ref, w_in, w_back, slope_in, *refs):
    grads, refs = refs[:count], refs[count:]
    grad_outs, refs = refs[:count], refs[count:]
    grad_all_ref, pre_ref, bias_out = refs[:3]
    held_grad, first, second, slope, grad_pre, total, low_grad = refs[3:10]
    sem_w, sem_s, sem_g, sem_p, sem_r = refs[10:]
    chunks, unused, chunk = first.shape
    arriving_grad = begin(piece_pairs(grads, held_grad), sem_g)
    slopes = lambda n: pltpu.make_async_copy(slope_in.at[n], slope.at[n], sem_s.at[n])
    weights = weight_copies(
        sub, w_in, w_back, first, second, sem_w, lambda n: slopes(n).start(), (1, 0)
    )
    low_grad[:, held_grad.shape[1] :] = logit_ref[...]
    finish(arriving_grad)
    leaving = begin([(held_grad, grad_all_ref)], sem_r.at[pl.ds(0, 1)])

    def step(n, unused):
        weights(n, 1).wait()
        grad_hidden = dot(held_grad[...], second[n], NT)
        slopes(n).wait()
        back = (grad_hidden * slope[n]).astype(BF)
        grad_pre[n] = back
        bias_out[n] = jnp.sum(back.astype(F32), axis=0, keepdims=True)
        begin([(grad_pre.at[n], pre_ref.at[n])], sem_r.at[pl.ds(n + 1, 1)])
        weights(n, 0).wait()
        add_to(total, n, dot(grad_pre[n], first[n], NT))
        return unused

    lax.fori_loop(0, chunks, step, 0)
    low_grad[:, : total.shape[1]] = total[...].astype(BF)
    finish(leaving + begin(back_pairs(grad_outs, low_grad), sem_p))
    for n in range(chunks):
        finish(copies_of([(grad_pre.at[n], pre_ref.at[n])], sem_r.at[pl.ds(n + 1, 1)]))


def expert_back(grads, slope, logit, sub, w_in, w_back):
    count = len(grads)
    rows, width = grads[0].shape
    rows = rows * count
    ff = w_in.shape[3]
    chunk = min(CHUNK, ff)
    chunks = ff // chunk
    out = pl.pallas_call(
        functools.partial(expert_back_kernel, sub, count),
        in_specs=[VMEM] + [ANY] * (3 + count),
        out_specs=[ANY] * (count + 2) + [VMEM],
        out_shape=[shape((rows // count, width + LANES), BF)] * count
        + [shape((rows, width), BF), shape((chunks, rows, chunk), BF), shape((chunks, 1, chunk), F32)],
        scratch_shapes=[
            pltpu.VMEM((rows, width), BF),
            pltpu.VMEM((chunks, width, chunk), BF),
            pltpu.VMEM((chunks, chunk, width), BF),
            pltpu.VMEM((chunks, rows, chunk), F32),
            pltpu.VMEM((chunks, rows, chunk), BF),
            pltpu.VMEM((rows, width), F32),
            pltpu.VMEM((rows, width + LANES), BF),
            pltpu.SemaphoreType.DMA((2 * chunks,)),
            pltpu.SemaphoreType.DMA((chunks,)),
            pltpu.SemaphoreType.DMA((count,)),
            pltpu.SemaphoreType.DMA((count,)),
            pltpu.SemaphoreType.DMA((chunks + 1,)),
        ],
        cost_estimate=pl.CostEstimate(
            flops=4 * rows * width * ff, bytes_accessed=10 * rows * width, transcendentals=0
        ),
        name="expert_back",
    )(logit, w_in, w_back, slope, *grads)
    return out[:count], *out[count:]


def weight_grads_kernel(chunked_left, left_ref, right_ref, *refs):
    out_ref = refs[-1]
    if chunked_left:
        left, right = left_ref[0], right_ref[...]
    else:
        left, right = left_ref[...], right_ref[0]
    out_ref[0, 0] = lax.dot_general(left, right, (((0,), (0,)), ((), ())), preferred_element_type=F32)


def weight_grads(left, right, sub, held, chunked_left):
    chunked, plain = (left, right) if chunked_left else (right, left)
    chunks, rows, chunk = chunked.shape
    width = plain.shape[1]
    pieces = pl.BlockSpec((1, rows, chunk), lambda n: (n, 0, 0))
    whole = pl.BlockSpec((rows, width), lambda n: (0, 0))
    if chunked_left:
        in_specs = [pieces, whole]
        out_spec = pl.BlockSpec((1, 1, chunk, width), lambda n: (0, sub, n, 0))
        dims = (1, 2, chunks * chunk, width)
    else:
        in_specs = [whole, pieces]
        out_spec = pl.BlockSpec((1, 1, width, chunk), lambda n: (0, sub, 0, n))
        dims = (1, 2, width, chunks * chunk)
    more = [] if held is None else [held]
    return pl.pallas_call(
        functools.partial(weight_grads_kernel, chunked_left),
        grid=(chunks,),
        in_specs=in_specs + [ANY] * len(more),
        out_specs=out_spec,
        out_shape=shape(dims, F32),
        input_output_aliases={2: 0} if more else {},
        cost_estimate=pl.CostEstimate(
            flops=2 * rows * width * chunks * chunk,
            bytes_accessed=4 * width * chunks * chunk + 2 * rows * (width + chunks * chunk),
            transcendentals=0,
        ),
        name="weight_grads",
    )(left, right, *more)


def stack_gather(value, axis, size):
    for bit in bits_of(size):
        value = jnp.concatenate([value, send_xor(value, axis, size, 1 << bit)])
    return value


def stack_scatter(value, axis, size):
    for bit in bits_of(size)[::-1]:
        half = value.shape[0] // 2
        value = value[:half] + send_xor(value[half:], axis, size, 1 << bit)
    return value


def together(*values):
    return lax.optimization_barrier(values)


def after(value, *earlier):
    return lax.optimization_barrier((value, *earlier))[0]


def gather_pieces(first, second, axis, size):
    bits = bits_of(size)
    return gather_path(first, axis, size, bits) + gather_path(second, axis, size, bits[::-1])


def scatter_pieces(pieces, axis, size):
    bits = bits_of(size)
    return scatter_path(pieces[:size], axis, size, bits) + scatter_path(
        pieces[size:], axis, size, bits[::-1]
    )


def shards(
    tokens,
    block_ids,
    expert_ids,
    cotangent,
    norm_gain,
    norm_shift,
    w_query,
    w_key,
    w_value,
    w_output,
    centroids,
    expert_gain,
    expert_shift,
    w_in,
    b_in,
    w_back,
    b_back,
):
    rows_n = lax.axis_size("row")
    cols_n = lax.axis_size("col")
    r = lax.axis_index("row")
    c = lax.axis_index("col")
    me = jnp.stack([r, c]).astype(jnp.int32)
    tok, width = tokens.shape
    fw = width // cols_n
    heads = HEADS // cols_n
    scale = float(width // HEADS) ** (-0.5)
    part = width // rows_n
    own = norm_gain.shape[0]
    slot = tok // cols_n

    count = 2 * own + part
    small_experts = jnp.concatenate([expert_gain[0], expert_shift[0], b_back[0]]).reshape(-1)
    more = 16 * -(-small_experts.shape[0] // (64 * fw))
    small_experts = jnp.pad(small_experts, (0, more * 4 * fw - small_experts.shape[0]))
    w_cat = jnp.concatenate(
        [
            jnp.concatenate([w_query, w_key, w_value, w_output], axis=1),
            small_experts.reshape(more, 4 * fw),
        ]
    )
    out_order = jnp.stack(col_order(c, cols_n)).astype(jnp.int32)

    def gather_tiles(value):
        return lax.all_gather(value, "col", axis=0, tiled=True).reshape(cols_n, rows_n, part, fw)

    def matrix_sums(part_qkv, part_output):
        parts = jnp.concatenate([part_qkv, part_output], axis=1).reshape(rows_n, part, 4 * fw)
        parts = reorder(parts, r, rows_n)
        return direct_exchange([parts[m] for m in range(rows_n)], "row", rows_n)

    def exchange(rows):
        return lax.all_to_all(
            rows.reshape(cols_n, -1, rows.shape[-1]), "col", split_axis=0, concat_axis=0, tiled=True
        ).reshape(rows.shape)

    onehot = expert_ids[:, None] == jnp.arange(LANES, dtype=jnp.int32)[None, :]
    onehot_low = onehot.astype(BF)
    below = (jnp.arange(tok)[:, None] > jnp.arange(tok)[None, :]).astype(BF)
    before = dot(below, onehot_low)
    rank = jnp.sum(jnp.where(onehot, before, 0.0), axis=1).astype(jnp.int32)
    place = expert_ids * slot + rank
    route = (jnp.arange(tok, dtype=jnp.int32)[:, None] == place[None, :]).astype(BF)
    unroute = (place[:, None] == jnp.arange(tok, dtype=jnp.int32)[None, :]).astype(BF)
    moved_cot = dot(route, cotangent).astype(BF)

    small = jnp.concatenate([norm_gain, norm_shift, centroids[0], block_ids[0].astype(BF)])[None]

    def small_params(small):
        small = small.reshape(cols_n, rows_n, count + tok)
        small = reorder(small.transpose(1, 0, 2), r, rows_n).transpose(1, 0, 2)
        gain, shift = [
            small[:, :, n * own : (n + 1) * own].transpose(1, 0, 2).reshape(1, width).astype(F32)
            for n in range(2)
        ]
        cents = small[:, :, 2 * own : count].reshape(cols_n, width)
        ids = lax.dynamic_index_in_dim(small[:, :, count:], r, 1, keepdims=False)
        return gain, shift, jnp.pad(cents, ((0, LANES - cols_n), (0, 0))), ids.astype(F32)

    if cols_n == 8:
        chips = cols_n // 2
        z, core = c // 2, c % 2
        move_right = lambda v, s: lax.ppermute(v, "col", right_pairs(s - 1, chips - 2, cols_n))
        move_left = lambda v, s: lax.ppermute(v, "col", left_pairs(1, chips - s, cols_n))
        swap = lambda v: swap_core(v, cols_n)
        right_1, left_1 = move_right(tokens, 1), move_left(tokens, 1)
        tokens_s, small_s = swap(tokens), swap(small)
        right_1, left_1, tokens_s, small_s = together(right_1, left_1, tokens_s, small_s)
        right_2, left_2 = move_right(right_1, 2), move_left(left_1, 2)
        near = jnp.where(z < 2, left_1, right_1)
        near_s = swap(near)
        small = jnp.concatenate(direct_gather(jnp.stack([small, small_s]), "row", rows_n), axis=1)
        from_z = [
            z,
            jnp.where(z % 2 == 0, 1, 2),
            jnp.where(z < 2, jnp.where(z == 0, 2, 0), jnp.where(z == 2, 3, 1)),
            jnp.where(z < 2, 3, 0),
        ]
        order = jnp.stack([at * 2 + (core ^ n) for at in from_z for n in range(2)]).astype(jnp.int32)
        right_2, left_2, near, near_s, small, order, out_order, me = together(
            right_2, left_2, near, near_s, small, order, out_order, me
        )
        right_3, left_3 = move_right(right_2, 3), move_left(left_2, 3)
        middle = jnp.where(
            z < 2, jnp.where(z == 0, left_2, right_1), jnp.where(z == 2, left_1, right_2)
        )
        middle_s = swap(middle)
        small = [small] + [send_xor(small, "col", cols_n, 2 * m) for m in range(1, chips)]
        w_pieces = direct_gather(after(w_cat, right_2), "row", rows_n)
        joined = together(
            right_3, left_3, middle, middle_s, onehot_low, route, unroute, moved_cot, *small, *w_pieces
        )
        right_3, left_3, middle, middle_s, onehot_low, route, unroute, moved_cot = joined[:8]
        small, w_pieces = joined[8 : 8 + chips], joined[8 + chips :]
        far = jnp.where(z < 2, jnp.where(z == 0, left_3, left_2), jnp.where(z == 2, right_2, right_3))
        far_s = swap(far)
        w_cat, tile_rows_own, small_experts = arrange_rows(w_pieces, part, (3 * fw, fw), me)
        small = reorder(reorder(jnp.stack(small), z, chips).transpose(1, 0, 2, 3), core, 2)
        gain_attn, shift_attn, full_centroids, ids = small_params(small.transpose(1, 0, 2, 3))
        tiles = gather_tiles(after(tile_rows_own, far))
        cot_own = exchange(after(moved_cot, far_s))
        projected = project(
            [tokens, tokens_s, near, near_s, middle, middle_s, far, far_s],
            gain_attn, shift_attn, w_cat, scale,
        )
        projected = [(p,) for p in projected]
    else:
        small = jnp.concatenate(direct_gather(small, "row", rows_n))
        small = lax.all_gather(small, "col", axis=0, tiled=True)
        gain_attn, shift_attn, full_centroids, ids = small_params(small)
        w_pieces = direct_gather(w_cat, "row", rows_n)
        cot_own = exchange(moved_cot)
        w_cat, tile_rows_own, small_experts = arrange_rows(w_pieces, part, (3 * fw, fw), me)
        tiles = gather_tiles(tile_rows_own)
        order = out_order
        blocks = col_gather(tokens, cols_n)
        projected = [(p,) for p in project(blocks, gain_attn, shift_attn, w_cat, scale)]
    normed, q, k, v, kt, vt = projected

    ctx_low, ctx, lse, ends = attend(q, k, vt, ids, order, heads, me)
    cot_own, small_experts, *ctx_low = together(cot_own, small_experts, *ctx_low)
    bits = bits_of(rows_n)
    near_cot = {
        half: gather_path(cot_own[half * tok // 2 : (half + 1) * tok // 2], "row", rows_n, [bit])
        for half, bit in ((0, bits[0]), (1, bits[-1]))
    }
    ctx_low = direct_exchange(ctx_low, "col", cols_n)
    rest = together(*ctx_low, *near_cot[0], *near_cot[1])
    ctx_low, near_cot = rest[:cols_n], {0: rest[cols_n : cols_n + 2], 1: rest[cols_n + 2 :]}
    cot_pieces = gather_path(near_cot[0], "row", rows_n, bits[1:], [bits[0]]) + gather_path(
        near_cot[1], "row", rows_n, bits[::-1][1:], [bits[-1]]
    )
    experts = small_experts.reshape(rows_n, -1)[:, : 6 * part].reshape(rows_n, 6, part)
    experts = experts.transpose(1, 0, 2).reshape(6, width).astype(F32)
    moved, ctx_low, residual, gate = forward_rows(
        ctx_low, tiles, tokens, full_centroids, onehot_low, route, me
    )

    rest = together(*direct_exchange(moved, "col", cols_n), *cot_pieces)
    arrived, cot_pieces = rest[:cols_n], rest[cols_n:]
    stream_0, grad_2, half_1, half_2 = enter_expert(arrived, experts, cot_own, me)
    wide_pieces = gather_pieces(half_1, half_2, "row", rows_n)
    partial, normed_all_0, hidden_0, slope_0 = expert_first(wide_pieces, 0, w_in, w_back, b_in[0, 0])
    stream_1, half_1, half_2 = between_experts(
        experts, stream_0, scatter_pieces(partial, "row", rows_n)
    )
    pieces = gather_pieces(half_1, half_2, "row", rows_n)
    partial, normed_all_1, grad_all_1, hidden_1, grad_pre_1, bias_1 = expert_second(
        pieces, wide_pieces, cot_pieces, 1, w_in, w_back, b_in[0, 1]
    )
    sums = scatter_pieces(partial, "row", rows_n)
    branch, logit = expert_branch(hidden_1, cot_pieces, 1, w_back, me)
    branch, logit, *sums = together(branch, logit, *sums)
    grad_1, half_1, half_2, sums_1 = middle_back(experts, stream_1, grad_2, sums)
    pieces = gather_pieces(half_1, half_2, "row", rows_n)
    w_back_grad = weight_grads(hidden_1, after(grad_all_1, grad_1), 1, None, True)
    w_back_grad, *pieces = together(w_back_grad, *pieces)
    partial, grad_all_0, grad_pre_0, bias_0 = expert_back(pieces, slope_0, logit, 0, w_in, w_back)
    sums = together(*scatter_pieces(partial, "row", rows_n))
    branch = lax.psum_scatter(after(branch, sums[0]), "row", scatter_dimension=0, tiled=True)
    *leaving, sums_0 = leave_back(experts, stream_0, grad_1, cot_own, stream_1, sums, me, cols_n)
    returned = direct_exchange(leaving, "col", cols_n)
    w_in_grad = weight_grads(normed_all_0, after(grad_pre_0, sums_0), 0, None, False)
    w_in_grad, *returned = together(w_in_grad, *returned)
    grad_residual, grad_attended, part_cent, grad_ctx = backward_rows(
        returned, tiles, unroute, cotangent, full_centroids, onehot_low, gate, residual, me
    )

    grad_ctx = exchange(grad_ctx)
    part_output = output_grads(ctx_low, grad_attended, rows_n, cols_n)
    w_back_grad = weight_grads(hidden_0, after(grad_all_0, grad_attended), 0, w_back_grad, True)
    expert_low = finish_rows(stream_1, branch, experts)
    part_output, w_back_grad, expert_low, grad_ctx = together(
        part_output, w_back_grad, expert_low, grad_ctx
    )
    expert_low = exchange(expert_low)
    part_output = lax.psum_scatter(
        part_output.reshape(cols_n * width, fw), "col", scatter_dimension=0, tiled=True
    )
    partial, dq, dk, dv = attend_back(
        q, k, v, kt, normed, grad_ctx.reshape(cols_n, fw, tok), ctx, lse, w_cat, gain_attn, shift_attn,
        part_cent, ends, order, out_order, heads, scale,
    )
    dq, expert_low, *partial = together(dq, expert_low, *partial)
    if cols_n == 8:
        halves = [
            add_low(partial[2 * turn], swap(partial[2 * turn + 1])) for turn in range(chips)
        ]
        into_right = lambda v, s: lax.ppermute(
            v, "col", right_pairs(0, min(s - 1, chips - 2), cols_n)
        )
        into_left = lambda v, s: lax.ppermute(
            v, "col", left_pairs(max(chips - s, 1), chips - 1, cols_n)
        )
        from_left, from_right = into_right(halves[3], 1), into_left(halves[1], 1)
        part_qkv = project_grads(after(dq, halves[3]), dk, dv, normed, order, rows_n)
        from_left, from_right, part_qkv, part_output = together(
            from_left, from_right, part_qkv, part_output
        )
        from_left = into_right(add_low(from_left, halves[2]), 2)
        from_right = into_left(add_low(from_right, halves[2]), 2)
        output = (residual + gate * dot(unroute, expert_low)).astype(BF)
        grad_sums = matrix_sums(part_qkv, part_output)
        from_left, from_right, output, *grad_sums = together(from_left, from_right, output, *grad_sums)
        normed_all_1, from_left, from_right = together(normed_all_1, from_left, from_right)
        from_left = into_right(add_low(from_left, halves[1]), 3)
        from_right = into_left(add_low(from_right, halves[3]), 3)
        w_in_grad = weight_grads(normed_all_1, grad_pre_1, 1, w_in_grad, False)
        from_left, from_right, w_in_grad = together(from_left, from_right, w_in_grad)
        summed = halves[0].astype(F32) + from_left.astype(F32) + from_right.astype(F32)
    else:
        part_qkv = project_grads(dq, dk, dv, normed, order, rows_n)
        output = (residual + gate * dot(unroute, expert_low)).astype(BF)
        grad_sums = matrix_sums(part_qkv, part_output)
        w_in_grad = weight_grads(normed_all_1, grad_pre_1, 1, w_in_grad, False)
        summed = col_scatter(partial, cols_n)
    grad_matrices = sum(v.astype(F32) for v in grad_sums)
    grad_qkv, grad_output = grad_matrices[:, : 3 * fw], grad_matrices[:, 3 * fw :]
    grad_normed_attn = summed[:tok]

    norm_rows = summed[tok : tok + 2].reshape(2, rows_n, cols_n, own)
    norm_rows = lax.dynamic_index_in_dim(norm_rows, c, 2, keepdims=False).transpose(1, 0, 2)
    expert_rows = jnp.concatenate([sums_0, sums_1]).reshape(6, rows_n, part).transpose(1, 0, 2)
    packed = jnp.concatenate(
        [
            norm_rows.reshape(rows_n, 2 * own),
            summed[tok + 2].reshape(rows_n, part),
            expert_rows.reshape(rows_n, 6 * part),
        ],
        axis=1,
    )[:, None]
    packed = reorder(packed, r, rows_n)
    packed = sum(direct_exchange([packed[m] for m in range(rows_n)], "row", rows_n))[0]
    expert_sums = packed[count:].reshape(2, 3, part).transpose(1, 0, 2)

    inputs = tokens.astype(F32)
    unit_attn, inv_attn = layer_stats(inputs)
    tokens_grad = grad_residual + norm_back(grad_normed_attn, unit_attn, inv_attn, gain_attn)
    return (
        output,
        tokens_grad,
        packed[:own],
        packed[own : 2 * own],
        grad_qkv[:, :fw],
        grad_qkv[:, fw : 2 * fw],
        grad_qkv[:, 2 * fw :],
        grad_output,
        packed[None, 2 * own : count],
        expert_sums[None, 0],
        expert_sums[None, 1],
        w_in_grad,
        jnp.stack([bias_0.reshape(-1), bias_1.reshape(-1)])[None],
        w_back_grad,
        expert_sums[None, 2],
    )


def solution(mesh):
    placed = (
        P(("row", "col"), None),
        P("row", "col"),
        P(("row", "col")),
        P(("row", "col"), None),
        P(("row", "col")),
        P(("row", "col")),
        P("row", "col"),
        P("row", "col"),
        P("row", "col"),
        P("row", "col"),
        P("col", "row"),
        P("col", None, "row"),
        P("col", None, "row"),
        P("col", None, None, "row"),
        P("col", None, "row"),
        P("col", None, "row", None),
        P("col", None, "row"),
    )
    return jax.shard_map(
        shards,
        mesh=mesh,
        in_specs=placed,
        out_specs=(
            P(("row", "col"), None),
            P(("row", "col"), None),
            P(("row", "col")),
            P(("row", "col")),
            P("row", "col"),
            P("row", "col"),
            P("row", "col"),
            P("row", "col"),
            P("col", "row"),
            P("col", None, "row"),
            P("col", None, "row"),
            P("col", None, None, "row"),
            P("col", None, "row"),
            P("col", None, "row", None),
            P("col", None, "row"),
        ),
        check_vma=False,
    )
```
